32 devices in a mesh: rows: 8 (over y, x, core), cols: 4 (over z).
Axes of the slice: x: 2, y: 2, z: 4, core: 2. Of those that a mesh axis runs over, the one named last changes fastest.
Arguments:
- raw_panel: float32 [256, 32768], P('cols', 'rows')
- raw_trail: float32 [1024, 32768], P('cols', 'rows')
- panel_shift: int32 [256], P('cols'), may hold values from 0 to 255, as said below
- trail_shift: int32 [1024], P('cols'), may hold values from 0 to 255, as said below
Outputs:
- r_factor: float32 [256, 256], replicated
- coupling: float32 [256, 1024], P(None, 'cols')
- q_panel: float32 [256, 32768], P('cols', 'rows')
- trail_out: float32 [1024, 32768], P('cols', 'rows')
The draws below stay inside these ranges and needn't reach their ends.
Inputs may be any that keep to these rules, and one draw needn't show every extreme that they name: `panel_shift`: among the 64 panel and 256 trailing PSFs held by one index of cols, at most 40 have the same value of shift // 32, and exactly 40 share some value. `trail_shift`: as for panel_shift, over the same PSFs of one index of cols.
All inputs are finite; a program needn't handle non-finite values.
Results may differ from the reference program's by a relative error of at most 0.0003.
Values sent between devices are 32-bit elements; how exact they have to be, the bound alone decides.
A program may use at most 64 MiB of HBM per device.

```python
import math
import jax
import jax.numpy as jnp
from jax import lax

PANEL = 256
TRAIL = 1024
BW = 128
BLK_DEV = 32
NBLK = 256
NPIX = 32768
ROWGROUPS = 8
COLGROUPS = 4
PCOLS = 64
CW = 320
CAP = 40


def shift_table(key):
    base_key = jax.random.fold_in(key, 7)
    key_heavy, key_order, key_within = jax.random.split(base_key, 3)
    positions = jnp.arange(CW, dtype=jnp.int32)
    offsets = jnp.where(positions < CAP, 0, 1 + (positions - CAP) % (ROWGROUPS - 1))
    heavy = jax.random.randint(key_heavy, (COLGROUPS, 1), 0, ROWGROUPS)
    hops = (heavy + offsets[None, :]) % ROWGROUPS
    scores = jax.random.randint(key_order, (COLGROUPS, CW), 0, 1 << 20) * CW + positions[None, :]
    order = jnp.argsort(scores, axis=1)
    hops = jnp.take_along_axis(hops, order, axis=1)
    within = jax.random.randint(key_within, (COLGROUPS, CW), 0, BLK_DEV)
    table = (hops * BLK_DEV + within).astype(jnp.int32)
    return (table[:, :PCOLS].reshape(PANEL), table[:, PCOLS:].reshape(TRAIL))


def fresh_noise(key, salt, count):
    sub_key = jax.random.fold_in(key, salt)
    return jax.random.normal(sub_key, (count, NPIX), jnp.float32)


def row_scale(key):
    sub_key = jax.random.fold_in(key, 29)
    ramp = jnp.arange(NPIX, dtype=jnp.float32) / (NPIX - 1)
    rough = jnp.exp(jax.random.uniform(sub_key, (NPIX,), jnp.float32, math.log(0.5), math.log(2.0)))
    return rough * (1.0 + 2.0 * ramp)


def column_scale(key, salt, count):
    sub_key = jax.random.fold_in(key, salt)
    return jnp.exp(jax.random.uniform(sub_key, (count,), jnp.float32, math.log(0.3), math.log(3.0)))


def finish(key, fields, salt, shifts):
    count = fields.shape[0]
    values = fields * row_scale(key)[None, :] * column_scale(key, salt, count)[:, None]
    block_view = values.reshape(count, NBLK, BW)
    positions = jnp.arange(NBLK, dtype=jnp.int32)
    source_idx = (positions[None, :] + shifts[:, None]) % NBLK
    raw = jnp.take_along_axis(block_view, source_idx[:, :, None], axis=1)
    return raw.reshape(count, NPIX)


def draw_panel_shift(key, part):
    return shift_table(key)[0]


def draw_trail_shift(key, part):
    return shift_table(key)[1]


def draw_raw_panel(key, part):
    noise = fresh_noise(key, 11, PANEL + 1)
    fields = noise[1:] + 0.6 * noise[:-1]
    return finish(key, fields, 21, shift_table(key)[0])


def draw_raw_trail(key, part):
    noise = fresh_noise(key, 11, PANEL + 1)
    own_noise = fresh_noise(key, 13, TRAIL + 1)
    partner = 1 + jnp.arange(TRAIL, dtype=jnp.int32) % PANEL
    fields = own_noise[1:] + 0.6 * own_noise[:-1] + 0.8 * noise[partner]
    return finish(key, fields, 23, shift_table(key)[1])


def setup_inputs(seed: int = 0) -> dict:
    key_list = jax.random.split(jax.random.key(seed), 5)
    return {
        "raw_panel": draw_raw_panel(jax.random.fold_in(key_list[4], 71), 0),
        "raw_trail": draw_raw_trail(jax.random.fold_in(key_list[4], 71), 0),
        "panel_shift": draw_panel_shift(jax.random.fold_in(key_list[4], 71), 0),
        "trail_shift": draw_trail_shift(jax.random.fold_in(key_list[4], 71), 0),
    }


def register(raw_rows, shifts):
    count = raw_rows.shape[0]
    block_view = raw_rows.reshape(count, NBLK, BW)
    positions = jnp.arange(NBLK, dtype=jnp.int32)
    source_idx = ((positions[None, :] - shifts[:, None].astype(jnp.int32)) % NBLK).astype(jnp.int32)
    moved = jnp.take_along_axis(block_view, source_idx[:, :, None], axis=1)
    return moved.reshape(count, NPIX)

def reference(raw_panel, raw_trail, panel_shift, trail_shift):
    highest = lax.Precision.HIGHEST
    reg_panel = register(raw_panel, panel_shift)
    reg_trail = register(raw_trail, trail_shift)
    q_factor, r_upper = jnp.linalg.qr(reg_panel.T)
    flips = jnp.where(jnp.diagonal(r_upper) < 0, -1.0, 1.0).astype(r_upper.dtype)
    r_full = r_upper * flips[:, None]
    basis_t = (q_factor * flips[None, :]).T
    coupling_full = jnp.dot(basis_t, reg_trail.T, precision=highest)
    trail_out = reg_trail - jnp.dot(coupling_full.T, basis_t, precision=highest)
    root = math.sqrt(NPIX)
    return (r_full / root, coupling_full / root, basis_t * root, trail_out)
```

```python
import functools
import math

import jax
import jax.numpy as jnp
from jax import lax
from jax.experimental import pallas as pl
from jax.experimental.pallas import tpu as pltpu
from jax.sharding import PartitionSpec as P

BW = 128
SUB = 8
MESH = pl.DeviceIdType.MESH
F32 = jnp.float32
HIGHEST = lax.Precision.HIGHEST
HIGH = lax.Precision.HIGH


def rows_dot(left, right, precision):
    return lax.dot_general(
        left,
        right,
        (((1,), (1,)), ((), ())),
        precision=precision,
        preferred_element_type=F32,
    )


def plain_dot(left, right, precision):
    return lax.dot_general(
        left,
        right,
        (((1,), (0,)), ((), ())),
        precision=precision,
        preferred_element_type=F32,
    )


def only(cond, always):
    if always:
        return lambda fn: fn()
    return pl.when(cond)


def fused_kernel(
    n,
    depth,
    pieces,
    scale,
    panel_shift,
    trail_shift,
    panel,
    trail,
    full,
    reg,
    upper_ref,
    inv_ref,
    own_ref,
    cross_ref,
    ring_p,
    moved_p,
    moved_t,
    gram_part,
    gram_land,
    gram_sum,
    cross_part,
    cross_land,
    aug,
    pair,
    p1_send,
    p1_recv,
    p2_send,
    p2_recv,
    t1_send,
    t1_recv,
    t2_send,
    t2_recv,
    z_send,
    z_recv,
    g_send,
    g_recv,
    c_send,
    c_recv,
    f_send,
    f_recv,
    local_sem,
    *rings,
):
    me = lax.axis_index("rows")
    z = lax.axis_index("cols")
    ctp, blocks = panel.shape[0], panel.shape[1]
    ctt = trail.shape[0]
    total = n * blocks
    tp = ring_p.shape[0]
    tt = len(rings)
    op, ot = ctp // tp, ctt // tt
    rows_t = ot * SUB
    sr = cross_land.shape[2]
    oc = rows_t // sr
    size = inv_ref.shape[0]
    mid_lo = max(depth // 2 - 1, 0)
    mid_hi = min(depth // 2, depth - 1)
    mine = pl.ds(pl.multiple_of(me * blocks, blocks), blocks)

    def each_peer(fn):
        def body(d, carry):
            fn(d, lax.rem(me + d, n), lax.rem(me - d + n, n))
            return carry

        lax.fori_loop(1, n, body, 0)

    def linked(other):
        near = (z - other == 1) | (other - z == 1)
        low = ((z == mid_lo) & (other < mid_lo)) | ((z < mid_lo) & (other == mid_lo))
        high = ((z == mid_hi) & (other > mid_hi)) | ((z > mid_hi) & (other == mid_hi))
        return near | low | high

    barrier = pltpu.get_barrier_semaphore()
    for d in range(1, n):
        pl.semaphore_signal(
            barrier, inc=1, device_id={"rows": lax.rem(me + d, n)}, device_id_type=MESH
        )
    greeted = n - 1
    for other in range(depth):

        @pl.when(linked(other))
        def _():
            pl.semaphore_signal(barrier, inc=1, device_id={"cols": other}, device_id_type=MESH)

        greeted = greeted + jnp.where(linked(other), 1, 0)
    pl.semaphore_wait(barrier, greeted)

    def row_copy(src, dst, send, recv, to):
        return pltpu.make_async_remote_copy(
            src_ref=src,
            dst_ref=dst,
            send_sem=send,
            recv_sem=recv,
            device_id={"rows": to},
            device_id_type=MESH,
        )

    def p1(d, to):
        return row_copy(
            panel.at[pl.ds(to * tp, tp)],
            ring_p.at[:, mine],
            p1_send.at[d - 1],
            p1_recv.at[d - 1],
            to,
        )

    def p2(d, to):
        return row_copy(
            moved_p.at[to],
            full.at[z, pl.ds(me * tp, tp)],
            p2_send.at[d - 1],
            p2_recv.at[d - 1],
            to,
        )

    def t1(t, d, to):
        return row_copy(
            trail.at[to * tt + t],
            rings[t].at[mine],
            t1_send.at[t, d - 1],
            t1_recv.at[t, d - 1],
            to,
        )

    def t2(t, d, to):
        return row_copy(
            moved_t.at[t, to],
            reg.at[me, t],
            t2_send.at[t, d - 1],
            t2_recv.at[t, d - 1],
            to,
        )

    own_p = pltpu.make_async_copy(
        panel.at[pl.ds(me * tp, tp)], ring_p.at[:, mine], local_sem.at[0]
    )

    def own_t(t):
        return pltpu.make_async_copy(
            trail.at[me * tt + t], rings[t].at[mine], local_sem.at[1 + t]
        )

    def started(copies, active, count):
        def go(d, to, origin):
            @only(active(to), count == n)
            def _():
                copies(d, to).start()

        each_peer(go)

    def landed(copies, active, count, by_origin):
        def go(d, to, origin):
            @only(active(origin if by_origin else me), count == n)
            def _():
                copies(d, to).wait_recv()

        each_peer(go)

    def left(copies, active, count, by_target):
        def go(d, to, origin):
            @only(active(to if by_target else me), count == n)
            def _():
                copies(d, to).wait_send()

        each_peer(go)

    def has_p(j):
        return j < op

    def has_t(j):
        return j < ot

    sub = lax.broadcasted_iota(jnp.int32, (1, SUB, BW), 1)
    step = min(16, blocks)

    def compose(ring, shifts, to, put):
        starts = [lax.rem(to * blocks - s + total, total) for s in shifts]
        for h in range(0, blocks, step):
            block = ring[pl.ds(starts[0] + h, step)]
            for c in range(1, SUB):
                block = jnp.where(sub == c, ring[pl.ds(starts[c] + h, step)], block)
            put(h, block)

    def wrap(ring):
        ring[pl.ds(total, blocks)] = ring[pl.ds(0, blocks)]

    def line(side, d, q):
        step_z = 1 if side == 0 else -1
        origin = z - step_z * (d - 1)
        rows = pl.ds(q * (ctp // pieces), ctp // pieces)
        return pltpu.make_async_remote_copy(
            src_ref=full.at[origin, rows],
            dst_ref=full.at[origin, rows],
            send_sem=z_send.at[side, d - 1, q],
            recv_sem=z_recv.at[side, d - 1, q],
            device_id={"cols": z + step_z},
            device_id_type=MESH,
        )

    def sends(side, d):
        if side == 0:
            return (z + 1 < depth) & (z - (d - 1) >= 0)
        return (z >= 1) & (z + (d - 1) < depth)

    def receives(side, d):
        return z - d >= 0 if side == 0 else z + d < depth

    def arrived(side, d, q):
        step_z = 1 if side == 0 else -1
        origin = z - step_z * d
        rows = pl.ds(q * (ctp // pieces), ctp // pieces)
        return pltpu.make_async_remote_copy(
            src_ref=full.at[origin, rows],
            dst_ref=full.at[origin, rows],
            send_sem=z_send.at[side, d - 1, q],
            recv_sem=z_recv.at[side, d - 1, q],
            device_id={"cols": z - step_z},
            device_id_type=MESH,
        )

    def forward(d):
        for q in range(pieces):
            for side in (0, 1):

                @pl.when(receives(side, d))
                def _():
                    arrived(side, d, q).wait_recv()

                if d + 1 < depth:

                    @pl.when(sends(side, d + 1))
                    def _():
                        line(side, d + 1, q).start()

    def start_t1(t):
        @only(has_t(me), ot == n)
        def _():
            own_t(t).start()

        started(functools.partial(t1, t), has_t, ot)

    def turn_t(t):
        @only(has_t(me), ot == n)
        def _():
            own_t(t).wait()

        landed(functools.partial(t1, t), has_t, ot, False)

        @only(has_t(me), ot == n)
        def _():
            wrap(rings[t])
            shifts = [trail_shift[(me * tt + t) * SUB + c] for c in range(SUB)]

            def turn(d, to, origin):
                def put(h, block):
                    moved_t[t, to, pl.ds(h, step)] = block

                compose(rings[t], shifts, to, put)

            each_peer(turn)

            def keep(h, block):
                reg[me, t, pl.ds(h, step)] = block

            compose(rings[t], shifts, me, keep)

    def start_t2(t):
        def go(d, to, origin):
            t2(t, d, to).start()

        @only(has_t(me), ot == n)
        def _():
            each_peer(go)

    def wait_t2(t):
        landed(functools.partial(t2, t), has_t, ot, True)

    def panel_pair(b):
        cut = [full[:, :, 2 * b + k].reshape(size, BW) for k in range(2)]
        return jnp.concatenate(cut, axis=1)

    def make_gram():
        gram_part[...] = jnp.zeros_like(gram_part)

        def body(b, carry):
            block = panel_pair(b)
            gram_part[...] += rows_dot(block, block, HIGHEST).reshape(gram_part.shape)
            return carry

        lax.fori_loop(0, blocks // 2, body, 0)

    def g_one(d, to):
        return row_copy(
            gram_part.at[to], gram_land.at[d - 1], g_send.at[0, d - 1], g_recv.at[0, d - 1], to
        )

    def g_two(d, to):
        return row_copy(
            gram_sum.at[me], gram_sum.at[me], g_send.at[1, d - 1], g_recv.at[1, d - 1], to
        )

    def every(j):
        return j >= 0

    def has_c(j):
        return j < oc

    def make_cross(t):
        cross_part[t] = jnp.zeros_like(cross_part[t])

        def body(b, carry):
            cut = [reg[:, t, 2 * b + k].reshape(rows_t, BW) for k in range(2)]
            block = jnp.concatenate(cut, axis=1)
            cross_part[t] += rows_dot(block, panel_pair(b), HIGH).reshape(oc, sr, size)
            return carry

        lax.fori_loop(0, blocks // 2, body, 0)

    def c_one(t, d, to):
        return row_copy(
            cross_part.at[t, to],
            cross_land.at[t, d - 1],
            c_send.at[0, t, d - 1],
            c_recv.at[0, t, d - 1],
            to,
        )

    def c_two(t, d, to):
        return row_copy(
            cross_ref.at[t, me],
            cross_ref.at[t, me],
            c_send.at[1, t, d - 1],
            c_recv.at[1, t, d - 1],
            to,
        )

    def cross_scatter(t):
        started(functools.partial(c_one, t), has_c, oc)

    def cross_spread(t):
        @only(has_c(me), oc == n)
        def _():
            total_c = cross_part[t, me]
            for d in range(1, n):
                c_one(t, d, lax.rem(me + d, n)).wait_recv()
                total_c = total_c + cross_land[t, d - 1]
            cross_ref[t, me] = total_c

            def go(d, to, origin):
                c_two(t, d, to).start()

            each_peer(go)

    def cross_done(t):
        landed(functools.partial(c_two, t), has_c, oc, True)

    tile = min(64, size)
    tiles = size // tile
    low_count = mid_lo
    high_count = depth - 1 - mid_hi

    def factor_copy(i, k, slot, to):
        ref = inv_ref if k == 0 else upper_ref
        rows = pl.ds(i * tile, tile)
        return pltpu.make_async_remote_copy(
            src_ref=ref.at[rows],
            dst_ref=ref.at[rows],
            send_sem=f_send.at[slot, i, k],
            recv_sem=f_recv.at[i, k],
            device_id={"cols": to},
            device_id_type=MESH,
        )

    def factor_sends(act):
        for k in (0, 1):
            for i in range(tiles):
                send_factor(i, k, act)

    def send_factor(i, k, act):
        for slot in range(low_count):

            @pl.when(z == mid_lo)
            def _():
                act(factor_copy(i, k, slot, slot))

        for slot in range(high_count):

            @pl.when(z == mid_hi)
            def _():
                act(factor_copy(i, k, slot, mid_hi + 1 + slot))

    def factor_tile(i):
        lo = i * tile
        hi = lo + tile
        row = lax.broadcasted_iota(jnp.int32, (tile, 2 * tile), 0)
        col = lax.broadcasted_iota(jnp.int32, (tile, 2 * tile), 1)
        pair[...] = jnp.where(col == row + tile, 1.0, 0.0)
        pair[:, 0:tile] = aug[lo:hi, lo:hi]
        w = pair[...]
        pivots = jnp.zeros((tile, 1), F32)
        for j in range(tile):
            base = j // 8 * 8
            live = w[base:, :]
            lead = w[j : j + 1, :]
            pivot = lead[:, j : j + 1]
            pivots = jnp.where(row[:, 0:1] == j, pivot, pivots)
            if j + 1 == tile:
                break
            mult = jnp.where(row[base:, 0:1] > j, live[:, j : j + 1], 0.0)
            live = live - mult * (lead / pivot)
            w = live if base == 0 else jnp.concatenate([w[:base], live], axis=0)
        pair[...] = w * (1.0 / jnp.sqrt(pivots))
        inverse = pair[:, tile : 2 * tile]
        lead_rows = plain_dot(inverse, aug[lo:hi, :], HIGHEST)
        grow = lax.broadcasted_iota(jnp.int32, (tile, size), 0) + lo
        gcol = lax.broadcasted_iota(jnp.int32, (tile, size), 1)
        upper = jnp.where(gcol >= grow, lead_rows[:, 0:size], 0.0)
        upper_ref[lo:hi, :] = upper * scale
        inv_ref[lo:hi, :] = lead_rows[:, size : 2 * size]
        if hi < size:
            aug[...] = aug[...] - lax.dot_general(
                upper,
                lead_rows,
                (((0,), (0,)), ((), ())),
                precision=HIGHEST,
                preferred_element_type=F32,
            )

    def start_copy(copy):
        copy.start()

    @only(has_p(me), op == n)
    def _():
        own_p.start()

    started(p1, has_p, op)

    @only(has_p(me), op == n)
    def _():
        own_p.wait()

    landed(p1, has_p, op, False)

    @only(has_p(me), op == n)
    def _():
        for t in range(tp):
            wrap(ring_p.at[t])
        shifts = [
            [panel_shift[(me * tp + t) * SUB + c] for c in range(SUB)] for t in range(tp)
        ]

        def turn(d, to, origin):
            for t in range(tp):

                def put(h, block, t=t):
                    moved_p[to, t, pl.ds(h, step)] = block

                compose(ring_p.at[t], shifts[t], to, put)

        each_peer(turn)

        def go(d, to, origin):
            p2(d, to).start()

        each_peer(go)
        for t in range(tp):

            def keep(h, block, t=t):
                full[z, me * tp + t, pl.ds(h, step)] = block

            compose(ring_p.at[t], shifts[t], me, keep)

    last = tt - 1
    start_t1(0)
    if tt > 1:
        start_t1(1)
    landed(p2, has_p, op, True)
    for q in range(pieces):
        for side in (0, 1):

            @pl.when(sends(side, 1))
            def _():
                line(side, 1, q).start()

    middle = max(depth // 2, 1)
    turn_t(0)
    if last > 0:
        start_t2(0)
    for t in range(2, last):
        start_t1(t)
    if depth > 1:
        forward(1)
    for t in range(1, last):
        turn_t(t)
        if t + 1 < last:
            start_t2(t)
        if t == 1:
            for d in range(2, middle + 1):
                forward(d)
    if last < 2:
        for d in range(2, middle + 1):
            forward(d)

    def rest_t1():
        if last > 1:
            start_t1(last)

    def rest_t2():
        if last > 1:
            start_t2(last - 1)

    def finish_turns():
        if last > 0:
            turn_t(last)
        start_t2(last)

    central = (z == mid_lo) | (z == mid_hi)

    @pl.when(central)
    def _():
        make_gram()
        started(g_one, every, n)
        aug_row = lax.broadcasted_iota(jnp.int32, (size, size), 0)
        aug_col = lax.broadcasted_iota(jnp.int32, (size, size), 1)
        aug[:, size : 2 * size] = jnp.where(aug_row == aug_col, 1.0, 0.0)
        total_g = gram_part[me]
        for d in range(1, n):
            g_one(d, lax.rem(me + d, n)).wait_recv()
            total_g = total_g + gram_land[d - 1]
        gram_sum[me] = total_g
        started(g_two, every, n)
        rest_t1()
        rest_t2()
        landed(g_two, every, n, True)
        aug[:, 0:size] = gram_sum[...].reshape(size, size)
        for i in range(tiles):
            factor_tile(i)
            send_factor(i, 0, start_copy)
            if i == min(1, tiles - 1):
                finish_turns()
        for i in range(tiles):
            send_factor(i, 1, start_copy)
        left(g_one, every, n, True)
        left(g_two, every, n, True)

    @pl.when(jnp.logical_not(central))
    def _():
        rest_t1()
        rest_t2()
        for d in range(middle + 1, depth):
            forward(d)
        finish_turns()

    for t in range(last):
        wait_t2(t)
        make_cross(t)
        cross_scatter(t)
    for t in range(last):
        cross_spread(t)
    wait_t2(last)
    make_cross(last)
    cross_scatter(last)
    cross_spread(last)

    @pl.when(jnp.logical_not(central))
    def _():
        for i in range(tiles):
            for k in (0, 1):
                factor_copy(i, k, 0, mid_lo).wait_recv()

    own = inv_ref.shape[0] // depth
    own_ref[...] = inv_ref[pl.ds(pl.multiple_of(z * own, own), own), :]
    for t in range(tt):
        cross_done(t)

    @pl.when(central)
    def _():
        factor_sends(lambda copy: copy.wait_send())

    left(p1, has_p, op, True)
    left(p2, has_p, op, False)
    for t in range(tt):
        left(functools.partial(t1, t), has_t, ot, True)
        left(functools.partial(t2, t), has_t, ot, False)
        left(functools.partial(c_one, t), has_c, oc, True)
        left(functools.partial(c_two, t), has_c, oc, False)
    for d in range(1, depth):
        for q in range(pieces):
            for side in (0, 1):

                @pl.when(sends(side, d))
                def _():
                    line(side, d, q).wait_send()


def fused(panel, trail, panel_shift, trail_shift, n, depth, scale):
    ctp, blocks = panel.shape[0], panel.shape[1]
    ctt = trail.shape[0]
    tp = -(-ctp // n)
    tt = -(-ctt // n)
    op, ot = ctp // tp, ctt // tt
    size = depth * ctp * SUB
    rows_t = ot * SUB
    sr = max(SUB, rows_t // n)
    oc = rows_t // sr
    tiles = max(size // 64, 1)
    pieces = 4 if ctp % 4 == 0 else 1
    total = n * blocks
    smem = pl.BlockSpec(memory_space=pltpu.SMEM)
    vmem = pl.BlockSpec(memory_space=pltpu.VMEM)
    hbm = pl.BlockSpec(memory_space=pl.ANY)
    dma = pltpu.SemaphoreType.DMA
    peers = max(n - 1, 1)
    lines = max(depth - 1, 1)
    square = jax.ShapeDtypeStruct((size, size), F32)
    return pl.pallas_call(
        functools.partial(fused_kernel, n, depth, pieces, scale),
        out_shape=(
            jax.ShapeDtypeStruct((depth, ctp, blocks, SUB, BW), F32),
            jax.ShapeDtypeStruct((ot, tt, blocks, SUB, BW), F32),
            square,
            square,
            jax.ShapeDtypeStruct((size // depth, size), F32),
            jax.ShapeDtypeStruct((tt, oc, sr, size), F32),
        ),
        in_specs=[smem, smem, hbm, hbm],
        out_specs=(vmem,) * 6,
        scratch_shapes=[
            pltpu.VMEM((tp, total + blocks, SUB, BW), F32),
            pltpu.VMEM((n, tp, blocks, SUB, BW), F32),
            pltpu.VMEM((tt, n, blocks, SUB, BW), F32),
            pltpu.VMEM((n, size // n, size), F32),
            pltpu.VMEM((peers, size // n, size), F32),
            pltpu.VMEM((n, size // n, size), F32),
            pltpu.VMEM((tt, oc, sr, size), F32),
            pltpu.VMEM((tt, peers, sr, size), F32),
            pltpu.VMEM((size, 2 * size), F32),
            pltpu.VMEM((size // tiles, 2 * (size // tiles)), F32),
            dma((peers,)),
            dma((peers,)),
            dma((peers,)),
            dma((peers,)),
            dma((tt, peers)),
            dma((tt, peers)),
            dma((tt, peers)),
            dma((tt, peers)),
            dma((2, lines, pieces)),
            dma((2, lines, pieces)),
            dma((2, peers)),
            dma((2, peers)),
            dma((2, tt, peers)),
            dma((2, tt, peers)),
            dma((lines, tiles, 2)),
            dma((tiles, 2)),
            dma((1 + tt,)),
        ]
        + [pltpu.VMEM((total + blocks, SUB, BW), F32)] * tt,
        compiler_params=pltpu.CompilerParams(collective_id=3, has_side_effects=True),
        cost_estimate=pl.CostEstimate(
            flops=0, bytes_accessed=40 * trail.size * 4, transcendentals=0
        ),
    )(panel_shift, trail_shift, panel, trail)


def final_kernel(
    root, full, reg, upper, inv, own, cross, r_ref, coupling_ref, q_ref, out_ref, weights
):
    size = inv.shape[0]
    ot, tt = reg.shape[0], reg.shape[1]
    part = full.shape[2]

    @pl.when(pl.program_id(0) == 0)
    def _():
        r_ref[...] = upper[...]
        for t in range(tt):
            rows = cross[t].reshape(ot * SUB, size)
            turned = rows_dot(rows, inv[...], HIGHEST)
            coupling_ref[:, t] = (turned * (1.0 / root)).reshape(ot, SUB, size)
            weights[:, t] = plain_dot(turned, inv[...], HIGHEST).reshape(ot, SUB, size)

    block = jnp.concatenate(
        [full[:, :, k].reshape(size, BW) for k in range(part)], axis=1
    )
    both = plain_dot(weights[...].reshape(ot * tt * SUB, size), block, HIGH)
    basis = plain_dot(own[...] * root, block, HIGH)
    for k in range(part):
        lanes = slice(k * BW, (k + 1) * BW)
        out_ref[:, :, k] = reg[:, :, k] - both[:, lanes].reshape(ot, tt, SUB, BW)
        q_ref[:, k] = basis[:, lanes].reshape(q_ref.shape[0], SUB, BW)


def final(full, reg, upper, inv, own, cross, root):
    depth, ctp, blocks = full.shape[:3]
    ot, tt = reg.shape[:2]
    size = inv.shape[0]
    part = 4 if blocks % 4 == 0 else 1
    whole = lambda shape: pl.BlockSpec(shape, lambda i: (0,) * len(shape))
    reg_spec = pl.BlockSpec((ot, tt, part, SUB, BW), lambda i: (0, 0, i, 0, 0))
    return pl.pallas_call(
        functools.partial(final_kernel, root),
        grid=(blocks // part,),
        out_shape=(
            jax.ShapeDtypeStruct((size, size), F32),
            jax.ShapeDtypeStruct((ot, tt, SUB, size), F32),
            jax.ShapeDtypeStruct((ctp, blocks, SUB, BW), F32),
            jax.ShapeDtypeStruct((ot, tt, blocks, SUB, BW), F32),
        ),
        in_specs=[
            pl.BlockSpec((depth, ctp, part, SUB, BW), lambda i: (0, 0, i, 0, 0)),
            reg_spec,
            whole((size, size)),
            whole((size, size)),
            whole((size // depth, size)),
            whole(cross.shape),
        ],
        out_specs=(
            whole((size, size)),
            whole((ot, tt, SUB, size)),
            pl.BlockSpec((ctp, part, SUB, BW), lambda i: (0, i, 0, 0)),
            reg_spec,
        ),
        scratch_shapes=[pltpu.VMEM((ot, tt, SUB, size), F32)],
        cost_estimate=pl.CostEstimate(
            flops=2 * size * (reg.size + full.size), bytes_accessed=12 * reg.size, transcendentals=0
        ),
    )(full, reg, upper, inv, own, cross)


def tiled(raw):
    rows, pixels = raw.shape
    return raw.reshape(rows // SUB, SUB, pixels // BW, BW).transpose(0, 2, 1, 3)


def flat(blocked):
    cut, blocks = blocked.shape[0], blocked.shape[1]
    return blocked.transpose(0, 2, 1, 3).reshape(cut * SUB, blocks * BW)


def on_device(raw_panel, raw_trail, panel_shift, trail_shift):
    n = lax.axis_size("rows")
    depth = lax.axis_size("cols")
    pixels = raw_panel.shape[1]
    root = math.sqrt(pixels * n)
    full, reg, upper, inv, own, cross = fused(
        tiled(raw_panel), tiled(raw_trail), panel_shift, trail_shift, n, depth, 1.0 / root
    )
    r_factor, coupling, q_panel, out = final(full, reg, upper, inv, own, cross, root)
    coupling = coupling.reshape(-1, coupling.shape[-1]).T
    out = flat(out.reshape((-1,) + out.shape[2:]))
    return (r_factor, coupling, flat(q_panel), out)


def solution(mesh):
    placed = (P("cols", "rows"), P("cols", "rows"), P("cols"), P("cols"))
    return jax.shard_map(
        on_device,
        mesh=mesh,
        in_specs=placed,
        out_specs=(P(), P(None, "cols"), P("cols", "rows"), P("cols", "rows")),
        check_vma=False,
    )
```

```python
import functools
import math

import jax
import jax.numpy as jnp
from jax import lax
from jax.experimental import pallas as pl
from jax.experimental.pallas import tpu as pltpu
from jax.sharding import PartitionSpec as P

BW = 128
SUB = 8
MESH = pl.DeviceIdType.MESH
F32 = jnp.float32
HIGHEST = lax.Precision.HIGHEST
HIGH = lax.Precision.HIGH


def rows_dot(left, right, precision):
    return lax.dot_general(
        left,
        right,
        (((1,), (1,)), ((), ())),
        precision=precision,
        preferred_element_type=F32,
    )


def plain_dot(left, right, precision):
    return lax.dot_general(
        left,
        right,
        (((1,), (0,)), ((), ())),
        precision=precision,
        preferred_element_type=F32,
    )


def joined(parts):
    return jnp.concatenate(parts, axis=0) if len(parts) > 1 else parts[0]


def three_part(value):
    high = value.astype(jnp.bfloat16)
    low = (value - high.astype(F32)).astype(jnp.bfloat16)
    return jnp.concatenate([high, high, low], axis=1)


def removed(left_side, high_ref, low_ref, first, count):
    high = jnp.concatenate([high_ref[first + k] for k in range(count)], axis=1)
    low = jnp.concatenate([low_ref[first + k] for k in range(count)], axis=1)
    return plain_dot(left_side, jnp.concatenate([high, low, high], axis=0), None)


def only(cond, always):
    if always:
        return lambda fn: fn()
    return pl.when(cond)


def fused_kernel(
    n,
    depth,
    pieces,
    root,
    panel_shift,
    trail_shift,
    panel,
    trail,
    upper_ref,
    inv_ref,
    cross_ref,
    q_ref,
    reg,
    high_ref,
    low_ref,
    full,
    ring_p,
    moved_p,
    moved_t,
    gram_part,
    gram_land,
    gram_sum,
    cross_part,
    cross_land,
    aug,
    pair,
    p1_send,
    p1_recv,
    p2_send,
    p2_recv,
    t1_send,
    t1_recv,
    t2_send,
    t2_recv,
    z_send,
    z_recv,
    g_send,
    g_recv,
    c_send,
    c_recv,
    f_send,
    f_recv,
    local_sem,
    *rings,
):
    me = lax.axis_index("rows")
    z = lax.axis_index("cols")
    ctp, blocks = panel.shape[0], panel.shape[1]
    ctt = trail.shape[0]
    total = n * blocks
    tp = ring_p.shape[0]
    tt = len(rings)
    op, ot = ctp // tp, ctt // tt
    rows_t = ot * SUB
    sr = cross_land.shape[2]
    oc = rows_t // sr
    size = inv_ref.shape[0]
    mid_lo = max(depth // 2 - 1, 0)
    mid_hi = min(depth // 2, depth - 1)
    mine = pl.ds(pl.multiple_of(me * blocks, blocks), blocks)

    def each_peer(fn):
        def body(d, carry):
            fn(d, lax.rem(me + d, n), lax.rem(me - d + n, n))
            return carry

        lax.fori_loop(1, n, body, 0)

    def linked(other):
        near = (z - other == 1) | (other - z == 1)
        low = ((z == mid_lo) & (other < mid_lo)) | ((z < mid_lo) & (other == mid_lo))
        high = ((z == mid_hi) & (other > mid_hi)) | ((z > mid_hi) & (other == mid_hi))
        return near | low | high

    barrier = pltpu.get_barrier_semaphore()
    for d in range(1, n):
        pl.semaphore_signal(
            barrier, inc=1, device_id={"rows": lax.rem(me + d, n)}, device_id_type=MESH
        )
    greeted = n - 1
    for other in range(depth):

        @pl.when(linked(other))
        def _():
            pl.semaphore_signal(barrier, inc=1, device_id={"cols": other}, device_id_type=MESH)

        greeted = greeted + jnp.where(linked(other), 1, 0)
    pl.semaphore_wait(barrier, greeted)

    def row_copy(src, dst, send, recv, to):
        return pltpu.make_async_remote_copy(
            src_ref=src,
            dst_ref=dst,
            send_sem=send,
            recv_sem=recv,
            device_id={"rows": to},
            device_id_type=MESH,
        )

    def p1(d, to):
        return row_copy(
            panel.at[pl.ds(to * tp, tp)],
            ring_p.at[:, mine],
            p1_send.at[d - 1],
            p1_recv.at[d - 1],
            to,
        )

    def p2(d, to):
        return row_copy(
            moved_p.at[to],
            full.at[z, pl.ds(me * tp, tp)],
            p2_send.at[d - 1],
            p2_recv.at[d - 1],
            to,
        )

    def t1(t, d, to):
        return row_copy(
            trail.at[to * tt + t],
            rings[t].at[mine],
            t1_send.at[t, d - 1],
            t1_recv.at[t, d - 1],
            to,
        )

    def t2(t, d, to):
        return row_copy(
            moved_t.at[t, to],
            reg.at[me, t],
            t2_send.at[t, d - 1],
            t2_recv.at[t, d - 1],
            to,
        )

    own_p = pltpu.make_async_copy(
        panel.at[pl.ds(me * tp, tp)], ring_p.at[:, mine], local_sem.at[0]
    )

    def own_t(t):
        return pltpu.make_async_copy(
            trail.at[me * tt + t], rings[t].at[mine], local_sem.at[1 + t]
        )

    def started(copies, active, count):
        def go(d, to, origin):
            @only(active(to), count == n)
            def _():
                copies(d, to).start()

        each_peer(go)

    def landed(copies, active, count, by_origin):
        def go(d, to, origin):
            @only(active(origin if by_origin else me), count == n)
            def _():
                copies(d, to).wait_recv()

        each_peer(go)

    def left(copies, active, count, by_target):
        def go(d, to, origin):
            @only(active(to if by_target else me), count == n)
            def _():
                copies(d, to).wait_send()

        each_peer(go)

    def has_p(j):
        return j < op

    def has_t(j):
        return j < ot

    sub = lax.broadcasted_iota(jnp.int32, (1, SUB, BW), 1)
    step = min(16, blocks)

    def compose(ring, shifts, to, put):
        starts = [lax.rem(to * blocks - s + total, total) for s in shifts]
        for h in range(0, blocks, step):
            block = ring[pl.ds(starts[0] + h, step)]
            for c in range(1, SUB):
                block = jnp.where(sub == c, ring[pl.ds(starts[c] + h, step)], block)
            put(h, block)

    def wrap(ring):
        ring[pl.ds(total, blocks)] = ring[pl.ds(0, blocks)]

    def line(side, d, q):
        step_z = 1 if side == 0 else -1
        origin = z - step_z * (d - 1)
        rows = pl.ds(q * (ctp // pieces), ctp // pieces)
        return pltpu.make_async_remote_copy(
            src_ref=full.at[origin, rows],
            dst_ref=full.at[origin, rows],
            send_sem=z_send.at[side, d - 1, q],
            recv_sem=z_recv.at[side, d - 1, q],
            device_id={"cols": z + step_z},
            device_id_type=MESH,
        )

    def sends(side, d):
        if side == 0:
            return (z + 1 < depth) & (z - (d - 1) >= 0)
        return (z >= 1) & (z + (d - 1) < depth)

    def receives(side, d):
        return z - d >= 0 if side == 0 else z + d < depth

    def arrived(side, d, q):
        step_z = 1 if side == 0 else -1
        origin = z - step_z * d
        rows = pl.ds(q * (ctp // pieces), ctp // pieces)
        return pltpu.make_async_remote_copy(
            src_ref=full.at[origin, rows],
            dst_ref=full.at[origin, rows],
            send_sem=z_send.at[side, d - 1, q],
            recv_sem=z_recv.at[side, d - 1, q],
            device_id={"cols": z - step_z},
            device_id_type=MESH,
        )

    def forward(d):
        for q in range(pieces):
            for side in (0, 1):

                @pl.when(receives(side, d))
                def _():
                    arrived(side, d, q).wait_recv()

                if d + 1 < depth:

                    @pl.when(sends(side, d + 1))
                    def _():
                        line(side, d + 1, q).start()

    def start_t1(t):
        @only(has_t(me), ot == n)
        def _():
            own_t(t).start()

        started(functools.partial(t1, t), has_t, ot)

    def turn_t(t):
        @only(has_t(me), ot == n)
        def _():
            own_t(t).wait()

        landed(functools.partial(t1, t), has_t, ot, False)

        @only(has_t(me), ot == n)
        def _():
            wrap(rings[t])
            shifts = [trail_shift[(me * tt + t) * SUB + c] for c in range(SUB)]

            def turn(d, to, origin):
                def put(h, block):
                    moved_t[t, to, pl.ds(h, step)] = block

                compose(rings[t], shifts, to, put)

            each_peer(turn)

            def keep(h, block):
                reg[me, t, pl.ds(h, step)] = block

            compose(rings[t], shifts, me, keep)

    def start_t2(t):
        def go(d, to, origin):
            t2(t, d, to).start()

        @only(has_t(me), ot == n)
        def _():
            each_peer(go)

    def wait_t2(t):
        landed(functools.partial(t2, t), has_t, ot, True)

    def panel_block(b, count):
        cut = [full[:, :, count * b + k].reshape(size, BW) for k in range(count)]
        return jnp.concatenate(cut, axis=1)

    narrow = min(4, blocks)
    wide = min(8, blocks)

    def make_gram():
        gram_part[...] = jnp.zeros_like(gram_part)

        def body(b, carry):
            block = panel_block(b, narrow)
            gram_part[...] += rows_dot(block, block, HIGHEST).reshape(gram_part.shape)
            return carry

        lax.fori_loop(0, blocks // narrow, body, 0)

    def g_one(d, to):
        return row_copy(
            gram_part.at[to], gram_land.at[d - 1], g_send.at[0, d - 1], g_recv.at[0, d - 1], to
        )

    def g_two(d, to):
        return row_copy(
            gram_sum.at[me], gram_sum.at[me], g_send.at[1, d - 1], g_recv.at[1, d - 1], to
        )

    def every(j):
        return j >= 0

    def has_c(j):
        return j < oc

    def make_cross(t):
        cross_part[t] = jnp.zeros_like(cross_part[t])

        def body(b, carry):
            cut = [reg[:, t, wide * b + k].reshape(rows_t, BW) for k in range(wide)]
            block = jnp.concatenate(cut, axis=1)
            both = rows_dot(block, panel_block(b, wide), HIGH)
            cross_part[t] += both.reshape(oc, sr, size)
            return carry

        lax.fori_loop(0, blocks // wide, body, 0)

    def c_one(t, d, to):
        return row_copy(
            cross_part.at[t, to],
            cross_land.at[t, d - 1],
            c_send.at[0, t, d - 1],
            c_recv.at[0, t, d - 1],
            to,
        )

    def c_two(t, d, to):
        return row_copy(
            cross_ref.at[t, me],
            cross_ref.at[t, me],
            c_send.at[1, t, d - 1],
            c_recv.at[1, t, d - 1],
            to,
        )

    def cross_scatter(t):
        started(functools.partial(c_one, t), has_c, oc)

    def cross_spread(t):
        @only(has_c(me), oc == n)
        def _():
            total_c = cross_part[t, me]
            for d in range(1, n):
                c_one(t, d, lax.rem(me + d, n)).wait_recv()
                total_c = total_c + cross_land[t, d - 1]
            cross_ref[t, me] = total_c

            def go(d, to, origin):
                c_two(t, d, to).start()

            each_peer(go)

    def cross_done(t):
        landed(functools.partial(c_two, t), has_c, oc, True)

    tile = min(64, size)
    tiles = size // tile
    low_count = mid_lo
    high_count = depth - 1 - mid_hi

    def factor_copy(i, k, slot, to):
        ref = inv_ref if k == 0 else upper_ref
        rows = pl.ds(i * tile, tile)
        return pltpu.make_async_remote_copy(
            src_ref=ref.at[rows],
            dst_ref=ref.at[rows],
            send_sem=f_send.at[slot, i, k],
            recv_sem=f_recv.at[i, k],
            device_id={"cols": to},
            device_id_type=MESH,
        )

    def factor_sends(act):
        for k in (0, 1):
            for i in range(tiles):
                send_factor(i, k, act)

    def send_factor(i, k, act):
        for slot in range(low_count):

            @pl.when(z == mid_lo)
            def _():
                act(factor_copy(i, k, slot, slot))

        for slot in range(high_count):

            @pl.when(z == mid_hi)
            def _():
                act(factor_copy(i, k, slot, mid_hi + 1 + slot))

    def factor_tile(i):
        lo = i * tile
        hi = lo + tile
        row = lax.broadcasted_iota(jnp.int32, (tile, 2 * tile), 0)
        col = lax.broadcasted_iota(jnp.int32, (tile, 2 * tile), 1)
        pair[...] = jnp.where(col == row + tile, 1.0, 0.0)
        pair[:, 0:tile] = aug[lo:hi, lo:hi]
        w = pair[...]
        pivots = jnp.zeros((tile, 1), F32)
        for j in range(tile):
            base = j // 8 * 8
            live = w[base:, :]
            lead = w[j : j + 1, :]
            pivot = lead[:, j : j + 1]
            pivots = jnp.where(row[:, 0:1] == j, pivot, pivots)
            if j + 1 == tile:
                break
            mult = jnp.where(row[base:, 0:1] > j, live[:, j : j + 1], 0.0)
            live = live - mult * (lead / pivot)
            w = live if base == 0 else jnp.concatenate([w[:base], live], axis=0)
        pair[...] = w * (1.0 / jnp.sqrt(pivots))
        inverse = pair[:, tile : 2 * tile]
        lead_rows = plain_dot(inverse, aug[lo:hi, :], HIGHEST)
        grow = lax.broadcasted_iota(jnp.int32, (tile, size), 0) + lo
        gcol = lax.broadcasted_iota(jnp.int32, (tile, size), 1)
        upper = jnp.where(gcol >= grow, lead_rows[:, 0:size], 0.0)
        upper_ref[lo:hi, :] = upper * (1.0 / root)
        inv_ref[lo:hi, :] = lead_rows[:, size : 2 * size]
        if hi < size:
            aug[...] = aug[...] - lax.dot_general(
                upper,
                lead_rows,
                (((0,), (0,)), ((), ())),
                precision=HIGHEST,
                preferred_element_type=F32,
            )

    def make_basis():
        factor = inv_ref[...]
        own = pl.ds(pl.multiple_of(z * (ctp * SUB), ctp * SUB), ctp * SUB)

        def body(b, carry):
            both = plain_dot(factor, panel_block(b, narrow), HIGH)
            mine_only = plain_dot(inv_ref[own, :] * root, panel_block(b, narrow), HIGH)
            for k in range(narrow):
                lanes = slice(k * BW, (k + 1) * BW)
                place = narrow * b + k
                part = both[:, lanes]
                upper_half = part.astype(jnp.bfloat16)
                high_ref[place] = upper_half
                low_ref[place] = (part - upper_half.astype(F32)).astype(jnp.bfloat16)
                q_ref[:, place] = mine_only[:, lanes].reshape(ctp, SUB, BW)
            return carry

        lax.fori_loop(0, blocks // narrow, body, 0)

    def emit(chunks):
        for t in chunks:
            cross_done(t)
        rows = [cross_ref[t].reshape(rows_t, size) for t in chunks]
        left_side = three_part(rows_dot(joined(rows), inv_ref[...], HIGHEST))

        def body(b, carry):
            both = removed(left_side, high_ref, low_ref, narrow * b, narrow)
            for k in range(narrow):
                lanes = slice(k * BW, (k + 1) * BW)
                place = narrow * b + k
                for i, t in enumerate(chunks):
                    part = both[i * rows_t : (i + 1) * rows_t, lanes]
                    reg[:, t, place] = reg[:, t, place] - part.reshape(ot, SUB, BW)
            return carry

        lax.fori_loop(0, blocks // narrow, body, 0)

    def start_copy(copy):
        copy.start()

    @only(has_p(me), op == n)
    def _():
        own_p.start()

    started(p1, has_p, op)

    @only(has_p(me), op == n)
    def _():
        own_p.wait()

    landed(p1, has_p, op, False)

    @only(has_p(me), op == n)
    def _():
        for t in range(tp):
            wrap(ring_p.at[t])
        shifts = [
            [panel_shift[(me * tp + t) * SUB + c] for c in range(SUB)] for t in range(tp)
        ]

        def turn(d, to, origin):
            for t in range(tp):

                def put(h, block, t=t):
                    moved_p[to, t, pl.ds(h, step)] = block

                compose(ring_p.at[t], shifts[t], to, put)

        each_peer(turn)

        def go(d, to, origin):
            p2(d, to).start()

        each_peer(go)
        for t in range(tp):

            def keep(h, block, t=t):
                full[z, me * tp + t, pl.ds(h, step)] = block

            compose(ring_p.at[t], shifts[t], me, keep)

    last = tt - 1
    start_t1(0)
    if tt > 1:
        start_t1(1)
    landed(p2, has_p, op, True)
    for q in range(pieces):
        for side in (0, 1):

            @pl.when(sends(side, 1))
            def _():
                line(side, 1, q).start()

    middle = max(depth // 2, 1)
    turn_t(0)
    if last > 0:
        start_t2(0)
    for t in range(2, last):
        start_t1(t)
    if depth > 1:
        forward(1)
    for t in range(1, last):
        turn_t(t)
        if t + 1 < last:
            start_t2(t)
        if t == 1:
            for d in range(2, middle + 1):
                forward(d)
    if last < 2:
        for d in range(2, middle + 1):
            forward(d)

    def rest_t1():
        if last > 1:
            start_t1(last)

    def rest_t2():
        if last > 1:
            start_t2(last - 1)

    def finish_turns():
        if last > 0:
            turn_t(last)
        start_t2(last)

    central = (z == mid_lo) | (z == mid_hi)

    def cross_chunk(t):
        wait_t2(t)
        make_cross(t)
        cross_scatter(t)

    early = min(2, last)

    @pl.when(central)
    def _():
        make_gram()
        started(g_one, every, n)
        aug_row = lax.broadcasted_iota(jnp.int32, (size, size), 0)
        aug_col = lax.broadcasted_iota(jnp.int32, (size, size), 1)
        aug[:, size : 2 * size] = jnp.where(aug_row == aug_col, 1.0, 0.0)
        if early > 0:
            cross_chunk(0)
        total_g = gram_part[me]
        for d in range(1, n):
            g_one(d, lax.rem(me + d, n)).wait_recv()
            total_g = total_g + gram_land[d - 1]
        gram_sum[me] = total_g
        started(g_two, every, n)
        rest_t1()
        rest_t2()
        if early > 1:
            cross_chunk(1)
        landed(g_two, every, n, True)
        aug[:, 0:size] = gram_sum[...].reshape(size, size)
        for i in range(tiles):
            factor_tile(i)
            send_factor(i, 0, start_copy)
            if i == min(1, tiles - 1):
                finish_turns()
        for i in range(tiles):
            send_factor(i, 1, start_copy)
        for t in range(early):
            cross_spread(t)
        for t in range(early, last):
            cross_chunk(t)
        left(g_one, every, n, True)
        left(g_two, every, n, True)

    @pl.when(jnp.logical_not(central))
    def _():
        rest_t1()
        rest_t2()
        for d in range(middle + 1, depth):
            forward(d)
        finish_turns()
        for t in range(last):
            cross_chunk(t)
        for t in range(early):
            cross_spread(t)

    cross_chunk(last)

    @pl.when(jnp.logical_not(central))
    def _():
        for i in range(tiles):
            factor_copy(i, 0, 0, mid_lo).wait_recv()

    make_basis()
    for t in range(early, tt):
        cross_spread(t)
    if early > 0:
        emit(list(range(early)))
    for t in range(early, tt):
        cross_done(t)

    @pl.when(jnp.logical_not(central))
    def _():
        for i in range(tiles):
            factor_copy(i, 1, 0, mid_lo).wait_recv()

    @pl.when(central)
    def _():
        factor_sends(lambda copy: copy.wait_send())

    left(p1, has_p, op, True)
    left(p2, has_p, op, False)
    for t in range(tt):
        left(functools.partial(t1, t), has_t, ot, True)
        left(functools.partial(t2, t), has_t, ot, False)
        left(functools.partial(c_one, t), has_c, oc, True)
        left(functools.partial(c_two, t), has_c, oc, False)
    for d in range(1, depth):
        for q in range(pieces):
            for side in (0, 1):

                @pl.when(sends(side, d))
                def _():
                    line(side, d, q).wait_send()


def fused(panel, trail, panel_shift, trail_shift, n, depth, root):
    ctp, blocks = panel.shape[0], panel.shape[1]
    ctt = trail.shape[0]
    tp = -(-ctp // n)
    tt = -(-ctt // n)
    op, ot = ctp // tp, ctt // tt
    size = depth * ctp * SUB
    rows_t = ot * SUB
    sr = max(SUB, rows_t // n)
    oc = rows_t // sr
    tiles = max(size // 64, 1)
    pieces = 4 if ctp % 4 == 0 else 1
    total = n * blocks
    smem = pl.BlockSpec(memory_space=pltpu.SMEM)
    vmem = pl.BlockSpec(memory_space=pltpu.VMEM)
    hbm = pl.BlockSpec(memory_space=pl.ANY)
    dma = pltpu.SemaphoreType.DMA
    peers = max(n - 1, 1)
    lines = max(depth - 1, 1)
    return pl.pallas_call(
        functools.partial(fused_kernel, n, depth, pieces, root),
        out_shape=(
            pltpu.VMEM((size, size), F32),
            pltpu.VMEM((size, size), F32),
            pltpu.VMEM((tt, oc, sr, size), F32),
            pltpu.VMEM(panel.shape, F32),
            pltpu.VMEM((ot, tt) + trail.shape[1:], F32),
            pltpu.VMEM((blocks, size, BW), jnp.bfloat16),
            pltpu.VMEM((blocks, size, BW), jnp.bfloat16),
        ),
        in_specs=[smem, smem, hbm, hbm],
        out_specs=(vmem,) * 7,
        scratch_shapes=[
            pltpu.VMEM((depth,) + panel.shape, F32),
            pltpu.VMEM((tp, total + blocks, SUB, BW), F32),
            pltpu.VMEM((n, tp, blocks, SUB, BW), F32),
            pltpu.VMEM((tt, n, blocks, SUB, BW), F32),
            pltpu.VMEM((n, size // n, size), F32),
            pltpu.VMEM((peers, size // n, size), F32),
            pltpu.VMEM((n, size // n, size), F32),
            pltpu.VMEM((tt, oc, sr, size), F32),
            pltpu.VMEM((tt, peers, sr, size), F32),
            pltpu.VMEM((size, 2 * size), F32),
            pltpu.VMEM((size // tiles, 2 * (size // tiles)), F32),
            dma((peers,)),
            dma((peers,)),
            dma((peers,)),
            dma((peers,)),
            dma((tt, peers)),
            dma((tt, peers)),
            dma((tt, peers)),
            dma((tt, peers)),
            dma((2, lines, pieces)),
            dma((2, lines, pieces)),
            dma((2, peers)),
            dma((2, peers)),
            dma((2, tt, peers)),
            dma((2, tt, peers)),
            dma((lines, tiles, 2)),
            dma((tiles, 2)),
            dma((1 + tt,)),
        ]
        + [pltpu.VMEM((total + blocks, SUB, BW), F32)] * tt,
        compiler_params=pltpu.CompilerParams(
            collective_id=3, has_side_effects=True, vmem_limit_bytes=40 << 20
        ),
        cost_estimate=pl.CostEstimate(
            flops=0, bytes_accessed=40 * trail.size * 4, transcendentals=0
        ),
    )(panel_shift, trail_shift, panel, trail)


def final_kernel(
    root,
    early,
    upper,
    inv,
    cross,
    q,
    reg,
    high_ref,
    low_ref,
    r_ref,
    coupling_ref,
    q_ref,
    out_ref,
    late,
    coupling,
    sems,
):
    size = inv.shape[0]
    ot, tt, blocks = reg.shape[:3]
    rows_t = ot * SUB
    chunks = list(range(early, tt))
    steps = 2 if blocks % 2 == 0 else 1
    span = blocks // steps
    copies = [pltpu.make_async_copy(q, q_ref, sems.at[0])]
    copies.append(pltpu.make_async_copy(upper, r_ref, sems.at[1]))
    for t in range(early):
        copies.append(pltpu.make_async_copy(reg.at[:, t], out_ref.at[:, t], sems.at[2 + t]))
    for copy in copies:
        copy.start()
    rows = joined([cross[t].reshape(rows_t, size) for t in chunks])
    left_side = three_part(rows_dot(rows, inv[...], HIGHEST))
    narrow = min(4, span)
    for h in range(steps):

        def body(b, carry, h=h):
            first = h * span + narrow * b
            both = removed(left_side, high_ref, low_ref, first, narrow)
            for k in range(narrow):
                lanes = slice(k * BW, (k + 1) * BW)
                for i, t in enumerate(chunks):
                    part = both[i * rows_t : (i + 1) * rows_t, lanes]
                    late[:, i, first + k] = reg[:, t, first + k] - part.reshape(ot, SUB, BW)
            return carry

        lax.fori_loop(0, span // narrow, body, 0)
        for i, t in enumerate(chunks):
            place = pl.ds(h * span, span)
            copy = pltpu.make_async_copy(
                late.at[:, i, place], out_ref.at[:, t, place], sems.at[2 + early + h * len(chunks) + i]
            )
            copy.start()
            copies.append(copy)
    every = jnp.stack([cross[t].reshape(ot, SUB, size) for t in range(tt)], axis=1)
    coupling[...] = rows_dot(
        inv[...] * (1.0 / root), every.reshape(ot * tt * SUB, size), HIGHEST
    )
    last = pltpu.make_async_copy(coupling, coupling_ref, sems.at[2 + early + steps * len(chunks)])
    last.start()
    copies.append(last)
    for copy in copies:
        copy.wait()


def final(upper, inv, cross, q, reg, high, low, root):
    size = inv.shape[0]
    ot, tt = reg.shape[:2]
    early = min(2, tt - 1)
    vmem = pl.BlockSpec(memory_space=pltpu.VMEM)
    hbm = pl.BlockSpec(memory_space=pl.ANY)
    near = [pltpu.with_memory_space_constraint(x, pltpu.VMEM) for x in (upper, inv, cross, q, reg, high, low)]
    return pl.pallas_call(
        functools.partial(final_kernel, root, early),
        out_shape=(
            jax.ShapeDtypeStruct((size, size), F32),
            jax.ShapeDtypeStruct((size, ot * tt * SUB), F32),
            jax.ShapeDtypeStruct(q.shape, F32),
            jax.ShapeDtypeStruct(reg.shape, F32),
        ),
        in_specs=[vmem] * 7,
        out_specs=(hbm,) * 4,
        scratch_shapes=[
            pltpu.VMEM((ot, tt - early) + reg.shape[2:], F32),
            pltpu.VMEM((size, ot * tt * SUB), F32),
            pltpu.SemaphoreType.DMA((3 + early + 2 * (tt - early),)),
        ],
        compiler_params=pltpu.CompilerParams(vmem_limit_bytes=24 << 20),
        cost_estimate=pl.CostEstimate(
            flops=2 * size * reg.size, bytes_accessed=8 * reg.size, transcendentals=0
        ),
    )(*near)


def tiled(raw):
    rows, pixels = raw.shape
    return raw.reshape(rows // SUB, SUB, pixels // BW, BW).transpose(0, 2, 1, 3)


def flat(blocked):
    cut, blocks = blocked.shape[0], blocked.shape[1]
    return blocked.transpose(0, 2, 1, 3).reshape(cut * SUB, blocks * BW)


def on_device(raw_panel, raw_trail, panel_shift, trail_shift):
    n = lax.axis_size("rows")
    depth = lax.axis_size("cols")
    pixels = raw_panel.shape[1]
    root = math.sqrt(pixels * n)
    raw = [
        pltpu.with_memory_space_constraint(tiled(x), pltpu.HBM) for x in (raw_panel, raw_trail)
    ]
    held = fused(
        *raw, panel_shift, trail_shift, n, depth, root
    )
    r_factor, coupling, q_panel, out = final(*held, root)
    return (r_factor, coupling, flat(q_panel), flat(out.reshape((-1,) + out.shape[2:])))


def solution(mesh):
    placed = (P("cols", "rows"), P("cols", "rows"), P("cols"), P("cols"))
    return jax.shard_map(
        on_device,
        mesh=mesh,
        in_specs=placed,
        out_specs=(P(), P(None, "cols"), P("cols", "rows"), P("cols", "rows")),
        check_vma=False,
    )
```

```python
import functools
import math

import jax
import jax.numpy as jnp
from jax import lax
from jax.experimental import pallas as pl
from jax.experimental.pallas import tpu as pltpu
from jax.sharding import PartitionSpec as P

BW = 128
SUB = 8
MESH = pl.DeviceIdType.MESH
F32 = jnp.float32
HIGHEST = lax.Precision.HIGHEST
HIGH = lax.Precision.HIGH


def rows_dot(left, right, precision):
    return lax.dot_general(
        left,
        right,
        (((1,), (1,)), ((), ())),
        precision=precision,
        preferred_element_type=F32,
    )


def plain_dot(left, right, precision):
    return lax.dot_general(
        left,
        right,
        (((1,), (0,)), ((), ())),
        precision=precision,
        preferred_element_type=F32,
    )


def joined(parts):
    return jnp.concatenate(parts, axis=0) if len(parts) > 1 else parts[0]


def three_part(value):
    high = value.astype(jnp.bfloat16)
    low = (value - high.astype(F32)).astype(jnp.bfloat16)
    return jnp.concatenate([high, high, low], axis=1)


def removed(left_side, high_ref, low_ref, first, count):
    high = jnp.concatenate([high_ref[first + k] for k in range(count)], axis=1)
    low = jnp.concatenate([low_ref[first + k] for k in range(count)], axis=1)
    return plain_dot(left_side, jnp.concatenate([high, low, high], axis=0), None)


def only(cond, always):
    if always:
        return lambda fn: fn()
    return pl.when(cond)


def fused_kernel(
    n,
    depth,
    pieces,
    root,
    panel_shift,
    trail_shift,
    panel,
    trail,
    upper_ref,
    inv_ref,
    cross_ref,
    q_ref,
    reg,
    high_ref,
    low_ref,
    full,
    ring_p,
    moved_p,
    moved_t,
    near_part,
    near_land,
    near_sum,
    far_part,
    far_land,
    far_sum,
    cross_part,
    cross_land,
    aug,
    pair,
    p1_send,
    p1_recv,
    p2_send,
    p2_recv,
    t1_send,
    t1_recv,
    t2_send,
    t2_recv,
    z_send,
    z_recv,
    g_send,
    g_recv,
    c_send,
    c_recv,
    f_send,
    f_recv,
    local_sem,
    *rings,
):
    me = lax.axis_index("rows")
    z = lax.axis_index("cols")
    ctp, blocks = panel.shape[0], panel.shape[1]
    ctt = trail.shape[0]
    total = n * blocks
    tp = ring_p.shape[0]
    tt = len(rings)
    op, ot = ctp // tp, ctt // tt
    rows_t = ot * SUB
    sr = cross_land.shape[2]
    oc = rows_t // sr
    size = inv_ref.shape[0]
    lead_z = max(depth // 2 - 1, 0)
    leads = z == lead_z
    tile = pair.shape[0]
    tiles = size // tile
    edge = size - tile
    near_count = edge // (ctp * SUB)
    mine = pl.ds(pl.multiple_of(me * blocks, blocks), blocks)

    def each_peer(fn):
        def body(d, carry):
            fn(d, lax.rem(me + d, n), lax.rem(me - d + n, n))
            return carry

        lax.fori_loop(1, n, body, 0)

    def linked(other):
        near = (z - other == 1) | (other - z == 1)
        return near | (z != other) & (leads | (other == lead_z))

    barrier = pltpu.get_barrier_semaphore()
    for d in range(1, n):
        pl.semaphore_signal(
            barrier, inc=1, device_id={"rows": lax.rem(me + d, n)}, device_id_type=MESH
        )
    greeted = n - 1
    for other in range(depth):

        @pl.when(linked(other))
        def _():
            pl.semaphore_signal(barrier, inc=1, device_id={"cols": other}, device_id_type=MESH)

        greeted = greeted + jnp.where(linked(other), 1, 0)
    pl.semaphore_wait(barrier, greeted)

    def row_copy(src, dst, send, recv, to):
        return pltpu.make_async_remote_copy(
            src_ref=src,
            dst_ref=dst,
            send_sem=send,
            recv_sem=recv,
            device_id={"rows": to},
            device_id_type=MESH,
        )

    def p1(d, to):
        return row_copy(
            panel.at[pl.ds(to * tp, tp)],
            ring_p.at[:, mine],
            p1_send.at[0],
            p1_recv.at[0],
            to,
        )

    def p2(d, to):
        return row_copy(
            moved_p.at[to],
            full.at[z, pl.ds(me * tp, tp)],
            p2_send.at[0],
            p2_recv.at[0],
            to,
        )

    def t1(t, d, to):
        return row_copy(
            trail.at[to * tt + t],
            rings[t].at[mine],
            t1_send.at[t],
            t1_recv.at[t],
            to,
        )

    def t2(t, d, to):
        return row_copy(
            moved_t.at[t, to],
            reg.at[me, t],
            t2_send.at[t],
            t2_recv.at[t],
            to,
        )

    own_p = pltpu.make_async_copy(
        panel.at[pl.ds(me * tp, tp)], ring_p.at[:, mine], local_sem.at[0]
    )

    def own_t(t):
        return pltpu.make_async_copy(
            trail.at[me * tt + t], rings[t].at[mine], local_sem.at[1 + t]
        )

    def started(copies, active, count, first=1, stride=1):
        def go(k, carry):
            d = first + stride * k
            to = lax.rem(me + d, n)

            @only(active(to), count == n)
            def _():
                copies(d, to).start()

            return carry

        lax.fori_loop(0, -(-(n - first) // stride), go, 0)

    def whole(region, send, recv):
        return row_copy(region, region, send, recv, lax.rem(me + 1, n))

    def counted(active, count, per_copy, done):
        if count == n:
            done(per_copy(n - 1))
        else:

            @pl.when(active(me))
            def _():
                done(per_copy(count - 1))

            @pl.when(jnp.logical_not(active(me)))
            def _():
                done(per_copy(count))

    def once(active, count, per_copy, done):
        @only(active(me), count == n)
        def _():
            done(per_copy(n - 1))

    def take(copy):
        copy.wait_recv()

    def clear(copy):
        copy.wait_send()

    def has_p(j):
        return j < op

    def has_t(j):
        return j < ot

    sub = lax.broadcasted_iota(jnp.int32, (1, SUB, BW), 1)
    step = min(16, blocks)

    def compose(ring, shifts, to, put):
        starts = [lax.rem(to * blocks - s + total, total) for s in shifts]
        for h in range(0, blocks, step):
            block = ring[pl.ds(starts[0] + h, step)]
            for c in range(1, SUB):
                block = jnp.where(sub == c, ring[pl.ds(starts[c] + h, step)], block)
            put(h, block)

    def wrap(ring):
        ring[pl.ds(total, blocks)] = ring[pl.ds(0, blocks)]

    def line(side, d, q):
        step_z = 1 if side == 0 else -1
        origin = z - step_z * (d - 1)
        rows = pl.ds(q * (ctp // pieces), ctp // pieces)
        return pltpu.make_async_remote_copy(
            src_ref=full.at[origin, rows],
            dst_ref=full.at[origin, rows],
            send_sem=z_send.at[side, d - 1, q],
            recv_sem=z_recv.at[side, d - 1, q],
            device_id={"cols": z + step_z},
            device_id_type=MESH,
        )

    def sends(side, d):
        if side == 0:
            return (z + 1 < depth) & (z - (d - 1) >= 0)
        return (z >= 1) & (z + (d - 1) < depth)

    def receives(side, d):
        return z - d >= 0 if side == 0 else z + d < depth

    def arrived(side, d, q):
        step_z = 1 if side == 0 else -1
        origin = z - step_z * d
        rows = pl.ds(q * (ctp // pieces), ctp // pieces)
        return pltpu.make_async_remote_copy(
            src_ref=full.at[origin, rows],
            dst_ref=full.at[origin, rows],
            send_sem=z_send.at[side, d - 1, q],
            recv_sem=z_recv.at[side, d - 1, q],
            device_id={"cols": z - step_z},
            device_id_type=MESH,
        )

    def forward(d, some=None):
        for q in range(pieces) if some is None else some:
            for side in (0, 1):

                @pl.when(receives(side, d))
                def _():
                    arrived(side, d, q).wait_recv()

                if d + 1 < depth:

                    @pl.when(sends(side, d + 1))
                    def _():
                        line(side, d + 1, q).start()

    def start_t1(t, halves=(0, 1)):
        if 0 in halves:

            @only(has_t(me), ot == n)
            def _():
                own_t(t).start()

        if len(halves) == 2:
            started(functools.partial(t1, t), has_t, ot)
        else:
            started(functools.partial(t1, t), has_t, ot, 2 - halves[0], 2)

    def turn_t(t):
        @only(has_t(me), ot == n)
        def _():
            own_t(t).wait()

        once(has_t, ot, lambda k: whole(rings[t].at[pl.ds(0, k * blocks)], t1_send.at[t], t1_recv.at[t]), take)

        @only(has_t(me), ot == n)
        def _():
            wrap(rings[t])
            shifts = [trail_shift[(me * tt + t) * SUB + c] for c in range(SUB)]

            def turn(d, to, origin):
                def put(h, block):
                    moved_t[t, to, pl.ds(h, step)] = block

                compose(rings[t], shifts, to, put)

            each_peer(turn)

            def keep(h, block):
                reg[me, t, pl.ds(h, step)] = block

            compose(rings[t], shifts, me, keep)

    def start_t2(t, halves=(0, 1)):
        @only(has_t(me), ot == n)
        def _():
            if len(halves) == 2:
                started(functools.partial(t2, t), has_t, n)
            else:
                started(functools.partial(t2, t), has_t, n, 2 - halves[0], 2)

    def wait_t2(t):
        counted(has_t, ot, lambda k: whole(reg.at[pl.ds(0, k), t], t2_send.at[t], t2_recv.at[t]), take)

    def panel_block(b, count, lo=0, hi=depth):
        rows = (hi - lo) * ctp * SUB
        cut = [full[lo:hi, :, count * b + k].reshape(rows, BW) for k in range(count)]
        return jnp.concatenate(cut, axis=1)

    narrow = min(4, blocks)
    wide = min(8, blocks)

    def gram_near():
        near_part[...] = jnp.zeros_like(near_part)

        def body(b, carry):
            block = panel_block(b, narrow, 0, near_count)
            near_part[...] += rows_dot(block, block, HIGHEST).reshape(near_part.shape)
            return carry

        lax.fori_loop(0, blocks // narrow, body, 0)

    def gram_far():
        far_part[...] = jnp.zeros_like(far_part)

        def body(b, carry):
            block = panel_block(b, narrow, near_count, depth)
            both = rows_dot(block, panel_block(b, narrow), HIGHEST)
            far_part[...] += both.reshape(far_part.shape)
            return carry

        lax.fori_loop(0, blocks // narrow, body, 0)

    grams = ((near_part, near_land, near_sum), (far_part, far_land, far_sum))

    def g_one(k, d, to):
        part, land, _ = grams[k]
        return row_copy(part.at[to], land.at[d - 1], g_send.at[k, 0], g_recv.at[k, 0], to)

    def g_two(k, d, to):
        ref = grams[k][2]
        return row_copy(ref.at[me], ref.at[me], g_send.at[k, 1], g_recv.at[k, 1], to)

    def g_count(k):
        return grams[k][0].shape[0]

    def has_g(k):
        return lambda j: j < g_count(k)

    def gram_scatter(k):
        started(functools.partial(g_one, k), has_g(k), g_count(k))

    def gram_spread(k):
        part, land, total_ref = grams[k]

        @only(me < g_count(k), g_count(k) == n)
        def _():
            take(whole(land, g_send.at[k, 0], g_recv.at[k, 0]))
            total_g = part[me]
            for d in range(1, n):
                total_g = total_g + land[d - 1]
            total_ref[me] = total_g

            def go(d, to, origin):
                g_two(k, d, to).start()

            each_peer(go)

    def gram_done(k):
        ref = grams[k][2]
        counted(has_g(k), g_count(k), lambda m: whole(ref.at[pl.ds(0, m)], g_send.at[k, 1], g_recv.at[k, 1]), take)

    def has_c(j):
        return j < oc

    def make_cross(t):
        cross_part[t] = jnp.zeros_like(cross_part[t])

        def body(b, carry):
            cut = [reg[:, t, wide * b + k].reshape(rows_t, BW) for k in range(wide)]
            block = jnp.concatenate(cut, axis=1)
            both = rows_dot(block, panel_block(b, wide), HIGH)
            cross_part[t] += both.reshape(oc, sr, size)
            return carry

        lax.fori_loop(0, blocks // wide, body, 0)

    def c_one(t, d, to):
        return row_copy(
            cross_part.at[t, to],
            cross_land.at[t, d - 1],
            c_send.at[0, t],
            c_recv.at[0, t],
            to,
        )

    def c_two(t, d, to):
        return row_copy(
            cross_ref.at[t, me],
            cross_ref.at[t, me],
            c_send.at[1, t],
            c_recv.at[1, t],
            to,
        )

    def cross_scatter(t):
        started(functools.partial(c_one, t), has_c, oc)

    def cross_spread(t):
        @only(has_c(me), oc == n)
        def _():
            take(whole(cross_land.at[t], c_send.at[0, t], c_recv.at[0, t]))
            total_c = cross_part[t, me]
            for d in range(1, n):
                total_c = total_c + cross_land[t, d - 1]
            cross_ref[t, me] = total_c

            def go(d, to, origin):
                c_two(t, d, to).start()

            each_peer(go)

    def cross_done(t):
        counted(has_c, oc, lambda k: whole(cross_ref.at[t, pl.ds(0, k)], c_send.at[1, t], c_recv.at[1, t]), take)

    def factor_copy(i, k, slot, to):
        ref = inv_ref if k == 0 else upper_ref
        rows = pl.ds(i * tile, tile)
        return pltpu.make_async_remote_copy(
            src_ref=ref.at[rows],
            dst_ref=ref.at[rows],
            send_sem=f_send.at[slot, k],
            recv_sem=f_recv.at[k],
            device_id={"cols": to},
            device_id_type=MESH,
        )

    def factor_whole(k, slot=0):
        ref = inv_ref if k == 0 else upper_ref
        return pltpu.make_async_remote_copy(
            src_ref=ref,
            dst_ref=ref,
            send_sem=f_send.at[slot, k],
            recv_sem=f_recv.at[k],
            device_id={"cols": lax.rem(z + 1, depth)},
            device_id_type=MESH,
        )

    def send_factor(i, k, act):
        for other in range(depth):
            if other != lead_z:
                act(factor_copy(i, k, other, other))

    def factor_tile(i):
        lo = i * tile
        hi = lo + tile
        row = lax.broadcasted_iota(jnp.int32, (tile, 2 * tile), 0)
        col = lax.broadcasted_iota(jnp.int32, (tile, 2 * tile), 1)
        pair[...] = jnp.where(col == row + tile, 1.0, 0.0)
        pair[:, 0:tile] = aug[lo:hi, lo:hi]
        w = pair[...]
        pivots = jnp.zeros((tile, 1), F32)
        for j in range(tile):
            base = j // 8 * 8
            live = w[base:, :]
            lead = w[j : j + 1, :]
            pivot = lead[:, j : j + 1]
            pivots = jnp.where(row[:, 0:1] == j, pivot, pivots)
            if j + 1 == tile:
                break
            mult = jnp.where(row[base:, 0:1] > j, live[:, j : j + 1], 0.0)
            live = live - mult * (lead / pivot)
            w = live if base == 0 else jnp.concatenate([w[:base], live], axis=0)
        pair[...] = w * (1.0 / jnp.sqrt(pivots))
        inverse = pair[:, tile : 2 * tile]
        lead_rows = plain_dot(inverse, aug[lo:hi, :], HIGHEST)
        grow = lax.broadcasted_iota(jnp.int32, (tile, size), 0) + lo
        gcol = lax.broadcasted_iota(jnp.int32, (tile, size), 1)
        upper = jnp.where(gcol >= grow, lead_rows[:, 0:size], 0.0)
        upper_ref[lo:hi, :] = upper * (1.0 / root)
        inv_ref[lo:hi, :] = lead_rows[:, size : 2 * size]
        if hi < edge:
            aug[...] = aug[...] - lax.dot_general(
                upper,
                lead_rows,
                (((0,), (0,)), ((), ())),
                precision=HIGHEST,
                preferred_element_type=F32,
            )

    def make_basis():
        factor = inv_ref[...]
        own = pl.ds(pl.multiple_of(z * (ctp * SUB), ctp * SUB), ctp * SUB)

        def body(b, carry):
            both = plain_dot(factor, panel_block(b, narrow), HIGH)
            mine_only = plain_dot(inv_ref[own, :] * root, panel_block(b, narrow), HIGH)
            for k in range(narrow):
                lanes = slice(k * BW, (k + 1) * BW)
                place = narrow * b + k
                part = both[:, lanes]
                upper_half = part.astype(jnp.bfloat16)
                high_ref[place] = upper_half
                low_ref[place] = (part - upper_half.astype(F32)).astype(jnp.bfloat16)
                q_ref[:, place] = mine_only[:, lanes].reshape(ctp, SUB, BW)
            return carry

        lax.fori_loop(0, blocks // narrow, body, 0)

    def emit(chunks):
        for t in chunks:
            cross_done(t)
        rows = [cross_ref[t].reshape(rows_t, size) for t in chunks]
        left_side = three_part(rows_dot(joined(rows), inv_ref[...], HIGHEST))

        def body(b, carry):
            both = removed(left_side, high_ref, low_ref, narrow * b, narrow)
            for k in range(narrow):
                lanes = slice(k * BW, (k + 1) * BW)
                place = narrow * b + k
                for i, t in enumerate(chunks):
                    part = both[i * rows_t : (i + 1) * rows_t, lanes]
                    reg[:, t, place] = reg[:, t, place] - part.reshape(ot, SUB, BW)
            return carry

        lax.fori_loop(0, blocks // narrow, body, 0)

    def start_copy(copy):
        copy.start()

    @only(has_p(me), op == n)
    def _():
        own_p.start()

    started(p1, has_p, op)

    @only(has_p(me), op == n)
    def _():
        own_p.wait()

    once(has_p, op, lambda k: whole(ring_p.at[:, pl.ds(0, k * blocks)], p1_send.at[0], p1_recv.at[0]), take)

    @only(has_p(me), op == n)
    def _():
        for t in range(tp):
            wrap(ring_p.at[t])
        shifts = [
            [panel_shift[(me * tp + t) * SUB + c] for c in range(SUB)] for t in range(tp)
        ]

        def turn(d, to, origin):
            for t in range(tp):

                def put(h, block, t=t):
                    moved_p[to, t, pl.ds(h, step)] = block

                compose(ring_p.at[t], shifts[t], to, put)

        each_peer(turn)

        def go(d, to, origin):
            p2(d, to).start()

        each_peer(go)
        for t in range(tp):

            def keep(h, block, t=t):
                full[z, me * tp + t, pl.ds(h, step)] = block

            compose(ring_p.at[t], shifts[t], me, keep)

    last = tt - 1
    start_t1(0)
    if tt > 1:
        start_t1(1)
    counted(has_p, op, lambda k: whole(full.at[z, pl.ds(0, k * tp)], p2_send.at[0], p2_recv.at[0]), take)
    for q in range(pieces):
        for side in (0, 1):

            @pl.when(sends(side, 1))
            def _():
                line(side, 1, q).start()

    middle = max(depth // 2, 1)
    turn_t(0)
    if last > 0:
        start_t2(0)
    follows = jnp.logical_not(leads)

    @pl.when(follows)
    def _():
        for t in range(2, last):
            start_t1(t)

    for d in range(1, middle):
        forward(d)

    def rest_t1():
        if last > 1:
            start_t1(last)

    def rest_t2():
        for t in range(2, last):
            start_t2(t)

    def finish_turns():
        if last > 0:
            turn_t(last)
        start_t2(last)

    def cross_chunk(t):
        wait_t2(t)
        make_cross(t)
        cross_scatter(t)

    early = min(2, last)

    def border():
        far = far_sum[...].reshape(tile, size)
        corner = rows_dot(inv_ref[0:edge, 0:edge], far[:, 0:edge], HIGHEST)
        upper_ref[0:edge, edge:size] = corner * (1.0 / root)

        def turned(right):
            return lax.dot_general(
                corner,
                right,
                (((0,), (0,)), ((), ())),
                precision=HIGHEST,
                preferred_element_type=F32,
            )

        aug[edge:size, edge:size] = far[:, edge:size] - turned(corner)
        aug[edge:size, size : 2 * size] = aug[edge:size, size : 2 * size] - turned(inv_ref[0:edge, :])

    @pl.when(leads)
    def _():
        gram_near()
        gram_scatter(0)
        if last > 2:
            start_t1(2, (0,))
        if last > 1:
            turn_t(1)
        aug_row = lax.broadcasted_iota(jnp.int32, (size, 2 * size), 0)
        aug_col = lax.broadcasted_iota(jnp.int32, (size, 2 * size), 1)
        aug[...] = jnp.where(aug_col == aug_row + size, 1.0, 0.0)
        gram_spread(0)
        for t in range(2, last):
            start_t1(t, (1,) if t == 2 else (0, 1))
        if last > 1:
            start_t2(1)
        forward(middle, range(pieces // 2))
        gram_done(0)
        forward(middle, range(pieces // 2, pieces - 1))
        aug[0:edge, 0:edge] = near_sum[...].reshape(edge, edge)
        for i in range(tiles - 1):
            factor_tile(i)
            send_factor(i, 0, start_copy)
            if i == 0:
                forward(middle, range(pieces - 1, pieces))
                gram_far()
                gram_scatter(1)
                if last > 1:
                    start_t1(last, (0,))
                for t in range(2, last):
                    turn_t(t)
            if i == min(1, tiles - 2):
                gram_spread(1)
                if last > 1:
                    start_t1(last, (1,))
                rest_t2()
        gram_done(1)
        border()
        factor_tile(tiles - 1)
        send_factor(tiles - 1, 0, start_copy)
        for i in range(tiles):
            send_factor(i, 1, start_copy)
        for t in range(early):
            cross_chunk(t)
        finish_turns()
        for k in (0, 1):
            part, land, _ = grams[k]
            row = lambda m: pl.ds(0, m)
            counted(has_g(k), g_count(k), lambda m: whole(land.at[row(m)], g_send.at[k, 0], g_recv.at[k, 0]), clear)
            once(has_g(k), g_count(k), lambda m: whole(land.at[row(m)], g_send.at[k, 1], g_recv.at[k, 1]), clear)

    @pl.when(follows)
    def _():
        for t in range(1, last):
            turn_t(t)
            if t == 1:
                start_t2(t)
                for d in range(middle, middle + 1):
                    forward(d)
        if last < 2:
            for d in range(middle, middle + 1):
                forward(d)
        rest_t1()
        rest_t2()
        finish_turns()
        for d in range(middle + 1, depth):
            forward(d)
        for t in range(early):
            cross_chunk(t)
        factor_whole(0).wait_recv()

    make_basis()
    for t in range(early, last):
        cross_chunk(t)
    for t in range(early):
        cross_spread(t)
    cross_chunk(last)
    for t in range(early, last):
        cross_spread(t)
    cross_spread(last)
    if last > 0:
        emit(list(range(last)))
    cross_done(last)

    @pl.when(follows)
    def _():
        factor_whole(1).wait_recv()

    @pl.when(leads)
    def _():
        for other in range(depth):
            if other != lead_z:
                for k in (0, 1):
                    factor_whole(k, other).wait_send()

    counted(has_p, op, lambda k: whole(ring_p.at[:, pl.ds(0, k * blocks)], p1_send.at[0], p1_recv.at[0]), clear)
    once(has_p, op, lambda k: whole(ring_p.at[:, pl.ds(0, k * blocks)], p2_send.at[0], p2_recv.at[0]), clear)
    for t in range(tt):
        ring = rings[t]
        counted(has_t, ot, lambda k: whole(ring.at[pl.ds(0, k * blocks)], t1_send.at[t], t1_recv.at[t]), clear)
        once(has_t, ot, lambda k: whole(ring.at[pl.ds(0, k * blocks)], t2_send.at[t], t2_recv.at[t]), clear)
        land = cross_land.at[t]
        counted(has_c, oc, lambda k: whole(land.at[pl.ds(0, k)], c_send.at[0, t], c_recv.at[0, t]), clear)
        once(has_c, oc, lambda k: whole(land.at[pl.ds(0, k)], c_send.at[1, t], c_recv.at[1, t]), clear)
    for d in range(1, depth):
        for q in range(pieces):
            for side in (0, 1):

                @pl.when(sends(side, d))
                def _():
                    line(side, d, q).wait_send()


def fused(panel, trail, panel_shift, trail_shift, n, depth, root):
    ctp, blocks = panel.shape[0], panel.shape[1]
    ctt = trail.shape[0]
    tp = -(-ctp // n)
    tt = -(-ctt // n)
    op, ot = ctp // tp, ctt // tt
    size = depth * ctp * SUB
    rows_t = ot * SUB
    sr = max(SUB, rows_t // n)
    oc = rows_t // sr
    tile = 64
    tiles = size // tile
    edge = size - tile
    near_rows = -(-edge // (n * SUB)) * SUB
    far_rows = -(-tile // (n * SUB)) * SUB
    pieces = 4 if ctp % 4 == 0 else 1
    total = n * blocks
    smem = pl.BlockSpec(memory_space=pltpu.SMEM)
    vmem = pl.BlockSpec(memory_space=pltpu.VMEM)
    hbm = pl.BlockSpec(memory_space=pl.ANY)
    dma = pltpu.SemaphoreType.DMA
    peers = max(n - 1, 1)
    lines = max(depth - 1, 1)
    return pl.pallas_call(
        functools.partial(fused_kernel, n, depth, pieces, root),
        out_shape=(
            pltpu.VMEM((size, size), F32),
            pltpu.VMEM((size, size), F32),
            pltpu.VMEM((tt, oc, sr, size), F32),
            pltpu.VMEM(panel.shape, F32),
            pltpu.VMEM((ot, tt) + trail.shape[1:], F32),
            pltpu.VMEM((blocks, size, BW), jnp.bfloat16),
            pltpu.VMEM((blocks, size, BW), jnp.bfloat16),
        ),
        in_specs=[smem, smem, hbm, hbm],
        out_specs=(vmem,) * 7,
        scratch_shapes=[
            pltpu.VMEM((depth,) + panel.shape, F32),
            pltpu.VMEM((tp, total + blocks, SUB, BW), F32),
            pltpu.VMEM((n, tp, blocks, SUB, BW), F32),
            pltpu.VMEM((tt, n, blocks, SUB, BW), F32),
            pltpu.VMEM((edge // near_rows, near_rows, edge), F32),
            pltpu.VMEM((peers, near_rows, edge), F32),
            pltpu.VMEM((edge // near_rows, near_rows, edge), F32),
            pltpu.VMEM((tile // far_rows, far_rows, size), F32),
            pltpu.VMEM((peers, far_rows, size), F32),
            pltpu.VMEM((tile // far_rows, far_rows, size), F32),
            pltpu.VMEM((tt, oc, sr, size), F32),
            pltpu.VMEM((tt, peers, sr, size), F32),
            pltpu.VMEM((size, 2 * size), F32),
            pltpu.VMEM((tile, 2 * tile), F32),
            dma((1,)),
            dma((1,)),
            dma((1,)),
            dma((1,)),
            dma((tt,)),
            dma((tt,)),
            dma((tt,)),
            dma((tt,)),
            dma((2, lines, pieces)),
            dma((2, lines, pieces)),
            dma((2, 2)),
            dma((2, 2)),
            dma((2, tt)),
            dma((2, tt)),
            dma((depth, 2)),
            dma((2,)),
            dma((1 + tt,)),
        ]
        + [pltpu.VMEM((total + blocks, SUB, BW), F32)] * tt,
        compiler_params=pltpu.CompilerParams(
            collective_id=3, has_side_effects=True, vmem_limit_bytes=40 << 20
        ),
        cost_estimate=pl.CostEstimate(
            flops=0, bytes_accessed=40 * trail.size * 4, transcendentals=0
        ),
    )(panel_shift, trail_shift, panel, trail)


def final_kernel(
    root,
    early,
    upper,
    inv,
    cross,
    q,
    reg,
    high_ref,
    low_ref,
    r_ref,
    coupling_ref,
    q_ref,
    out_ref,
    late,
    coupling,
    sems,
):
    size = inv.shape[0]
    ot, tt, blocks = reg.shape[:3]
    rows_t = ot * SUB
    chunks = list(range(early, tt))
    steps = 2 if blocks % 2 == 0 else 1
    span = blocks // steps
    copies = [pltpu.make_async_copy(q, q_ref, sems.at[0])]
    copies.append(pltpu.make_async_copy(upper, r_ref, sems.at[1]))
    for t in range(early):
        copies.append(pltpu.make_async_copy(reg.at[:, t], out_ref.at[:, t], sems.at[2 + t]))
    for copy in copies:
        copy.start()
    rows = joined([cross[t].reshape(rows_t, size) for t in chunks])
    left_side = three_part(rows_dot(rows, inv[...], HIGHEST))
    narrow = min(4, span)
    for h in range(steps):

        def body(b, carry, h=h):
            first = h * span + narrow * b
            both = removed(left_side, high_ref, low_ref, first, narrow)
            for k in range(narrow):
                lanes = slice(k * BW, (k + 1) * BW)
                for i, t in enumerate(chunks):
                    part = both[i * rows_t : (i + 1) * rows_t, lanes]
                    late[:, i, first + k] = reg[:, t, first + k] - part.reshape(ot, SUB, BW)
            return carry

        lax.fori_loop(0, span // narrow, body, 0)
        for i, t in enumerate(chunks):
            place = pl.ds(h * span, span)
            copy = pltpu.make_async_copy(
                late.at[:, i, place], out_ref.at[:, t, place], sems.at[2 + early + h * len(chunks) + i]
            )
            copy.start()
            copies.append(copy)
    every = jnp.stack([cross[t].reshape(ot, SUB, size) for t in range(tt)], axis=1)
    coupling[...] = rows_dot(
        inv[...] * (1.0 / root), every.reshape(ot * tt * SUB, size), HIGHEST
    )
    last = pltpu.make_async_copy(coupling, coupling_ref, sems.at[2 + early + steps * len(chunks)])
    last.start()
    copies.append(last)
    for copy in copies:
        copy.wait()


def final(upper, inv, cross, q, reg, high, low, root):
    size = inv.shape[0]
    ot, tt = reg.shape[:2]
    early = tt - 1
    vmem = pl.BlockSpec(memory_space=pltpu.VMEM)
    hbm = pl.BlockSpec(memory_space=pl.ANY)
    near = [pltpu.with_memory_space_constraint(x, pltpu.VMEM) for x in (upper, inv, cross, q, reg, high, low)]
    return pl.pallas_call(
        functools.partial(final_kernel, root, early),
        out_shape=(
            jax.ShapeDtypeStruct((size, size), F32),
            jax.ShapeDtypeStruct((size, ot * tt * SUB), F32),
            jax.ShapeDtypeStruct(q.shape, F32),
            jax.ShapeDtypeStruct(reg.shape, F32),
        ),
        in_specs=[vmem] * 7,
        out_specs=(hbm,) * 4,
        scratch_shapes=[
            pltpu.VMEM((ot, tt - early) + reg.shape[2:], F32),
            pltpu.VMEM((size, ot * tt * SUB), F32),
            pltpu.SemaphoreType.DMA((3 + early + 2 * (tt - early),)),
        ],
        compiler_params=pltpu.CompilerParams(vmem_limit_bytes=24 << 20),
        cost_estimate=pl.CostEstimate(
            flops=2 * size * reg.size, bytes_accessed=8 * reg.size, transcendentals=0
        ),
    )(*near)


def tiled(raw):
    rows, pixels = raw.shape
    return raw.reshape(rows // SUB, SUB, pixels // BW, BW).transpose(0, 2, 1, 3)


def flat(blocked):
    cut, blocks = blocked.shape[0], blocked.shape[1]
    return blocked.transpose(0, 2, 1, 3).reshape(cut * SUB, blocks * BW)


def on_device(raw_panel, raw_trail, panel_shift, trail_shift):
    n = lax.axis_size("rows")
    depth = lax.axis_size("cols")
    pixels = raw_panel.shape[1]
    root = math.sqrt(pixels * n)
    raw = [
        pltpu.with_memory_space_constraint(tiled(x), pltpu.HBM) for x in (raw_panel, raw_trail)
    ]
    held = fused(
        *raw, panel_shift, trail_shift, n, depth, root
    )
    r_factor, coupling, q_panel, out = final(*held, root)
    return (r_factor, coupling, flat(q_panel), flat(out.reshape((-1,) + out.shape[2:])))


def solution(mesh):
    placed = (P("cols", "rows"), P("cols", "rows"), P("cols"), P("cols"))
    return jax.shard_map(
        on_device,
        mesh=mesh,
        in_specs=placed,
        out_specs=(P(), P(None, "cols"), P("cols", "rows"), P("cols", "rows")),
        check_vma=False,
    )
```

```python
import functools
import math

import jax
import jax.numpy as jnp
from jax import lax
from jax.experimental import pallas as pl
from jax.experimental.pallas import tpu as pltpu
from jax.sharding import PartitionSpec as P

BW = 128
SUB = 8
MESH = pl.DeviceIdType.MESH
F32 = jnp.float32
HIGHEST = lax.Precision.HIGHEST
HIGH = lax.Precision.HIGH


def rows_dot(left, right, precision):
    return lax.dot_general(
        left,
        right,
        (((1,), (1,)), ((), ())),
        precision=precision,
        preferred_element_type=F32,
    )


def plain_dot(left, right, precision):
    return lax.dot_general(
        left,
        right,
        (((1,), (0,)), ((), ())),
        precision=precision,
        preferred_element_type=F32,
    )


def joined(parts):
    return jnp.concatenate(parts, axis=0) if len(parts) > 1 else parts[0]


def three_part(value):
    high = value.astype(jnp.bfloat16)
    low = (value - high.astype(F32)).astype(jnp.bfloat16)
    return jnp.concatenate([high, high, low], axis=1)


def removed(left_side, high_ref, low_ref, first, count):
    high = jnp.concatenate([high_ref[first + k] for k in range(count)], axis=1)
    low = jnp.concatenate([low_ref[first + k] for k in range(count)], axis=1)
    return plain_dot(left_side, jnp.concatenate([high, low, high], axis=0), None)


def only(cond, always):
    if always:
        return lambda fn: fn()
    return pl.when(cond)


def fused_kernel(
    n,
    depth,
    pieces,
    root,
    panel_shift,
    trail_shift,
    panel,
    trail,
    upper_ref,
    inv_ref,
    cross_ref,
    q_ref,
    reg,
    high_ref,
    low_ref,
    full,
    ring_p,
    moved_p,
    moved_t,
    near_all,
    near_part,
    near_land,
    near_sum,
    far_part,
    far_land,
    far_sum,
    cross_part,
    cross_land,
    aug,
    pair,
    p1_send,
    p1_recv,
    p2_send,
    p2_recv,
    t1_send,
    t1_recv,
    t2_send,
    t2_recv,
    z_send,
    z_recv,
    g_send,
    g_recv,
    c_send,
    c_recv,
    f_send,
    f_recv,
    local_sem,
    *rings,
):
    me = lax.axis_index("rows")
    z = lax.axis_index("cols")
    ctp, blocks = panel.shape[0], panel.shape[1]
    ctt = trail.shape[0]
    total = n * blocks
    tp = ring_p.shape[0]
    tt = len(rings)
    op, ot = ctp // tp, ctt // tt
    rows_t = ot * SUB
    sr = cross_land.shape[2]
    oc = rows_t // sr
    size = inv_ref.shape[0]
    lead_z = max(depth // 2 - 1, 0)
    leads = z == lead_z
    tile = pair.shape[0]
    tiles = size // tile
    edge = size - tile
    near_count = edge // (ctp * SUB)
    mine = pl.ds(pl.multiple_of(me * blocks, blocks), blocks)

    def each_peer(fn):
        def body(d, carry):
            fn(d, lax.rem(me + d, n), lax.rem(me - d + n, n))
            return carry

        lax.fori_loop(1, n, body, 0)

    def linked(other):
        near = (z - other == 1) | (other - z == 1)
        return near | (z != other) & (leads | (other == lead_z))

    barrier = pltpu.get_barrier_semaphore()
    for d in range(1, n):
        pl.semaphore_signal(
            barrier, inc=1, device_id={"rows": lax.rem(me + d, n)}, device_id_type=MESH
        )
    greeted = n - 1
    for other in range(depth):

        @pl.when(linked(other))
        def _():
            pl.semaphore_signal(barrier, inc=1, device_id={"cols": other}, device_id_type=MESH)

        greeted = greeted + jnp.where(linked(other), 1, 0)
    pl.semaphore_wait(barrier, greeted)

    def row_copy(src, dst, send, recv, to):
        return pltpu.make_async_remote_copy(
            src_ref=src,
            dst_ref=dst,
            send_sem=send,
            recv_sem=recv,
            device_id={"rows": to},
            device_id_type=MESH,
        )

    def p1(d, to):
        return row_copy(
            panel.at[pl.ds(to * tp, tp)],
            ring_p.at[:, mine],
            p1_send.at[0],
            p1_recv.at[0],
            to,
        )

    def p2(d, to):
        return row_copy(
            moved_p.at[to],
            full.at[z, pl.ds(me * tp, tp)],
            p2_send.at[0],
            p2_recv.at[0],
            to,
        )

    def t1(t, d, to):
        return row_copy(
            trail.at[to * tt + t],
            rings[t].at[mine],
            t1_send.at[t],
            t1_recv.at[t],
            to,
        )

    def t2(t, half, d, to):
        cut = pl.ds(0, blocks) if half is None else pl.ds(half * (blocks // 2), blocks // 2)
        return row_copy(
            moved_t.at[t, to, cut],
            reg.at[me, t, cut],
            t2_send.at[t + (1 if half == 1 else 0)],
            t2_recv.at[t + (1 if half == 1 else 0)],
            to,
        )

    own_p = pltpu.make_async_copy(
        panel.at[pl.ds(me * tp, tp)], ring_p.at[:, mine], local_sem.at[0]
    )

    def own_t(t):
        return pltpu.make_async_copy(
            trail.at[me * tt + t], rings[t].at[mine], local_sem.at[1 + t]
        )

    def started(copies, active, count, first=1, stride=1, pick=None):
        def go(k, carry):
            d = first + stride * k
            to = lax.rem(me + d, n)
            wanted = active(to) if pick is None else active(to) & pick(d)

            @only(wanted, count == n and pick is None)
            def _():
                copies(d, to).start()

            return carry

        lax.fori_loop(0, -(-(n - first) // stride), go, 0)

    def whole(region, send, recv):
        return row_copy(region, region, send, recv, lax.rem(me + 1, n))

    def counted(active, count, per_copy, done):
        if count == n:
            done(per_copy(n - 1))
        else:

            @pl.when(active(me))
            def _():
                done(per_copy(count - 1))

            @pl.when(jnp.logical_not(active(me)))
            def _():
                done(per_copy(count))

    def once(active, count, per_copy, done):
        @only(active(me), count == n)
        def _():
            done(per_copy(n - 1))

    def take(copy):
        copy.wait_recv()

    def clear(copy):
        copy.wait_send()

    def has_p(j):
        return j < op

    def has_t(j):
        return j < ot

    sub = lax.broadcasted_iota(jnp.int32, (1, SUB, BW), 1)
    step = min(16, blocks)

    def compose(ring, shifts, to, put):
        starts = [lax.rem(to * blocks - s + total, total) for s in shifts]
        for h in range(0, blocks, step):
            block = ring[pl.ds(starts[0] + h, step)]
            for c in range(1, SUB):
                block = jnp.where(sub == c, ring[pl.ds(starts[c] + h, step)], block)
            put(h, block)

    def wrap(ring):
        ring[pl.ds(total, blocks)] = ring[pl.ds(0, blocks)]

    def line(side, d, q):
        step_z = 1 if side == 0 else -1
        origin = z - step_z * (d - 1)
        rows = pl.ds(q * (ctp // pieces), ctp // pieces)
        return pltpu.make_async_remote_copy(
            src_ref=full.at[origin, rows],
            dst_ref=full.at[origin, rows],
            send_sem=z_send.at[side, d - 1, q],
            recv_sem=z_recv.at[side, d - 1, q],
            device_id={"cols": z + step_z},
            device_id_type=MESH,
        )

    def sends(side, d):
        if side == 0:
            return (z + 1 < depth) & (z - (d - 1) >= 0)
        return (z >= 1) & (z + (d - 1) < depth)

    def receives(side, d):
        return z - d >= 0 if side == 0 else z + d < depth

    def arrived(side, d, q):
        step_z = 1 if side == 0 else -1
        origin = z - step_z * d
        rows = pl.ds(q * (ctp // pieces), ctp // pieces)
        return pltpu.make_async_remote_copy(
            src_ref=full.at[origin, rows],
            dst_ref=full.at[origin, rows],
            send_sem=z_send.at[side, d - 1, q],
            recv_sem=z_recv.at[side, d - 1, q],
            device_id={"cols": z - step_z},
            device_id_type=MESH,
        )

    def forward(d, some=None):
        for q in range(pieces) if some is None else some:
            for side in (0, 1):

                @pl.when(receives(side, d))
                def _():
                    arrived(side, d, q).wait_recv()

                if d + 1 < depth:

                    @pl.when(sends(side, d + 1))
                    def _():
                        line(side, d + 1, q).start()

    def start_t1(t, halves=(0, 1)):
        if 0 in halves:

            @only(has_t(me), ot == n)
            def _():
                own_t(t).start()

        if len(halves) == 2:
            started(functools.partial(t1, t), has_t, ot)
        else:
            started(functools.partial(t1, t), has_t, ot, 2 - halves[0], 2)

    def turn_t(t):
        @only(has_t(me), ot == n)
        def _():
            own_t(t).wait()

        once(has_t, ot, lambda k: whole(rings[t].at[pl.ds(0, k * blocks)], t1_send.at[t], t1_recv.at[t]), take)

        @only(has_t(me), ot == n)
        def _():
            wrap(rings[t])
            shifts = [trail_shift[(me * tt + t) * SUB + c] for c in range(SUB)]

            def turn(d, to, origin):
                def put(h, block):
                    moved_t[t, to, pl.ds(h, step)] = block

                compose(rings[t], shifts, to, put)

            each_peer(turn)

            def keep(h, block):
                reg[me, t, pl.ds(h, step)] = block

            compose(rings[t], shifts, me, keep)

    def start_t2(t):
        @only(has_t(me), ot == n)
        def _():
            for half in (0, 1) if t == tt - 1 else (None,):
                started(functools.partial(t2, t, half), has_t, n)

    def wait_t2(t, half=None):
        cut = pl.ds(0, blocks if half is None else blocks // 2)
        sem = t + (1 if half == 1 else 0)
        counted(has_t, ot, lambda k: whole(reg.at[pl.ds(0, k), t, cut], t2_send.at[sem], t2_recv.at[sem]), take)

    def panel_block(b, count, lo=0, hi=depth):
        rows = (hi - lo) * ctp * SUB
        cut = [full[lo:hi, :, count * b + k].reshape(rows, BW) for k in range(count)]
        return jnp.concatenate(cut, axis=1)

    narrow = min(4, blocks)
    wide = min(8, blocks // 2)

    def gram_near():
        near_all[...] = jnp.zeros_like(near_all)

        def body(b, carry):
            block = panel_block(b, narrow, 0, near_count)
            near_all[...] += rows_dot(block, block, HIGHEST)
            return carry

        lax.fori_loop(0, blocks // narrow, body, 0)
        packed = [near_all[lo : lo + tile, lo:edge] for lo in range(0, edge, tile)]
        near_part[...] = jnp.concatenate(packed, axis=1).reshape(near_part.shape)

    def unpack_near():
        packed = near_sum[...].reshape(tile, near_sum.shape[2])
        first = 0
        for lo in range(0, edge, tile):
            aug[lo : lo + tile, lo:edge] = packed[:, first : first + edge - lo]
            first += edge - lo

    def gram_far():
        far_part[...] = jnp.zeros_like(far_part)

        def body(b, carry):
            block = panel_block(b, narrow, near_count, depth)
            both = rows_dot(block, panel_block(b, narrow), HIGHEST)
            far_part[...] += both.reshape(far_part.shape)
            return carry

        lax.fori_loop(0, blocks // narrow, body, 0)

    grams = ((near_part, near_land, near_sum), (far_part, far_land, far_sum))

    def g_one(k, d, to):
        part, land, _ = grams[k]
        return row_copy(part.at[to], land.at[d - 1], g_send.at[k, 0], g_recv.at[k, 0], to)

    def g_two(k, d, to):
        ref = grams[k][2]
        return row_copy(ref.at[me], ref.at[me], g_send.at[k, 1], g_recv.at[k, 1], to)

    def g_count(k):
        return grams[k][0].shape[0]

    def has_g(k):
        return lambda j: j < g_count(k)

    def gram_scatter(k):
        started(functools.partial(g_one, k), has_g(k), g_count(k))

    def gram_spread(k):
        part, land, total_ref = grams[k]

        @only(me < g_count(k), g_count(k) == n)
        def _():
            take(whole(land, g_send.at[k, 0], g_recv.at[k, 0]))
            total_g = part[me]
            for d in range(1, n):
                total_g = total_g + land[d - 1]
            total_ref[me] = total_g

            def go(d, to, origin):
                g_two(k, d, to).start()

            each_peer(go)

    def gram_done(k):
        ref = grams[k][2]
        counted(has_g(k), g_count(k), lambda m: whole(ref.at[pl.ds(0, m)], g_send.at[k, 1], g_recv.at[k, 1]), take)

    def has_c(j):
        return j < oc

    def make_cross(t, lo=0, hi=blocks):
        if lo == 0:
            cross_part[t] = jnp.zeros_like(cross_part[t])

        def body(b, carry):
            cut = [reg[:, t, wide * b + k].reshape(rows_t, BW) for k in range(wide)]
            block = jnp.concatenate(cut, axis=1)
            both = rows_dot(block, panel_block(b, wide), HIGH)
            cross_part[t] += both.reshape(oc, sr, size)
            return carry

        lax.fori_loop(lo // wide, hi // wide, body, 0)

    def c_one(t, d, to):
        return row_copy(
            cross_part.at[t, to],
            cross_land.at[t, d - 1],
            c_send.at[0, t],
            c_recv.at[0, t],
            to,
        )

    def c_two(t, d, to):
        return row_copy(
            cross_ref.at[t, me],
            cross_ref.at[t, me],
            c_send.at[1, t],
            c_recv.at[1, t],
            to,
        )

    def cross_scatter(t):
        started(functools.partial(c_one, t), has_c, oc)

    def cross_spread(t):
        @only(has_c(me), oc == n)
        def _():
            take(whole(cross_land.at[t], c_send.at[0, t], c_recv.at[0, t]))
            total_c = cross_part[t, me]
            for d in range(1, n):
                total_c = total_c + cross_land[t, d - 1]
            cross_ref[t, me] = total_c

            def go(d, to, origin):
                c_two(t, d, to).start()

            each_peer(go)

    def cross_done(t):
        counted(has_c, oc, lambda k: whole(cross_ref.at[t, pl.ds(0, k)], c_send.at[1, t], c_recv.at[1, t]), take)

    def factor_copy(i, k, slot, to):
        ref = inv_ref if k == 0 else upper_ref
        rows = pl.ds(i * tile, tile)
        return pltpu.make_async_remote_copy(
            src_ref=ref.at[rows],
            dst_ref=ref.at[rows],
            send_sem=f_send.at[slot, k],
            recv_sem=f_recv.at[k],
            device_id={"cols": to},
            device_id_type=MESH,
        )

    def factor_whole(k, slot=0):
        ref = inv_ref if k == 0 else upper_ref
        return pltpu.make_async_remote_copy(
            src_ref=ref,
            dst_ref=ref,
            send_sem=f_send.at[slot, k],
            recv_sem=f_recv.at[k],
            device_id={"cols": lax.rem(z + 1, depth)},
            device_id_type=MESH,
        )

    def send_factor(i, k, act):
        for other in range(depth):
            if other != lead_z:
                act(factor_copy(i, k, other, other))

    def factor_tile(i):
        lo = i * tile
        hi = lo + tile
        row = lax.broadcasted_iota(jnp.int32, (tile, 2 * tile), 0)
        col = lax.broadcasted_iota(jnp.int32, (tile, 2 * tile), 1)
        pair[...] = jnp.where(col == row + tile, 1.0, 0.0)
        pair[:, 0:tile] = aug[lo:hi, lo:hi]
        w = pair[...]
        pivots = jnp.zeros((tile, 1), F32)
        for j in range(tile):
            base = j // 8 * 8
            live = w[base:, :]
            lead = w[j : j + 1, :]
            pivot = lead[:, j : j + 1]
            pivots = jnp.where(row[:, 0:1] == j, pivot, pivots)
            if j + 1 == tile:
                break
            mult = jnp.where(row[base:, 0:1] > j, live[:, j : j + 1], 0.0)
            live = live - mult * (lead / pivot)
            w = live if base == 0 else jnp.concatenate([w[:base], live], axis=0)
        pair[...] = w * (1.0 / jnp.sqrt(pivots))
        inverse = pair[:, tile : 2 * tile]
        lead_rows = plain_dot(inverse, aug[lo:hi, :], HIGHEST)
        grow = lax.broadcasted_iota(jnp.int32, (tile, size), 0) + lo
        gcol = lax.broadcasted_iota(jnp.int32, (tile, size), 1)
        upper = jnp.where(gcol >= grow, lead_rows[:, 0:size], 0.0)
        upper_ref[lo:hi, :] = upper * (1.0 / root)
        inv_ref[lo:hi, :] = lead_rows[:, size : 2 * size]
        if hi < edge:
            aug[...] = aug[...] - lax.dot_general(
                upper,
                lead_rows,
                (((0,), (0,)), ((), ())),
                precision=HIGHEST,
                preferred_element_type=F32,
            )

    def make_basis():
        factor = inv_ref[...]
        own = pl.ds(pl.multiple_of(z * (ctp * SUB), ctp * SUB), ctp * SUB)

        def body(b, carry):
            both = plain_dot(factor, panel_block(b, narrow), HIGH)
            mine_only = plain_dot(inv_ref[own, :] * root, panel_block(b, narrow), HIGH)
            for k in range(narrow):
                lanes = slice(k * BW, (k + 1) * BW)
                place = narrow * b + k
                part = both[:, lanes]
                upper_half = part.astype(jnp.bfloat16)
                high_ref[place] = upper_half
                low_ref[place] = (part - upper_half.astype(F32)).astype(jnp.bfloat16)
                q_ref[:, place] = mine_only[:, lanes].reshape(ctp, SUB, BW)
            return carry

        lax.fori_loop(0, blocks // narrow, body, 0)

    def emit(chunks):
        for t in chunks:
            cross_done(t)
        rows = [cross_ref[t].reshape(rows_t, size) for t in chunks]
        left_side = three_part(rows_dot(joined(rows), inv_ref[...], HIGHEST))

        def body(b, carry):
            both = removed(left_side, high_ref, low_ref, wide * b, wide)
            for k in range(wide):
                lanes = slice(k * BW, (k + 1) * BW)
                place = wide * b + k
                for i, t in enumerate(chunks):
                    part = both[i * rows_t : (i + 1) * rows_t, lanes]
                    reg[:, t, place] = reg[:, t, place] - part.reshape(ot, SUB, BW)
            return carry

        lax.fori_loop(0, blocks // wide, body, 0)

    def start_copy(copy):
        copy.start()

    @only(has_p(me), op == n)
    def _():
        own_p.start()

    started(p1, has_p, op)

    def ahead(d):
        return (d == 2) | (d == 4)

    @only(has_t(me), ot == n)
    def _():
        own_t(0).start()

    started(functools.partial(t1, 0), has_t, ot, pick=ahead)

    @only(has_p(me), op == n)
    def _():
        own_p.wait()

    once(has_p, op, lambda k: whole(ring_p.at[:, pl.ds(0, k * blocks)], p1_send.at[0], p1_recv.at[0]), take)

    @only(has_p(me), op == n)
    def _():
        for t in range(tp):
            wrap(ring_p.at[t])
        shifts = [
            [panel_shift[(me * tp + t) * SUB + c] for c in range(SUB)] for t in range(tp)
        ]

        def turn(d, to, origin):
            for t in range(tp):

                def put(h, block, t=t):
                    moved_p[to, t, pl.ds(h, step)] = block

                compose(ring_p.at[t], shifts[t], to, put)

        each_peer(turn)

        def go(d, to, origin):
            p2(d, to).start()

        each_peer(go)
        for t in range(tp):

            def keep(h, block, t=t):
                full[z, me * tp + t, pl.ds(h, step)] = block

            compose(ring_p.at[t], shifts[t], me, keep)

    last = tt - 1
    started(functools.partial(t1, 0), has_t, ot, pick=lambda d: jnp.logical_not(ahead(d)))
    if tt > 1:
        start_t1(1)
    counted(has_p, op, lambda k: whole(full.at[z, pl.ds(0, k * tp)], p2_send.at[0], p2_recv.at[0]), take)
    for q in range(pieces):
        for side in (0, 1):

            @pl.when(sends(side, 1))
            def _():
                line(side, 1, q).start()

    middle = max(depth // 2, 1)
    turn_t(0)
    if last > 0:
        start_t2(0)
    follows = jnp.logical_not(leads)

    @pl.when(follows)
    def _():
        for t in range(2, last):
            start_t1(t)

    for d in range(1, middle):
        forward(d)

    def rest_t1():
        if last > 1:
            start_t1(last)

    def rest_t2():
        for t in range(2, last):
            start_t2(t)

    def finish_turns():
        if last > 0:
            turn_t(last)
        start_t2(last)

    def cross_chunk(t):
        if t == last:
            wait_t2(t, 0)
            make_cross(t, 0, blocks // 2)
            wait_t2(t, 1)
            make_cross(t, blocks // 2, blocks)
        else:
            wait_t2(t)
            make_cross(t)
        cross_scatter(t)

    early = min(2, last)

    def border():
        far = far_sum[...].reshape(tile, size)
        corner = rows_dot(inv_ref[0:edge, 0:edge], far[:, 0:edge], HIGHEST)
        upper_ref[0:edge, edge:size] = corner * (1.0 / root)

        def turned(right):
            return lax.dot_general(
                corner,
                right,
                (((0,), (0,)), ((), ())),
                precision=HIGHEST,
                preferred_element_type=F32,
            )

        aug[edge:size, edge:size] = far[:, edge:size] - turned(corner)
        aug[edge:size, size : 2 * size] = aug[edge:size, size : 2 * size] - turned(inv_ref[0:edge, :])

    @pl.when(leads)
    def _():
        gram_near()
        gram_scatter(0)
        if last > 2:
            start_t1(2, (0,))
        if last > 1:
            turn_t(1)
        aug_row = lax.broadcasted_iota(jnp.int32, (size, 2 * size), 0)
        aug_col = lax.broadcasted_iota(jnp.int32, (size, 2 * size), 1)
        aug[...] = jnp.where(aug_col == aug_row + size, 1.0, 0.0)
        gram_spread(0)
        for t in range(2, last):
            start_t1(t, (1,) if t == 2 else (0, 1))
        if last > 1:
            start_t2(1)
        forward(middle, range(pieces // 2))
        gram_done(0)
        forward(middle, range(pieces // 2, pieces - 1))
        unpack_near()
        for i in range(tiles - 1):
            factor_tile(i)
            send_factor(i, 0, start_copy)
            if i == 0:
                forward(middle, range(pieces - 1, pieces))
                gram_far()
                gram_scatter(1)
                if last > 1:
                    start_t1(last, (0,))
                for t in range(2, last):
                    turn_t(t)
            if i == min(1, tiles - 2):
                gram_spread(1)
                if last > 1:
                    start_t1(last, (1,))
                rest_t2()
        gram_done(1)
        border()
        factor_tile(tiles - 1)
        send_factor(tiles - 1, 0, start_copy)
        for i in range(tiles):
            send_factor(i, 1, start_copy)
        finish_turns()
        for t in range(early):
            cross_chunk(t)
        for k in (0, 1):
            part, land, _ = grams[k]
            row = lambda m: pl.ds(0, m)
            counted(has_g(k), g_count(k), lambda m: whole(land.at[row(m)], g_send.at[k, 0], g_recv.at[k, 0]), clear)
            once(has_g(k), g_count(k), lambda m: whole(land.at[row(m)], g_send.at[k, 1], g_recv.at[k, 1]), clear)

    @pl.when(follows)
    def _():
        for t in range(1, last):
            turn_t(t)
            if t == 1:
                start_t2(t)
                for d in range(middle, middle + 1):
                    forward(d)
        if last < 2:
            for d in range(middle, middle + 1):
                forward(d)
        rest_t1()
        rest_t2()
        finish_turns()
        for d in range(middle + 1, depth):
            forward(d)
        for t in range(early):
            cross_chunk(t)
        factor_whole(0).wait_recv()

    make_basis()
    for t in range(early, last):
        cross_chunk(t)
    cross_chunk(last)
    for t in range(last):
        cross_spread(t)
    cross_spread(last)
    if last > 0:
        emit(list(range(last)))
    cross_done(last)

    @pl.when(follows)
    def _():
        factor_whole(1).wait_recv()

    @pl.when(leads)
    def _():
        for other in range(depth):
            if other != lead_z:
                for k in (0, 1):
                    factor_whole(k, other).wait_send()

    counted(has_p, op, lambda k: whole(ring_p.at[:, pl.ds(0, k * blocks)], p1_send.at[0], p1_recv.at[0]), clear)
    once(has_p, op, lambda k: whole(ring_p.at[:, pl.ds(0, k * blocks)], p2_send.at[0], p2_recv.at[0]), clear)
    for t in range(tt):
        ring = rings[t]
        counted(has_t, ot, lambda k: whole(ring.at[pl.ds(0, k * blocks)], t1_send.at[t], t1_recv.at[t]), clear)
        for sem in (t, t + 1) if t == tt - 1 else (t,):
            bulk = blocks // 2 if t == tt - 1 else blocks
            once(has_t, ot, lambda k: whole(ring.at[pl.ds(0, k * bulk)], t2_send.at[sem], t2_recv.at[sem]), clear)
        land = cross_land.at[t]
        counted(has_c, oc, lambda k: whole(land.at[pl.ds(0, k)], c_send.at[0, t], c_recv.at[0, t]), clear)
        once(has_c, oc, lambda k: whole(land.at[pl.ds(0, k)], c_send.at[1, t], c_recv.at[1, t]), clear)
    for d in range(1, depth):
        for q in range(pieces):
            for side in (0, 1):

                @pl.when(sends(side, d))
                def _():
                    line(side, d, q).wait_send()


def fused(panel, trail, panel_shift, trail_shift, n, depth, root):
    ctp, blocks = panel.shape[0], panel.shape[1]
    ctt = trail.shape[0]
    tp = -(-ctp // n)
    tt = -(-ctt // n)
    op, ot = ctp // tp, ctt // tt
    size = depth * ctp * SUB
    rows_t = ot * SUB
    sr = max(SUB, rows_t // n)
    oc = rows_t // sr
    tile = 64
    tiles = size // tile
    edge = size - tile
    packed = tile * (tiles * (tiles - 1) // 2)
    far_rows = -(-tile // (n * SUB)) * SUB
    pieces = 4 if ctp % 4 == 0 else 1
    total = n * blocks
    smem = pl.BlockSpec(memory_space=pltpu.SMEM)
    vmem = pl.BlockSpec(memory_space=pltpu.VMEM)
    hbm = pl.BlockSpec(memory_space=pl.ANY)
    dma = pltpu.SemaphoreType.DMA
    peers = max(n - 1, 1)
    lines = max(depth - 1, 1)
    return pl.pallas_call(
        functools.partial(fused_kernel, n, depth, pieces, root),
        out_shape=(
            pltpu.VMEM((size, size), F32),
            pltpu.VMEM((size, size), F32),
            pltpu.VMEM((tt, oc, sr, size), F32),
            pltpu.VMEM(panel.shape, F32),
            pltpu.VMEM((ot, tt) + trail.shape[1:], F32),
            pltpu.VMEM((blocks, size, BW), jnp.bfloat16),
            pltpu.VMEM((blocks, size, BW), jnp.bfloat16),
        ),
        in_specs=[smem, smem, hbm, hbm],
        out_specs=(vmem,) * 7,
        scratch_shapes=[
            pltpu.VMEM((depth,) + panel.shape, F32),
            pltpu.VMEM((tp, total + blocks, SUB, BW), F32),
            pltpu.VMEM((n, tp, blocks, SUB, BW), F32),
            pltpu.VMEM((tt, n, blocks, SUB, BW), F32),
            pltpu.VMEM((edge, edge), F32),
            pltpu.VMEM((tile // far_rows, far_rows, packed), F32),
            pltpu.VMEM((peers, far_rows, packed), F32),
            pltpu.VMEM((tile // far_rows, far_rows, packed), F32),
            pltpu.VMEM((tile // far_rows, far_rows, size), F32),
            pltpu.VMEM((peers, far_rows, size), F32),
            pltpu.VMEM((tile // far_rows, far_rows, size), F32),
            pltpu.VMEM((tt, oc, sr, size), F32),
            pltpu.VMEM((tt, peers, sr, size), F32),
            pltpu.VMEM((size, 2 * size), F32),
            pltpu.VMEM((tile, 2 * tile), F32),
            dma((1,)),
            dma((1,)),
            dma((1,)),
            dma((1,)),
            dma((tt,)),
            dma((tt,)),
            dma((tt + 1,)),
            dma((tt + 1,)),
            dma((2, lines, pieces)),
            dma((2, lines, pieces)),
            dma((2, 2)),
            dma((2, 2)),
            dma((2, tt)),
            dma((2, tt)),
            dma((depth, 2)),
            dma((2,)),
            dma((1 + tt,)),
        ]
        + [pltpu.VMEM((total + blocks, SUB, BW), F32)] * tt,
        compiler_params=pltpu.CompilerParams(
            collective_id=3, has_side_effects=True, vmem_limit_bytes=40 << 20
        ),
        cost_estimate=pl.CostEstimate(
            flops=0, bytes_accessed=40 * trail.size * 4, transcendentals=0
        ),
    )(panel_shift, trail_shift, panel, trail)


def final_kernel(
    root,
    early,
    upper,
    inv,
    cross,
    q,
    reg,
    high_ref,
    low_ref,
    r_ref,
    coupling_ref,
    q_ref,
    out_ref,
    late,
    coupling,
    sems,
):
    size = inv.shape[0]
    ot, tt, blocks = reg.shape[:3]
    rows_t = ot * SUB
    chunks = list(range(early, tt))
    steps = 2 if blocks % 2 == 0 else 1
    span = blocks // steps
    copies = [pltpu.make_async_copy(q, q_ref, sems.at[0])]
    copies.append(pltpu.make_async_copy(upper, r_ref, sems.at[1]))
    for t in range(early):
        copies.append(pltpu.make_async_copy(reg.at[:, t], out_ref.at[:, t], sems.at[2 + t]))
    for copy in copies:
        copy.start()
    rows = joined([cross[t].reshape(rows_t, size) for t in chunks])
    left_side = three_part(rows_dot(rows, inv[...], HIGHEST))
    narrow = min(8, span)
    for h in range(steps):

        def body(b, carry, h=h):
            first = h * span + narrow * b
            both = removed(left_side, high_ref, low_ref, first, narrow)
            for k in range(narrow):
                lanes = slice(k * BW, (k + 1) * BW)
                for i, t in enumerate(chunks):
                    part = both[i * rows_t : (i + 1) * rows_t, lanes]
                    late[:, i, first + k] = reg[:, t, first + k] - part.reshape(ot, SUB, BW)
            return carry

        lax.fori_loop(0, span // narrow, body, 0)
        for i, t in enumerate(chunks):
            place = pl.ds(h * span, span)
            copy = pltpu.make_async_copy(
                late.at[:, i, place], out_ref.at[:, t, place], sems.at[2 + early + h * len(chunks) + i]
            )
            copy.start()
            copies.append(copy)
    every = jnp.stack([cross[t].reshape(ot, SUB, size) for t in range(tt)], axis=1)
    coupling[...] = rows_dot(
        inv[...] * (1.0 / root), every.reshape(ot * tt * SUB, size), HIGHEST
    )
    last = pltpu.make_async_copy(coupling, coupling_ref, sems.at[2 + early + steps * len(chunks)])
    last.start()
    copies.append(last)
    for copy in copies:
        copy.wait()


def final(upper, inv, cross, q, reg, high, low, root):
    size = inv.shape[0]
    ot, tt = reg.shape[:2]
    early = tt - 1
    vmem = pl.BlockSpec(memory_space=pltpu.VMEM)
    hbm = pl.BlockSpec(memory_space=pl.ANY)
    near = [pltpu.with_memory_space_constraint(x, pltpu.VMEM) for x in (upper, inv, cross, q, reg, high, low)]
    return pl.pallas_call(
        functools.partial(final_kernel, root, early),
        out_shape=(
            jax.ShapeDtypeStruct((size, size), F32),
            jax.ShapeDtypeStruct((size, ot * tt * SUB), F32),
            jax.ShapeDtypeStruct(q.shape, F32),
            jax.ShapeDtypeStruct(reg.shape, F32),
        ),
        in_specs=[vmem] * 7,
        out_specs=(hbm,) * 4,
        scratch_shapes=[
            pltpu.VMEM((ot, tt - early) + reg.shape[2:], F32),
            pltpu.VMEM((size, ot * tt * SUB), F32),
            pltpu.SemaphoreType.DMA((3 + early + 2 * (tt - early),)),
        ],
        compiler_params=pltpu.CompilerParams(vmem_limit_bytes=24 << 20),
        cost_estimate=pl.CostEstimate(
            flops=2 * size * reg.size, bytes_accessed=8 * reg.size, transcendentals=0
        ),
    )(*near)


def tiled(raw):
    rows, pixels = raw.shape
    return raw.reshape(rows // SUB, SUB, pixels // BW, BW).transpose(0, 2, 1, 3)


def flat(blocked):
    cut, blocks = blocked.shape[0], blocked.shape[1]
    return blocked.transpose(0, 2, 1, 3).reshape(cut * SUB, blocks * BW)


def on_device(raw_panel, raw_trail, panel_shift, trail_shift):
    n = lax.axis_size("rows")
    depth = lax.axis_size("cols")
    pixels = raw_panel.shape[1]
    root = math.sqrt(pixels * n)
    raw = [
        pltpu.with_memory_space_constraint(tiled(x), pltpu.HBM) for x in (raw_panel, raw_trail)
    ]
    shifts = [
        pltpu.with_memory_space_constraint(x, pltpu.HBM) for x in (panel_shift, trail_shift)
    ]
    held = fused(
        *raw, *shifts, n, depth, root
    )
    r_factor, coupling, q_panel, out = final(*held, root)
    return (r_factor, coupling, flat(q_panel), flat(out.reshape((-1,) + out.shape[2:])))


def solution(mesh):
    placed = (P("cols", "rows"), P("cols", "rows"), P("cols"), P("cols"))
    return jax.shard_map(
        on_device,
        mesh=mesh,
        in_specs=placed,
        out_specs=(P(), P(None, "cols"), P("cols", "rows"), P("cols", "rows")),
        check_vma=False,
    )
```

```python
import functools
import math

import jax
import jax.numpy as jnp
from jax import lax
from jax.experimental import pallas as pl
from jax.experimental.pallas import tpu as pltpu
from jax.sharding import PartitionSpec as P

BW = 128
SUB = 8
MESH = pl.DeviceIdType.MESH
F32 = jnp.float32
HIGHEST = lax.Precision.HIGHEST
HIGH = lax.Precision.HIGH


def rows_dot(left, right, precision):
    return lax.dot_general(
        left,
        right,
        (((1,), (1,)), ((), ())),
        precision=precision,
        preferred_element_type=F32,
    )


def plain_dot(left, right, precision):
    return lax.dot_general(
        left,
        right,
        (((1,), (0,)), ((), ())),
        precision=precision,
        preferred_element_type=F32,
    )


def joined(parts):
    return jnp.concatenate(parts, axis=0) if len(parts) > 1 else parts[0]


def three_part(value):
    high = value.astype(jnp.bfloat16)
    low = (value - high.astype(F32)).astype(jnp.bfloat16)
    return jnp.concatenate([high, high, low], axis=1)


def removed(left_side, high_ref, low_ref, first, count):
    high = jnp.concatenate([high_ref[first + k] for k in range(count)], axis=1)
    low = jnp.concatenate([low_ref[first + k] for k in range(count)], axis=1)
    return plain_dot(left_side, jnp.concatenate([high, low, high], axis=0), None)


def only(cond, always):
    if always:
        return lambda fn: fn()
    return pl.when(cond)


def fused_kernel(
    n,
    depth,
    pieces,
    root,
    panel_shift,
    trail_shift,
    panel,
    trail,
    upper_ref,
    inv_ref,
    cross_ref,
    q_ref,
    reg,
    high_ref,
    low_ref,
    full,
    ring_p,
    moved_p,
    moved_t,
    near_all,
    near_part,
    near_land,
    near_sum,
    far_part,
    far_land,
    far_sum,
    cross_part,
    cross_land,
    aug,
    pair,
    p1_send,
    p1_recv,
    p2_send,
    p2_recv,
    t1_send,
    t1_recv,
    t2_send,
    t2_recv,
    z_send,
    z_recv,
    g_send,
    g_recv,
    c_send,
    c_recv,
    f_send,
    f_recv,
    h_send,
    h_recv,
    local_sem,
    *rings,
):
    me = lax.axis_index("rows")
    z = lax.axis_index("cols")
    ctp, blocks = panel.shape[0], panel.shape[1]
    ctt = trail.shape[0]
    total = n * blocks
    tp = ring_p.shape[0]
    tt = len(rings)
    op, ot = ctp // tp, ctt // tt
    rows_t = ot * SUB
    sr = cross_land.shape[2]
    oc = rows_t // sr
    size = inv_ref.shape[0]
    lead_z = max(depth // 2 - 1, 0)
    leads = z == lead_z
    helper_z = min(lead_z + 1, depth - 1)
    helps = z == helper_z
    tile = pair.shape[0]
    tiles = size // tile
    edge = size - tile
    near_count = edge // (ctp * SUB)
    mine = pl.ds(pl.multiple_of(me * blocks, blocks), blocks)

    def each_peer(fn):
        def body(d, carry):
            fn(d, lax.rem(me + d, n), lax.rem(me - d + n, n))
            return carry

        lax.fori_loop(1, n, body, 0)

    def linked(other):
        near = (z - other == 1) | (other - z == 1)
        return near | (z != other) & (leads | (other == lead_z))

    barrier = pltpu.get_barrier_semaphore()
    for d in range(1, n):
        pl.semaphore_signal(
            barrier, inc=1, device_id={"rows": lax.rem(me + d, n)}, device_id_type=MESH
        )
    greeted = n - 1
    for other in range(depth):

        @pl.when(linked(other))
        def _():
            pl.semaphore_signal(barrier, inc=1, device_id={"cols": other}, device_id_type=MESH)

        greeted = greeted + jnp.where(linked(other), 1, 0)
    pl.semaphore_wait(barrier, greeted)

    def row_copy(src, dst, send, recv, to):
        return pltpu.make_async_remote_copy(
            src_ref=src,
            dst_ref=dst,
            send_sem=send,
            recv_sem=recv,
            device_id={"rows": to},
            device_id_type=MESH,
        )

    def p1(d, to):
        return row_copy(
            panel.at[pl.ds(to * tp, tp)],
            ring_p.at[:, mine],
            p1_send.at[0],
            p1_recv.at[0],
            to,
        )

    def p2(d, to):
        return row_copy(
            moved_p.at[to],
            full.at[z, pl.ds(me * tp, tp)],
            p2_send.at[0],
            p2_recv.at[0],
            to,
        )

    def t1(t, d, to):
        return row_copy(
            trail.at[to * tt + t],
            rings[t].at[mine],
            t1_send.at[t],
            t1_recv.at[t],
            to,
        )

    def t2(t, half, d, to):
        cut = pl.ds(0, blocks) if half is None else pl.ds(half * (blocks // 2), blocks // 2)
        return row_copy(
            moved_t.at[t, to, cut],
            reg.at[me, t, cut],
            t2_send.at[t + (1 if half == 1 else 0)],
            t2_recv.at[t + (1 if half == 1 else 0)],
            to,
        )

    own_p = pltpu.make_async_copy(
        panel.at[pl.ds(me * tp, tp)], ring_p.at[:, mine], local_sem.at[0]
    )

    def own_t(t):
        return pltpu.make_async_copy(
            trail.at[me * tt + t], rings[t].at[mine], local_sem.at[1 + t]
        )

    def started(copies, active, count, first=1, stride=1, pick=None):
        def go(k, carry):
            d = first + stride * k
            to = lax.rem(me + d, n)
            wanted = active(to) if pick is None else active(to) & pick(d)

            @only(wanted, count == n and pick is None)
            def _():
                copies(d, to).start()

            return carry

        lax.fori_loop(0, -(-(n - first) // stride), go, 0)

    def whole(region, send, recv):
        return row_copy(region, region, send, recv, lax.rem(me + 1, n))

    def counted(active, count, per_copy, done):
        if count == n:
            done(per_copy(n - 1))
        else:

            @pl.when(active(me))
            def _():
                done(per_copy(count - 1))

            @pl.when(jnp.logical_not(active(me)))
            def _():
                done(per_copy(count))

    def once(active, count, per_copy, done):
        @only(active(me), count == n)
        def _():
            done(per_copy(n - 1))

    def take(copy):
        copy.wait_recv()

    def clear(copy):
        copy.wait_send()

    def has_p(j):
        return j < op

    def has_t(j):
        return j < ot

    sub = lax.broadcasted_iota(jnp.int32, (1, SUB, BW), 1)
    step = min(16, blocks)

    def compose(ring, shifts, to, put):
        starts = [lax.rem(to * blocks - s + total, total) for s in shifts]
        for h in range(0, blocks, step):
            block = ring[pl.ds(starts[0] + h, step)]
            for c in range(1, SUB):
                block = jnp.where(sub == c, ring[pl.ds(starts[c] + h, step)], block)
            put(h, block)

    def wrap(ring):
        ring[pl.ds(total, blocks)] = ring[pl.ds(0, blocks)]

    def line(side, d, q):
        step_z = 1 if side == 0 else -1
        origin = z - step_z * (d - 1)
        rows = pl.ds(q * (ctp // pieces), ctp // pieces)
        return pltpu.make_async_remote_copy(
            src_ref=full.at[origin, rows],
            dst_ref=full.at[origin, rows],
            send_sem=z_send.at[side, d - 1, q],
            recv_sem=z_recv.at[side, d - 1, q],
            device_id={"cols": z + step_z},
            device_id_type=MESH,
        )

    def sends(side, d):
        if side == 0:
            return (z + 1 < depth) & (z - (d - 1) >= 0)
        return (z >= 1) & (z + (d - 1) < depth)

    def receives(side, d):
        return z - d >= 0 if side == 0 else z + d < depth

    def arrived(side, d, q):
        step_z = 1 if side == 0 else -1
        origin = z - step_z * d
        rows = pl.ds(q * (ctp // pieces), ctp // pieces)
        return pltpu.make_async_remote_copy(
            src_ref=full.at[origin, rows],
            dst_ref=full.at[origin, rows],
            send_sem=z_send.at[side, d - 1, q],
            recv_sem=z_recv.at[side, d - 1, q],
            device_id={"cols": z - step_z},
            device_id_type=MESH,
        )

    def forward(d, some=None):
        for q in range(pieces) if some is None else some:
            for side in (0, 1):

                @pl.when(receives(side, d))
                def _():
                    arrived(side, d, q).wait_recv()

                if d + 1 < depth:

                    @pl.when(sends(side, d + 1))
                    def _():
                        line(side, d + 1, q).start()

    def ahead(d):
        return (d == 2) | (d == 4)

    def behind(d):
        return jnp.logical_not(ahead(d))

    def start_t1(t, halves=(0, 1), picked=None):
        if 0 in halves and picked is not behind:

            @only(has_t(me), ot == n)
            def _():
                own_t(t).start()

        if len(halves) == 2:
            started(functools.partial(t1, t), has_t, ot, pick=picked)
        else:
            started(functools.partial(t1, t), has_t, ot, 2 - halves[0], 2)

    def turn_t(t):
        @only(has_t(me), ot == n)
        def _():
            own_t(t).wait()

        once(has_t, ot, lambda k: whole(rings[t].at[pl.ds(0, k * blocks)], t1_send.at[t], t1_recv.at[t]), take)

        @only(has_t(me), ot == n)
        def _():
            wrap(rings[t])
            shifts = [trail_shift[(me * tt + t) * SUB + c] for c in range(SUB)]

            def turn(d, to, origin):
                def put(h, block):
                    moved_t[t, to, pl.ds(h, step)] = block

                compose(rings[t], shifts, to, put)

            each_peer(turn)

            def keep(h, block):
                reg[me, t, pl.ds(h, step)] = block

            compose(rings[t], shifts, me, keep)

    def start_t2(t):
        @only(has_t(me), ot == n)
        def _():
            for half in (0, 1) if t == tt - 1 else (None,):
                started(functools.partial(t2, t, half), has_t, n)

    def wait_t2(t, half=None):
        cut = pl.ds(0, blocks if half is None else blocks // 2)
        sem = t + (1 if half == 1 else 0)
        counted(has_t, ot, lambda k: whole(reg.at[pl.ds(0, k), t, cut], t2_send.at[sem], t2_recv.at[sem]), take)

    def panel_block(b, count, lo=0, hi=depth):
        rows = (hi - lo) * ctp * SUB
        cut = [full[lo:hi, :, count * b + k].reshape(rows, BW) for k in range(count)]
        return jnp.concatenate(cut, axis=1)

    narrow = min(4, blocks)
    wide = min(8, blocks // 2)

    def gram_near():
        near_all[...] = jnp.zeros_like(near_all)

        def body(b, carry):
            block = panel_block(b, narrow, 0, near_count)
            near_all[...] += rows_dot(block, block, HIGHEST)
            return carry

        lax.fori_loop(0, blocks // narrow, body, 0)
        packed = [near_all[lo : lo + tile, lo:edge] for lo in range(0, edge, tile)]
        near_part[...] = jnp.concatenate(packed, axis=1).reshape(near_part.shape)

    def unpack_near():
        packed = near_sum[...].reshape(tile, near_sum.shape[2])
        first = 0
        for lo in range(0, edge, tile):
            aug[lo : lo + tile, lo:edge] = packed[:, first : first + edge - lo]
            first += edge - lo

    def gram_far():
        far_part[...] = jnp.zeros_like(far_part)

        def body(b, carry):
            block = panel_block(b, narrow, near_count, depth)
            both = rows_dot(block, panel_block(b, narrow), HIGHEST)
            far_part[...] += both.reshape(far_part.shape)
            return carry

        lax.fori_loop(0, blocks // narrow, body, 0)

    grams = ((near_part, near_land, near_sum), (far_part, far_land, far_sum))

    def g_one(k, d, to):
        part, land, _ = grams[k]
        return row_copy(part.at[to], land.at[d - 1], g_send.at[k, 0], g_recv.at[k, 0], to)

    def g_two(k, d, to):
        ref = grams[k][2]
        return row_copy(ref.at[me], ref.at[me], g_send.at[k, 1], g_recv.at[k, 1], to)

    def g_count(k):
        return grams[k][0].shape[0]

    def has_g(k):
        return lambda j: j < g_count(k)

    def gram_scatter(k):
        started(functools.partial(g_one, k), has_g(k), g_count(k))

    def gram_spread(k):
        part, land, total_ref = grams[k]

        @only(me < g_count(k), g_count(k) == n)
        def _():
            take(whole(land, g_send.at[k, 0], g_recv.at[k, 0]))
            total_g = part[me]
            for d in range(1, n):
                total_g = total_g + land[d - 1]
            total_ref[me] = total_g

            def go(d, to, origin):
                g_two(k, d, to).start()

            each_peer(go)

    def gram_done(k):
        ref = grams[k][2]
        counted(has_g(k), g_count(k), lambda m: whole(ref.at[pl.ds(0, m)], g_send.at[k, 1], g_recv.at[k, 1]), take)

    def gram_clear(k):
        land = grams[k][1]
        counted(has_g(k), g_count(k), lambda m: whole(land.at[pl.ds(0, m)], g_send.at[k, 0], g_recv.at[k, 0]), clear)
        once(has_g(k), g_count(k), lambda m: whole(land.at[pl.ds(0, m)], g_send.at[k, 1], g_recv.at[k, 1]), clear)

    def far_copy(to):
        return pltpu.make_async_remote_copy(
            src_ref=far_sum,
            dst_ref=far_sum,
            send_sem=h_send.at[0],
            recv_sem=h_recv.at[0],
            device_id={"cols": to},
            device_id_type=MESH,
        )

    def has_c(j):
        return j < oc

    def make_cross(t, lo=0, hi=blocks):
        if lo == 0:
            cross_part[t] = jnp.zeros_like(cross_part[t])

        def body(b, carry):
            cut = [reg[:, t, wide * b + k].reshape(rows_t, BW) for k in range(wide)]
            block = jnp.concatenate(cut, axis=1)
            both = rows_dot(block, panel_block(b, wide), HIGH)
            cross_part[t] += both.reshape(oc, sr, size)
            return carry

        lax.fori_loop(lo // wide, hi // wide, body, 0)

    def c_one(t, d, to):
        return row_copy(
            cross_part.at[t, to],
            cross_land.at[t, d - 1],
            c_send.at[0, t],
            c_recv.at[0, t],
            to,
        )

    def c_two(t, d, to):
        return row_copy(
            cross_ref.at[t, me],
            cross_ref.at[t, me],
            c_send.at[1, t],
            c_recv.at[1, t],
            to,
        )

    def cross_scatter(t):
        started(functools.partial(c_one, t), has_c, oc)

    def cross_spread(t):
        @only(has_c(me), oc == n)
        def _():
            take(whole(cross_land.at[t], c_send.at[0, t], c_recv.at[0, t]))
            total_c = cross_part[t, me]
            for d in range(1, n):
                total_c = total_c + cross_land[t, d - 1]
            cross_ref[t, me] = total_c

            def go(d, to, origin):
                c_two(t, d, to).start()

            each_peer(go)

    def cross_done(t):
        counted(has_c, oc, lambda k: whole(cross_ref.at[t, pl.ds(0, k)], c_send.at[1, t], c_recv.at[1, t]), take)

    def factor_copy(i, k, slot, to):
        ref = inv_ref if k == 0 else upper_ref
        rows = pl.ds(i * tile, tile)
        return pltpu.make_async_remote_copy(
            src_ref=ref.at[rows],
            dst_ref=ref.at[rows],
            send_sem=f_send.at[slot, k],
            recv_sem=f_recv.at[k],
            device_id={"cols": to},
            device_id_type=MESH,
        )

    def factor_whole(k, slot=0):
        ref = inv_ref if k == 0 else upper_ref
        return pltpu.make_async_remote_copy(
            src_ref=ref,
            dst_ref=ref,
            send_sem=f_send.at[slot, k],
            recv_sem=f_recv.at[k],
            device_id={"cols": lax.rem(z + 1, depth)},
            device_id_type=MESH,
        )

    def send_factor(i, k, act):
        for other in range(depth):
            if other != lead_z:
                act(factor_copy(i, k, other, other))

    def factor_tile(i):
        lo = i * tile
        hi = lo + tile
        row = lax.broadcasted_iota(jnp.int32, (tile, 2 * tile), 0)
        col = lax.broadcasted_iota(jnp.int32, (tile, 2 * tile), 1)
        pair[...] = jnp.where(col == row + tile, 1.0, 0.0)
        pair[:, 0:tile] = aug[lo:hi, lo:hi]
        w = pair[...]
        pivots = jnp.zeros((tile, 1), F32)
        for j in range(tile):
            base = j // 8 * 8
            live = w[base:, :]
            lead = w[j : j + 1, :]
            pivot = lead[:, j : j + 1]
            pivots = jnp.where(row[:, 0:1] == j, pivot, pivots)
            if j + 1 == tile:
                break
            mult = jnp.where(row[base:, 0:1] > j, live[:, j : j + 1], 0.0)
            live = live - mult * (lead / pivot)
            w = live if base == 0 else jnp.concatenate([w[:base], live], axis=0)
        pair[...] = w * (1.0 / jnp.sqrt(pivots))
        inverse = pair[:, tile : 2 * tile]
        lead_rows = plain_dot(inverse, aug[lo:hi, :], HIGHEST)
        grow = lax.broadcasted_iota(jnp.int32, (tile, size), 0) + lo
        gcol = lax.broadcasted_iota(jnp.int32, (tile, size), 1)
        upper = jnp.where(gcol >= grow, lead_rows[:, 0:size], 0.0)
        upper_ref[lo:hi, :] = upper * (1.0 / root)
        inv_ref[lo:hi, :] = lead_rows[:, size : 2 * size]
        if hi < edge:
            aug[...] = aug[...] - lax.dot_general(
                upper,
                lead_rows,
                (((0,), (0,)), ((), ())),
                precision=HIGHEST,
                preferred_element_type=F32,
            )

    def make_basis():
        factor = inv_ref[...]
        own = pl.ds(pl.multiple_of(z * (ctp * SUB), ctp * SUB), ctp * SUB)

        def body(b, carry):
            both = plain_dot(factor, panel_block(b, narrow), HIGH)
            mine_only = plain_dot(inv_ref[own, :] * root, panel_block(b, narrow), HIGH)
            for k in range(narrow):
                lanes = slice(k * BW, (k + 1) * BW)
                place = narrow * b + k
                part = both[:, lanes]
                upper_half = part.astype(jnp.bfloat16)
                high_ref[place] = upper_half
                low_ref[place] = (part - upper_half.astype(F32)).astype(jnp.bfloat16)
                q_ref[:, place] = mine_only[:, lanes].reshape(ctp, SUB, BW)
            return carry

        lax.fori_loop(0, blocks // narrow, body, 0)

    def emit(chunks):
        for t in chunks:
            cross_done(t)
        rows = [cross_ref[t].reshape(rows_t, size) for t in chunks]
        left_side = three_part(rows_dot(joined(rows), inv_ref[...], HIGHEST))

        def body(b, carry):
            both = removed(left_side, high_ref, low_ref, wide * b, wide)
            for k in range(wide):
                lanes = slice(k * BW, (k + 1) * BW)
                place = wide * b + k
                for i, t in enumerate(chunks):
                    part = both[i * rows_t : (i + 1) * rows_t, lanes]
                    reg[:, t, place] = reg[:, t, place] - part.reshape(ot, SUB, BW)
            return carry

        lax.fori_loop(0, blocks // wide, body, 0)

    def start_copy(copy):
        copy.start()

    @only(has_p(me), op == n)
    def _():
        own_p.start()

    started(p1, has_p, op)

    start_t1(0, picked=ahead)

    @only(has_p(me), op == n)
    def _():
        own_p.wait()

    once(has_p, op, lambda k: whole(ring_p.at[:, pl.ds(0, k * blocks)], p1_send.at[0], p1_recv.at[0]), take)

    @only(has_p(me), op == n)
    def _():
        for t in range(tp):
            wrap(ring_p.at[t])
        shifts = [
            [panel_shift[(me * tp + t) * SUB + c] for c in range(SUB)] for t in range(tp)
        ]

        def turn(d, to, origin):
            for t in range(tp):

                def put(h, block, t=t):
                    moved_p[to, t, pl.ds(h, step)] = block

                compose(ring_p.at[t], shifts[t], to, put)

        each_peer(turn)

        def go(d, to, origin):
            p2(d, to).start()

        each_peer(go)
        for t in range(tp):

            def keep(h, block, t=t):
                full[z, me * tp + t, pl.ds(h, step)] = block

            compose(ring_p.at[t], shifts[t], me, keep)

    last = tt - 1
    start_t1(0, picked=behind)
    if tt > 1:
        start_t1(1)
    counted(has_p, op, lambda k: whole(full.at[z, pl.ds(0, k * tp)], p2_send.at[0], p2_recv.at[0]), take)
    for q in range(pieces):
        for side in (0, 1):

            @pl.when(sends(side, 1))
            def _():
                line(side, 1, q).start()

    middle = max(depth // 2, 1)
    turn_t(0)
    if last > 0:
        start_t2(0)
    follows = jnp.logical_not(leads)

    @pl.when(follows)
    def _():
        for t in range(2, last):
            start_t1(t)

    for d in range(1, middle):
        forward(d)

    def rest_t1():
        if last > 1:
            start_t1(last)

    def rest_t2():
        for t in range(2, last):
            start_t2(t)

    def finish_turns():
        if last > 0:
            turn_t(last)
        start_t2(last)

    def cross_chunk(t):
        if t == last:
            wait_t2(t, 0)
            make_cross(t, 0, blocks // 2)
            wait_t2(t, 1)
            make_cross(t, blocks // 2, blocks)
        else:
            wait_t2(t)
            make_cross(t)
        cross_scatter(t)

    early = min(2, last)

    def border():
        far = far_sum[...].reshape(tile, size)
        corner = rows_dot(inv_ref[0:edge, 0:edge], far[:, 0:edge], HIGHEST)
        upper_ref[0:edge, edge:size] = corner * (1.0 / root)

        def turned(right):
            return lax.dot_general(
                corner,
                right,
                (((0,), (0,)), ((), ())),
                precision=HIGHEST,
                preferred_element_type=F32,
            )

        aug[edge:size, edge:size] = far[:, edge:size] - turned(corner)
        aug[edge:size, size : 2 * size] = aug[edge:size, size : 2 * size] - turned(inv_ref[0:edge, :])

    @pl.when(leads)
    def _():
        gram_near()
        gram_scatter(0)
        if last > 2:
            start_t1(2, (0,))
        if last > 1:
            turn_t(1)
        aug_row = lax.broadcasted_iota(jnp.int32, (size, 2 * size), 0)
        aug_col = lax.broadcasted_iota(jnp.int32, (size, 2 * size), 1)
        aug[...] = jnp.where(aug_col == aug_row + size, 1.0, 0.0)
        gram_spread(0)
        for t in range(2, last):
            start_t1(t, (1,) if t == 2 else (0, 1))
        if last > 1:
            start_t2(1)
        forward(middle, range(pieces // 2))
        gram_done(0)
        forward(middle, range(pieces // 2, pieces - 1))
        unpack_near()
        for i in range(tiles - 1):
            factor_tile(i)
            send_factor(i, 0, start_copy)
            if i == 0:
                forward(middle, range(pieces - 1, pieces))
                rest_t1()
                for t in range(2, last):
                    turn_t(t)
            if i == min(1, tiles - 2):
                rest_t2()
        far_copy(helper_z).wait_recv()
        border()
        factor_tile(tiles - 1)
        send_factor(tiles - 1, 0, start_copy)
        for i in range(tiles):
            send_factor(i, 1, start_copy)
        finish_turns()
        for t in range(early):
            cross_chunk(t)
        gram_clear(0)

    @pl.when(follows)
    def _():
        for t in range(1, last):
            turn_t(t)
            if t == 1:
                start_t2(t)
                for d in range(middle, middle + 1):
                    forward(d)
        if last < 2:
            for d in range(middle, middle + 1):
                forward(d)

        @pl.when(helps)
        def _():
            gram_far()
            gram_scatter(1)
            if last > 1:
                start_t1(last, picked=ahead)
            gram_spread(1)
            if last > 1:
                start_t1(last, picked=behind)

        @pl.when(jnp.logical_not(helps))
        def _():
            rest_t1()

        rest_t2()

        @pl.when(helps)
        def _():
            gram_done(1)
            far_copy(lead_z).start()
            gram_clear(1)

        finish_turns()
        for d in range(middle + 1, depth):
            forward(d)
        for t in range(early):
            cross_chunk(t)
        factor_whole(0).wait_recv()

    make_basis()
    for t in range(early, tt):
        cross_chunk(t)
    for t in range(tt):
        cross_spread(t)
    if early > 0:
        emit(list(range(early)))
    for t in range(early, tt):
        cross_done(t)

    @pl.when(follows)
    def _():
        factor_whole(1).wait_recv()

    @pl.when(helps)
    def _():
        far_copy(lead_z).wait_send()

    @pl.when(leads)
    def _():
        for other in range(depth):
            if other != lead_z:
                for k in (0, 1):
                    factor_whole(k, other).wait_send()

    counted(has_p, op, lambda k: whole(ring_p.at[:, pl.ds(0, k * blocks)], p1_send.at[0], p1_recv.at[0]), clear)
    once(has_p, op, lambda k: whole(ring_p.at[:, pl.ds(0, k * blocks)], p2_send.at[0], p2_recv.at[0]), clear)
    for t in range(tt):
        ring = rings[t]
        counted(has_t, ot, lambda k: whole(ring.at[pl.ds(0, k * blocks)], t1_send.at[t], t1_recv.at[t]), clear)
        for sem in (t, t + 1) if t == tt - 1 else (t,):
            bulk = blocks // 2 if t == tt - 1 else blocks
            once(has_t, ot, lambda k: whole(ring.at[pl.ds(0, k * bulk)], t2_send.at[sem], t2_recv.at[sem]), clear)
        land = cross_land.at[t]
        counted(has_c, oc, lambda k: whole(land.at[pl.ds(0, k)], c_send.at[0, t], c_recv.at[0, t]), clear)
        once(has_c, oc, lambda k: whole(land.at[pl.ds(0, k)], c_send.at[1, t], c_recv.at[1, t]), clear)
    for d in range(1, depth):
        for q in range(pieces):
            for side in (0, 1):

                @pl.when(sends(side, d))
                def _():
                    line(side, d, q).wait_send()


def fused(panel, trail, panel_shift, trail_shift, n, depth, root):
    ctp, blocks = panel.shape[0], panel.shape[1]
    ctt = trail.shape[0]
    tp = -(-ctp // n)
    tt = -(-ctt // n)
    op, ot = ctp // tp, ctt // tt
    size = depth * ctp * SUB
    rows_t = ot * SUB
    sr = max(SUB, rows_t // n)
    oc = rows_t // sr
    tile = 64
    tiles = size // tile
    edge = size - tile
    packed = tile * (tiles * (tiles - 1) // 2)
    far_rows = -(-tile // (n * SUB)) * SUB
    pieces = 4 if ctp % 4 == 0 else 1
    total = n * blocks
    smem = pl.BlockSpec(memory_space=pltpu.SMEM)
    vmem = pl.BlockSpec(memory_space=pltpu.VMEM)
    hbm = pl.BlockSpec(memory_space=pl.ANY)
    dma = pltpu.SemaphoreType.DMA
    peers = max(n - 1, 1)
    lines = max(depth - 1, 1)
    return pl.pallas_call(
        functools.partial(fused_kernel, n, depth, pieces, root),
        out_shape=(
            pltpu.VMEM((size, size), F32),
            pltpu.VMEM((size, size), F32),
            pltpu.VMEM((tt, oc, sr, size), F32),
            pltpu.VMEM(panel.shape, F32),
            pltpu.VMEM((ot, tt) + trail.shape[1:], F32),
            pltpu.VMEM((blocks, size, BW), jnp.bfloat16),
            pltpu.VMEM((blocks, size, BW), jnp.bfloat16),
        ),
        in_specs=[smem, smem, hbm, hbm],
        out_specs=(vmem,) * 7,
        scratch_shapes=[
            pltpu.VMEM((depth,) + panel.shape, F32),
            pltpu.VMEM((tp, total + blocks, SUB, BW), F32),
            pltpu.VMEM((n, tp, blocks, SUB, BW), F32),
            pltpu.VMEM((tt, n, blocks, SUB, BW), F32),
            pltpu.VMEM((edge, edge), F32),
            pltpu.VMEM((tile // far_rows, far_rows, packed), F32),
            pltpu.VMEM((peers, far_rows, packed), F32),
            pltpu.VMEM((tile // far_rows, far_rows, packed), F32),
            pltpu.VMEM((tile // far_rows, far_rows, size), F32),
            pltpu.VMEM((peers, far_rows, size), F32),
            pltpu.VMEM((tile // far_rows, far_rows, size), F32),
            pltpu.VMEM((tt, oc, sr, size), F32),
            pltpu.VMEM((tt, peers, sr, size), F32),
            pltpu.VMEM((size, 2 * size), F32),
            pltpu.VMEM((tile, 2 * tile), F32),
            dma((1,)),
            dma((1,)),
            dma((1,)),
            dma((1,)),
            dma((tt,)),
            dma((tt,)),
            dma((tt + 1,)),
            dma((tt + 1,)),
            dma((2, lines, pieces)),
            dma((2, lines, pieces)),
            dma((2, 2)),
            dma((2, 2)),
            dma((2, tt)),
            dma((2, tt)),
            dma((depth, 2)),
            dma((2,)),
            dma((1,)),
            dma((1,)),
            dma((1 + tt,)),
        ]
        + [pltpu.VMEM((total + blocks, SUB, BW), F32)] * tt,
        compiler_params=pltpu.CompilerParams(
            collective_id=3, has_side_effects=True, vmem_limit_bytes=40 << 20
        ),
        cost_estimate=pl.CostEstimate(
            flops=0, bytes_accessed=40 * trail.size * 4, transcendentals=0
        ),
    )(panel_shift, trail_shift, panel, trail)


def final_kernel(
    root,
    early,
    upper,
    inv,
    cross,
    q,
    reg,
    high_ref,
    low_ref,
    r_ref,
    coupling_ref,
    q_ref,
    out_ref,
    late,
    coupling,
    sems,
):
    size = inv.shape[0]
    ot, tt, blocks = reg.shape[:3]
    rows_t = ot * SUB
    chunks = list(range(early, tt))
    steps = 2 if blocks % 2 == 0 else 1
    span = blocks // steps
    copies = [pltpu.make_async_copy(q, q_ref, sems.at[0])]
    copies.append(pltpu.make_async_copy(upper, r_ref, sems.at[1]))
    for t in range(early):
        copies.append(pltpu.make_async_copy(reg.at[:, t], out_ref.at[:, t], sems.at[2 + t]))
    for copy in copies:
        copy.start()
    rows = joined([cross[t].reshape(rows_t, size) for t in chunks])
    left_side = three_part(rows_dot(rows, inv[...], HIGHEST))
    narrow = min(8, span)
    for h in range(steps):

        def body(b, carry, h=h):
            first = h * span + narrow * b
            both = removed(left_side, high_ref, low_ref, first, narrow)
            for k in range(narrow):
                lanes = slice(k * BW, (k + 1) * BW)
                for i, t in enumerate(chunks):
                    part = both[i * rows_t : (i + 1) * rows_t, lanes]
                    late[:, i, first + k] = reg[:, t, first + k] - part.reshape(ot, SUB, BW)
            return carry

        lax.fori_loop(0, span // narrow, body, 0)
        for i, t in enumerate(chunks):
            place = pl.ds(h * span, span)
            copy = pltpu.make_async_copy(
                late.at[:, i, place], out_ref.at[:, t, place], sems.at[2 + early + h * len(chunks) + i]
            )
            copy.start()
            copies.append(copy)
    every = jnp.stack([cross[t].reshape(ot, SUB, size) for t in range(tt)], axis=1)
    coupling[...] = rows_dot(
        inv[...] * (1.0 / root), every.reshape(ot * tt * SUB, size), HIGHEST
    )
    last = pltpu.make_async_copy(coupling, coupling_ref, sems.at[2 + early + steps * len(chunks)])
    last.start()
    copies.append(last)
    for copy in copies:
        copy.wait()


def final(upper, inv, cross, q, reg, high, low, root):
    size = inv.shape[0]
    ot, tt = reg.shape[:2]
    early = min(2, tt - 1)
    vmem = pl.BlockSpec(memory_space=pltpu.VMEM)
    hbm = pl.BlockSpec(memory_space=pl.ANY)
    near = [pltpu.with_memory_space_constraint(x, pltpu.VMEM) for x in (upper, inv, cross, q, reg, high, low)]
    return pl.pallas_call(
        functools.partial(final_kernel, root, early),
        out_shape=(
            jax.ShapeDtypeStruct((size, size), F32),
            jax.ShapeDtypeStruct((size, ot * tt * SUB), F32),
            jax.ShapeDtypeStruct(q.shape, F32),
            jax.ShapeDtypeStruct(reg.shape, F32),
        ),
        in_specs=[vmem] * 7,
        out_specs=(hbm,) * 4,
        scratch_shapes=[
            pltpu.VMEM((ot, tt - early) + reg.shape[2:], F32),
            pltpu.VMEM((size, ot * tt * SUB), F32),
            pltpu.SemaphoreType.DMA((3 + early + 2 * (tt - early),)),
        ],
        compiler_params=pltpu.CompilerParams(vmem_limit_bytes=24 << 20),
        cost_estimate=pl.CostEstimate(
            flops=2 * size * reg.size, bytes_accessed=8 * reg.size, transcendentals=0
        ),
    )(*near)


def tiled(raw):
    rows, pixels = raw.shape
    return raw.reshape(rows // SUB, SUB, pixels // BW, BW).transpose(0, 2, 1, 3)


def flat(blocked):
    cut, blocks = blocked.shape[0], blocked.shape[1]
    return blocked.transpose(0, 2, 1, 3).reshape(cut * SUB, blocks * BW)


def on_device(raw_panel, raw_trail, panel_shift, trail_shift):
    n = lax.axis_size("rows")
    depth = lax.axis_size("cols")
    pixels = raw_panel.shape[1]
    root = math.sqrt(pixels * n)
    raw = [
        pltpu.with_memory_space_constraint(tiled(x), pltpu.HBM) for x in (raw_panel, raw_trail)
    ]
    shifts = [
        pltpu.with_memory_space_constraint(x, pltpu.HBM) for x in (panel_shift, trail_shift)
    ]
    held = fused(
        *raw, *shifts, n, depth, root
    )
    r_factor, coupling, q_panel, out = final(*held, root)
    return (r_factor, coupling, flat(q_panel), flat(out.reshape((-1,) + out.shape[2:])))


def solution(mesh):
    placed = (P("cols", "rows"), P("cols", "rows"), P("cols"), P("cols"))
    return jax.shard_map(
        on_device,
        mesh=mesh,
        in_specs=placed,
        out_specs=(P(), P(None, "cols"), P("cols", "rows"), P("cols", "rows")),
        check_vma=False,
    )
```

```python
import functools
import math

import jax
import jax.numpy as jnp
from jax import lax
from jax.experimental import pallas as pl
from jax.experimental.pallas import tpu as pltpu
from jax.sharding import PartitionSpec as P

BW = 128
SUB = 8
MESH = pl.DeviceIdType.MESH
F32 = jnp.float32
HIGHEST = lax.Precision.HIGHEST
HIGH = lax.Precision.HIGH


def rows_dot(left, right, precision):
    return lax.dot_general(
        left,
        right,
        (((1,), (1,)), ((), ())),
        precision=precision,
        preferred_element_type=F32,
    )


def plain_dot(left, right, precision):
    return lax.dot_general(
        left,
        right,
        (((1,), (0,)), ((), ())),
        precision=precision,
        preferred_element_type=F32,
    )


def joined(parts):
    return jnp.concatenate(parts, axis=0) if len(parts) > 1 else parts[0]


def three_part(value):
    high = value.astype(jnp.bfloat16)
    low = (value - high.astype(F32)).astype(jnp.bfloat16)
    return jnp.concatenate([high, high, low], axis=1)


def removed(left_side, high_ref, low_ref, first, count):
    high = jnp.concatenate([high_ref[first + k] for k in range(count)], axis=1)
    low = jnp.concatenate([low_ref[first + k] for k in range(count)], axis=1)
    return plain_dot(left_side, jnp.concatenate([high, low, high], axis=0), None)


def only(cond, always):
    if always:
        return lambda fn: fn()
    return pl.when(cond)


def fused_kernel(
    n,
    depth,
    pieces,
    root,
    panel_shift,
    trail_shift,
    panel,
    trail,
    upper_ref,
    inv_ref,
    cross_ref,
    q_ref,
    reg,
    high_ref,
    low_ref,
    full,
    ring_p,
    moved_p,
    moved_t,
    near_all,
    near_part,
    near_land,
    near_sum,
    far_part,
    far_land,
    far_sum,
    cross_part,
    cross_land,
    aug,
    pair,
    p1_send,
    p1_recv,
    p2_send,
    p2_recv,
    t1_send,
    t1_recv,
    t2_send,
    t2_recv,
    z_send,
    z_recv,
    g_send,
    g_recv,
    c_send,
    c_recv,
    f_send,
    f_recv,
    h_send,
    h_recv,
    local_sem,
    *rings,
):
    me = lax.axis_index("rows")
    z = lax.axis_index("cols")
    ctp, blocks = panel.shape[0], panel.shape[1]
    ctt = trail.shape[0]
    total = n * blocks
    tp = ring_p.shape[0]
    tt = len(rings)
    op, ot = ctp // tp, ctt // tt
    rows_t = ot * SUB
    sr = cross_land.shape[2]
    oc = rows_t // sr
    size = inv_ref.shape[0]
    lead_z = max(depth // 2 - 1, 0)
    leads = z == lead_z
    helper_z = min(lead_z + 1, depth - 1)
    helps = z == helper_z
    tile = pair.shape[0]
    tiles = size // tile
    edge = size - tile
    near_count = edge // (ctp * SUB)
    mine = pl.ds(pl.multiple_of(me * blocks, blocks), blocks)

    def each_peer(fn):
        def body(d, carry):
            fn(d, lax.rem(me + d, n), lax.rem(me - d + n, n))
            return carry

        lax.fori_loop(1, n, body, 0)

    def linked(other):
        near = (z - other == 1) | (other - z == 1)
        return near | (z != other) & (leads | (other == lead_z))

    barrier = pltpu.get_barrier_semaphore()
    for d in range(1, n):
        pl.semaphore_signal(
            barrier, inc=1, device_id={"rows": lax.rem(me + d, n)}, device_id_type=MESH
        )
    greeted = n - 1
    for other in range(depth):

        @pl.when(linked(other))
        def _():
            pl.semaphore_signal(barrier, inc=1, device_id={"cols": other}, device_id_type=MESH)

        greeted = greeted + jnp.where(linked(other), 1, 0)
    pl.semaphore_wait(barrier, greeted)

    def row_copy(src, dst, send, recv, to):
        return pltpu.make_async_remote_copy(
            src_ref=src,
            dst_ref=dst,
            send_sem=send,
            recv_sem=recv,
            device_id={"rows": to},
            device_id_type=MESH,
        )

    def p1(d, to):
        return row_copy(
            panel.at[pl.ds(to * tp, tp)],
            ring_p.at[:, mine],
            p1_send.at[0],
            p1_recv.at[0],
            to,
        )

    def p2(d, to):
        return row_copy(
            moved_p.at[to],
            full.at[z, pl.ds(me * tp, tp)],
            p2_send.at[0],
            p2_recv.at[0],
            to,
        )

    def t1(t, d, to):
        return row_copy(
            trail.at[to * tt + t],
            rings[t].at[mine],
            t1_send.at[t],
            t1_recv.at[t],
            to,
        )

    def t2(t, half, d, to):
        cut = pl.ds(0, blocks) if half is None else pl.ds(half * (blocks // 2), blocks // 2)
        return row_copy(
            moved_t.at[t, to, cut],
            reg.at[me, t, cut],
            t2_send.at[t + (1 if half == 1 else 0)],
            t2_recv.at[t + (1 if half == 1 else 0)],
            to,
        )

    own_p = pltpu.make_async_copy(
        panel.at[pl.ds(me * tp, tp)], ring_p.at[:, mine], local_sem.at[0]
    )

    def own_t(t):
        return pltpu.make_async_copy(
            trail.at[me * tt + t], rings[t].at[mine], local_sem.at[1 + t]
        )

    def started(copies, active, count, first=1, stride=1, pick=None):
        def go(k, carry):
            d = first + stride * k
            to = lax.rem(me + d, n)
            wanted = active(to) if pick is None else active(to) & pick(d)

            @only(wanted, count == n and pick is None)
            def _():
                copies(d, to).start()

            return carry

        lax.fori_loop(0, -(-(n - first) // stride), go, 0)

    def whole(region, send, recv):
        return row_copy(region, region, send, recv, lax.rem(me + 1, n))

    def counted(active, count, per_copy, done):
        if count == n:
            done(per_copy(n - 1))
        else:

            @pl.when(active(me))
            def _():
                done(per_copy(count - 1))

            @pl.when(jnp.logical_not(active(me)))
            def _():
                done(per_copy(count))

    def once(active, count, per_copy, done):
        @only(active(me), count == n)
        def _():
            done(per_copy(n - 1))

    def take(copy):
        copy.wait_recv()

    def clear(copy):
        copy.wait_send()

    def has_p(j):
        return j < op

    def has_t(j):
        return j < ot

    sub = lax.broadcasted_iota(jnp.int32, (1, SUB, BW), 1)
    step = min(16, blocks)

    def compose(ring, shifts, to, put):
        starts = [lax.rem(to * blocks - s + total, total) for s in shifts]
        for h in range(0, blocks, step):
            block = ring[pl.ds(starts[0] + h, step)]
            for c in range(1, SUB):
                block = jnp.where(sub == c, ring[pl.ds(starts[c] + h, step)], block)
            put(h, block)

    def wrap(ring):
        ring[pl.ds(total, blocks)] = ring[pl.ds(0, blocks)]

    def line(side, d, q):
        step_z = 1 if side == 0 else -1
        origin = z - step_z * (d - 1)
        rows = pl.ds(q * (ctp // pieces), ctp // pieces)
        return pltpu.make_async_remote_copy(
            src_ref=full.at[origin, rows],
            dst_ref=full.at[origin, rows],
            send_sem=z_send.at[side, d - 1, q],
            recv_sem=z_recv.at[side, d - 1, q],
            device_id={"cols": z + step_z},
            device_id_type=MESH,
        )

    def sends(side, d):
        if side == 0:
            return (z + 1 < depth) & (z - (d - 1) >= 0)
        return (z >= 1) & (z + (d - 1) < depth)

    def receives(side, d):
        return z - d >= 0 if side == 0 else z + d < depth

    def arrived(side, d, q):
        step_z = 1 if side == 0 else -1
        origin = z - step_z * d
        rows = pl.ds(q * (ctp // pieces), ctp // pieces)
        return pltpu.make_async_remote_copy(
            src_ref=full.at[origin, rows],
            dst_ref=full.at[origin, rows],
            send_sem=z_send.at[side, d - 1, q],
            recv_sem=z_recv.at[side, d - 1, q],
            device_id={"cols": z - step_z},
            device_id_type=MESH,
        )

    def forward(d, some=None):
        for q in range(pieces) if some is None else some:
            for side in (0, 1):

                @pl.when(receives(side, d))
                def _():
                    arrived(side, d, q).wait_recv()

                if d + 1 < depth:

                    @pl.when(sends(side, d + 1))
                    def _():
                        line(side, d + 1, q).start()

    def ahead(d):
        return (d == 2) | (d == 4) | (d == 6)

    def behind(d):
        return jnp.logical_not(ahead(d))

    def start_t1(t, halves=(0, 1), picked=None):
        if 0 in halves and picked is not behind:

            @only(has_t(me), ot == n)
            def _():
                own_t(t).start()

        if len(halves) == 2:
            started(functools.partial(t1, t), has_t, ot, pick=picked)
        else:
            started(functools.partial(t1, t), has_t, ot, 2 - halves[0], 2)

    def turn_t(t):
        @only(has_t(me), ot == n)
        def _():
            own_t(t).wait()

        once(has_t, ot, lambda k: whole(rings[t].at[pl.ds(0, k * blocks)], t1_send.at[t], t1_recv.at[t]), take)

        @only(has_t(me), ot == n)
        def _():
            wrap(rings[t])
            shifts = [trail_shift[(me * tt + t) * SUB + c] for c in range(SUB)]

            def turn(d, to, origin):
                def put(h, block):
                    moved_t[t, to, pl.ds(h, step)] = block

                compose(rings[t], shifts, to, put)

            each_peer(turn)

            def keep(h, block):
                reg[me, t, pl.ds(h, step)] = block

            compose(rings[t], shifts, me, keep)

    def start_t2(t):
        @only(has_t(me), ot == n)
        def _():
            for half in (0, 1) if t == tt - 1 else (None,):
                started(functools.partial(t2, t, half), has_t, n)

    def wait_t2(t, half=None):
        cut = pl.ds(0, blocks if half is None else blocks // 2)
        sem = t + (1 if half == 1 else 0)
        counted(has_t, ot, lambda k: whole(reg.at[pl.ds(0, k), t, cut], t2_send.at[sem], t2_recv.at[sem]), take)

    def panel_block(b, count, lo=0, hi=depth):
        rows = (hi - lo) * ctp * SUB
        cut = [full[lo:hi, :, count * b + k].reshape(rows, BW) for k in range(count)]
        return jnp.concatenate(cut, axis=1)

    narrow = min(4, blocks)
    wide = min(8, blocks // 2)

    def gram_near():
        near_all[...] = jnp.zeros_like(near_all)

        def body(b, carry):
            block = panel_block(b, narrow, 0, near_count)
            near_all[...] += rows_dot(block, block, HIGHEST)
            return carry

        lax.fori_loop(0, blocks // narrow, body, 0)
        packed = [near_all[lo : lo + tile, lo:edge] for lo in range(0, edge, tile)]
        near_part[...] = jnp.concatenate(packed, axis=1).reshape(near_part.shape)

    def unpack_near():
        packed = near_sum[...].reshape(tile, near_sum.shape[2])
        first = 0
        for lo in range(0, edge, tile):
            aug[lo : lo + tile, lo:edge] = packed[:, first : first + edge - lo]
            first += edge - lo

    def gram_far():
        far_part[...] = jnp.zeros_like(far_part)

        def body(b, carry):
            block = panel_block(b, narrow, near_count, depth)
            both = rows_dot(block, panel_block(b, narrow), HIGHEST)
            far_part[...] += both.reshape(far_part.shape)
            return carry

        lax.fori_loop(0, blocks // narrow, body, 0)

    grams = ((near_part, near_land, near_sum), (far_part, far_land, far_sum))

    def g_one(k, d, to):
        part, land, _ = grams[k]
        return row_copy(part.at[to], land.at[d - 1], g_send.at[k, 0], g_recv.at[k, 0], to)

    def g_two(k, d, to):
        ref = grams[k][2]
        return row_copy(ref.at[me], ref.at[me], g_send.at[k, 1], g_recv.at[k, 1], to)

    def g_count(k):
        return grams[k][0].shape[0]

    def has_g(k):
        return lambda j: j < g_count(k)

    def gram_scatter(k):
        started(functools.partial(g_one, k), has_g(k), g_count(k))

    def gram_spread(k):
        part, land, total_ref = grams[k]

        @only(me < g_count(k), g_count(k) == n)
        def _():
            take(whole(land, g_send.at[k, 0], g_recv.at[k, 0]))
            total_g = part[me]
            for d in range(1, n):
                total_g = total_g + land[d - 1]
            total_ref[me] = total_g

            def go(d, to, origin):
                g_two(k, d, to).start()

            each_peer(go)

    def gram_done(k):
        ref = grams[k][2]
        counted(has_g(k), g_count(k), lambda m: whole(ref.at[pl.ds(0, m)], g_send.at[k, 1], g_recv.at[k, 1]), take)

    def gram_clear(k):
        land = grams[k][1]
        counted(has_g(k), g_count(k), lambda m: whole(land.at[pl.ds(0, m)], g_send.at[k, 0], g_recv.at[k, 0]), clear)
        once(has_g(k), g_count(k), lambda m: whole(land.at[pl.ds(0, m)], g_send.at[k, 1], g_recv.at[k, 1]), clear)

    def far_copy(to):
        return pltpu.make_async_remote_copy(
            src_ref=far_sum,
            dst_ref=far_sum,
            send_sem=h_send.at[0],
            recv_sem=h_recv.at[0],
            device_id={"cols": to},
            device_id_type=MESH,
        )

    def has_c(j):
        return j < oc

    def make_cross(t, lo=0, hi=blocks):
        if lo == 0:
            cross_part[t] = jnp.zeros_like(cross_part[t])

        def body(b, carry):
            cut = [reg[:, t, wide * b + k].reshape(rows_t, BW) for k in range(wide)]
            block = jnp.concatenate(cut, axis=1)
            both = rows_dot(block, panel_block(b, wide), HIGH)
            cross_part[t] += both.reshape(oc, sr, size)
            return carry

        lax.fori_loop(lo // wide, hi // wide, body, 0)

    def c_one(t, d, to):
        return row_copy(
            cross_part.at[t, to],
            cross_land.at[t, d - 1],
            c_send.at[0, t],
            c_recv.at[0, t],
            to,
        )

    def c_two(t, d, to):
        return row_copy(
            cross_ref.at[t, me],
            cross_ref.at[t, me],
            c_send.at[1, t],
            c_recv.at[1, t],
            to,
        )

    def cross_scatter(t):
        started(functools.partial(c_one, t), has_c, oc)

    def cross_spread(t):
        @only(has_c(me), oc == n)
        def _():
            take(whole(cross_land.at[t], c_send.at[0, t], c_recv.at[0, t]))
            total_c = cross_part[t, me]
            for d in range(1, n):
                total_c = total_c + cross_land[t, d - 1]
            cross_ref[t, me] = total_c

            def go(d, to, origin):
                c_two(t, d, to).start()

            each_peer(go)

    def cross_done(t):
        counted(has_c, oc, lambda k: whole(cross_ref.at[t, pl.ds(0, k)], c_send.at[1, t], c_recv.at[1, t]), take)

    def factor_copy(i, k, slot, to):
        ref = inv_ref if k == 0 else upper_ref
        rows = pl.ds(i * tile, tile)
        return pltpu.make_async_remote_copy(
            src_ref=ref.at[rows],
            dst_ref=ref.at[rows],
            send_sem=f_send.at[slot, k],
            recv_sem=f_recv.at[k],
            device_id={"cols": to},
            device_id_type=MESH,
        )

    def factor_whole(k, slot=0):
        ref = inv_ref if k == 0 else upper_ref
        return pltpu.make_async_remote_copy(
            src_ref=ref,
            dst_ref=ref,
            send_sem=f_send.at[slot, k],
            recv_sem=f_recv.at[k],
            device_id={"cols": lax.rem(z + 1, depth)},
            device_id_type=MESH,
        )

    def send_factor(i, k, act):
        for other in range(depth):
            if other != lead_z:
                act(factor_copy(i, k, other, other))

    def factor_tile(i):
        lo = i * tile
        hi = lo + tile
        row = lax.broadcasted_iota(jnp.int32, (tile, 2 * tile), 0)
        col = lax.broadcasted_iota(jnp.int32, (tile, 2 * tile), 1)
        pair[...] = jnp.where(col == row + tile, 1.0, 0.0)
        pair[:, 0:tile] = aug[lo:hi, lo:hi]
        w = pair[...]
        pivots = jnp.zeros((tile, 1), F32)
        for j in range(tile):
            base = j // 8 * 8
            live = w[base:, :]
            lead = w[j : j + 1, :]
            pivot = lead[:, j : j + 1]
            pivots = jnp.where(row[:, 0:1] == j, pivot, pivots)
            if j + 1 == tile:
                break
            mult = jnp.where(row[base:, 0:1] > j, live[:, j : j + 1], 0.0)
            live = live - mult * (lead / pivot)
            w = live if base == 0 else jnp.concatenate([w[:base], live], axis=0)
        pair[...] = w * (1.0 / jnp.sqrt(pivots))
        inverse = pair[:, tile : 2 * tile]
        lead_rows = plain_dot(inverse, aug[lo:hi, :], HIGHEST)
        grow = lax.broadcasted_iota(jnp.int32, (tile, size), 0) + lo
        gcol = lax.broadcasted_iota(jnp.int32, (tile, size), 1)
        upper = jnp.where(gcol >= grow, lead_rows[:, 0:size], 0.0)
        upper_ref[lo:hi, :] = upper * (1.0 / root)
        inv_ref[lo:hi, :] = lead_rows[:, size : 2 * size]
        if hi < edge:
            aug[...] = aug[...] - lax.dot_general(
                upper,
                lead_rows,
                (((0,), (0,)), ((), ())),
                precision=HIGHEST,
                preferred_element_type=F32,
            )

    def make_basis():
        factor = inv_ref[...]
        own = pl.ds(pl.multiple_of(z * (ctp * SUB), ctp * SUB), ctp * SUB)

        def body(b, carry):
            both = plain_dot(factor, panel_block(b, narrow), HIGH)
            mine_only = plain_dot(inv_ref[own, :] * root, panel_block(b, narrow), HIGH)
            for k in range(narrow):
                lanes = slice(k * BW, (k + 1) * BW)
                place = narrow * b + k
                part = both[:, lanes]
                upper_half = part.astype(jnp.bfloat16)
                high_ref[place] = upper_half
                low_ref[place] = (part - upper_half.astype(F32)).astype(jnp.bfloat16)
                q_ref[:, place] = mine_only[:, lanes].reshape(ctp, SUB, BW)
            return carry

        lax.fori_loop(0, blocks // narrow, body, 0)

    def emit(chunks):
        for t in chunks:
            cross_done(t)
        rows = [cross_ref[t].reshape(rows_t, size) for t in chunks]
        left_side = three_part(rows_dot(joined(rows), inv_ref[...], HIGHEST))

        def body(b, carry):
            both = removed(left_side, high_ref, low_ref, wide * b, wide)
            for k in range(wide):
                lanes = slice(k * BW, (k + 1) * BW)
                place = wide * b + k
                for i, t in enumerate(chunks):
                    part = both[i * rows_t : (i + 1) * rows_t, lanes]
                    reg[:, t, place] = reg[:, t, place] - part.reshape(ot, SUB, BW)
            return carry

        lax.fori_loop(0, blocks // wide, body, 0)

    def start_copy(copy):
        copy.start()

    @only(has_p(me), op == n)
    def _():
        own_p.start()

    started(p1, has_p, op)

    start_t1(0, picked=ahead)

    @only(has_p(me), op == n)
    def _():
        own_p.wait()

    once(has_p, op, lambda k: whole(ring_p.at[:, pl.ds(0, k * blocks)], p1_send.at[0], p1_recv.at[0]), take)

    @only(has_p(me), op == n)
    def _():
        for t in range(tp):
            wrap(ring_p.at[t])
        shifts = [
            [panel_shift[(me * tp + t) * SUB + c] for c in range(SUB)] for t in range(tp)
        ]

        def turn(d, to, origin):
            for t in range(tp):

                def put(h, block, t=t):
                    moved_p[to, t, pl.ds(h, step)] = block

                compose(ring_p.at[t], shifts[t], to, put)

        each_peer(turn)

        def go(d, to, origin):
            p2(d, to).start()

        each_peer(go)
        for t in range(tp):

            def keep(h, block, t=t):
                full[z, me * tp + t, pl.ds(h, step)] = block

            compose(ring_p.at[t], shifts[t], me, keep)

    last = tt - 1
    start_t1(0, picked=behind)
    if tt > 1:
        start_t1(1)
    counted(has_p, op, lambda k: whole(full.at[z, pl.ds(0, k * tp)], p2_send.at[0], p2_recv.at[0]), take)
    for q in range(pieces):
        for side in (0, 1):

            @pl.when(sends(side, 1))
            def _():
                line(side, 1, q).start()

    middle = max(depth // 2, 1)
    turn_t(0)
    if last > 0:
        start_t2(0)
    follows = jnp.logical_not(leads)

    @pl.when(follows)
    def _():
        for t in range(2, last):
            start_t1(t)

    for d in range(1, middle):
        forward(d)

    def rest_t1():
        if last > 1:
            start_t1(last)

    def rest_t2():
        for t in range(2, last):
            start_t2(t)

    def finish_turns():
        if last > 0:
            turn_t(last)
        start_t2(last)

    def cross_chunk(t):
        if t == last:
            wait_t2(t, 0)
            make_cross(t, 0, blocks // 2)
            wait_t2(t, 1)
            make_cross(t, blocks // 2, blocks)
        else:
            wait_t2(t)
            make_cross(t)
        cross_scatter(t)

    early = min(2, last)

    def border():
        far = far_sum[...].reshape(tile, size)
        corner = rows_dot(inv_ref[0:edge, 0:edge], far[:, 0:edge], HIGHEST)
        upper_ref[0:edge, edge:size] = corner * (1.0 / root)

        def turned(right):
            return lax.dot_general(
                corner,
                right,
                (((0,), (0,)), ((), ())),
                precision=HIGHEST,
                preferred_element_type=F32,
            )

        aug[edge:size, edge:size] = far[:, edge:size] - turned(corner)
        aug[edge:size, size : 2 * size] = aug[edge:size, size : 2 * size] - turned(inv_ref[0:edge, :])

    @pl.when(leads)
    def _():
        gram_near()
        gram_scatter(0)
        if last > 2:
            start_t1(2, (0,))
        if last > 1:
            turn_t(1)
        aug_row = lax.broadcasted_iota(jnp.int32, (size, 2 * size), 0)
        aug_col = lax.broadcasted_iota(jnp.int32, (size, 2 * size), 1)
        aug[...] = jnp.where(aug_col == aug_row + size, 1.0, 0.0)
        gram_spread(0)
        for t in range(2, last):
            start_t1(t, (1,) if t == 2 else (0, 1))
        if last > 1:
            start_t2(1)
        forward(middle, range(pieces // 2))
        gram_done(0)
        forward(middle, range(pieces // 2, pieces - 1))
        unpack_near()
        for i in range(tiles - 1):
            factor_tile(i)
            send_factor(i, 0, start_copy)
            if i == 0:
                forward(middle, range(pieces - 1, pieces))
                rest_t1()
                for t in range(2, last):
                    turn_t(t)
            if i == min(1, tiles - 2):
                rest_t2()
        far_copy(helper_z).wait_recv()
        border()
        factor_tile(tiles - 1)
        send_factor(tiles - 1, 0, start_copy)
        for i in range(tiles):
            send_factor(i, 1, start_copy)
        finish_turns()
        for t in range(early):
            cross_chunk(t)
        gram_clear(0)

    @pl.when(follows)
    def _():
        for t in range(1, last):
            turn_t(t)
            if t == 1:
                start_t2(t)
                for d in range(middle, middle + 1):
                    forward(d)
        if last < 2:
            for d in range(middle, middle + 1):
                forward(d)

        @pl.when(helps)
        def _():
            gram_far()
            gram_scatter(1)
            if last > 1:
                start_t1(last, picked=ahead)
            gram_spread(1)
            if last > 1:
                start_t1(last, picked=behind)

        @pl.when(jnp.logical_not(helps))
        def _():
            rest_t1()

        rest_t2()

        @pl.when(helps)
        def _():
            gram_done(1)
            far_copy(lead_z).start()
            gram_clear(1)

        finish_turns()
        for d in range(middle + 1, depth):
            forward(d)
        for t in range(early):
            cross_chunk(t)
        factor_whole(0).wait_recv()

    make_basis()
    for t in range(early, tt):
        cross_chunk(t)
    for t in range(tt):
        cross_spread(t)
    if early > 0:
        emit(list(range(early)))
    for t in range(early, tt):
        cross_done(t)

    @pl.when(follows)
    def _():
        factor_whole(1).wait_recv()

    @pl.when(helps)
    def _():
        far_copy(lead_z).wait_send()

    @pl.when(leads)
    def _():
        for other in range(depth):
            if other != lead_z:
                for k in (0, 1):
                    factor_whole(k, other).wait_send()

    counted(has_p, op, lambda k: whole(ring_p.at[:, pl.ds(0, k * blocks)], p1_send.at[0], p1_recv.at[0]), clear)
    once(has_p, op, lambda k: whole(ring_p.at[:, pl.ds(0, k * blocks)], p2_send.at[0], p2_recv.at[0]), clear)
    for t in range(tt):
        ring = rings[t]
        counted(has_t, ot, lambda k: whole(ring.at[pl.ds(0, k * blocks)], t1_send.at[t], t1_recv.at[t]), clear)
        for sem in (t, t + 1) if t == tt - 1 else (t,):
            bulk = blocks // 2 if t == tt - 1 else blocks
            once(has_t, ot, lambda k: whole(ring.at[pl.ds(0, k * bulk)], t2_send.at[sem], t2_recv.at[sem]), clear)
        land = cross_land.at[t]
        counted(has_c, oc, lambda k: whole(land.at[pl.ds(0, k)], c_send.at[0, t], c_recv.at[0, t]), clear)
        once(has_c, oc, lambda k: whole(land.at[pl.ds(0, k)], c_send.at[1, t], c_recv.at[1, t]), clear)
    for d in range(1, depth):
        for q in range(pieces):
            for side in (0, 1):

                @pl.when(sends(side, d))
                def _():
                    line(side, d, q).wait_send()


def fused(panel, trail, panel_shift, trail_shift, n, depth, root):
    ctp, blocks = panel.shape[0], panel.shape[1]
    ctt = trail.shape[0]
    tp = -(-ctp // n)
    tt = -(-ctt // n)
    op, ot = ctp // tp, ctt // tt
    size = depth * ctp * SUB
    rows_t = ot * SUB
    sr = max(SUB, rows_t // n)
    oc = rows_t // sr
    tile = 64
    tiles = size // tile
    edge = size - tile
    packed = tile * (tiles * (tiles - 1) // 2)
    far_rows = -(-tile // (n * SUB)) * SUB
    pieces = 2 if ctp % 2 == 0 else 1
    total = n * blocks
    smem = pl.BlockSpec(memory_space=pltpu.SMEM)
    vmem = pl.BlockSpec(memory_space=pltpu.VMEM)
    hbm = pl.BlockSpec(memory_space=pl.ANY)
    dma = pltpu.SemaphoreType.DMA
    peers = max(n - 1, 1)
    lines = max(depth - 1, 1)
    return pl.pallas_call(
        functools.partial(fused_kernel, n, depth, pieces, root),
        out_shape=(
            pltpu.VMEM((size, size), F32),
            pltpu.VMEM((size, size), F32),
            pltpu.VMEM((tt, oc, sr, size), F32),
            pltpu.VMEM(panel.shape, F32),
            pltpu.VMEM((ot, tt) + trail.shape[1:], F32),
            pltpu.VMEM((blocks, size, BW), jnp.bfloat16),
            pltpu.VMEM((blocks, size, BW), jnp.bfloat16),
        ),
        in_specs=[smem, smem, hbm, hbm],
        out_specs=(vmem,) * 7,
        scratch_shapes=[
            pltpu.VMEM((depth,) + panel.shape, F32),
            pltpu.VMEM((tp, total + blocks, SUB, BW), F32),
            pltpu.VMEM((n, tp, blocks, SUB, BW), F32),
            pltpu.VMEM((tt, n, blocks, SUB, BW), F32),
            pltpu.VMEM((edge, edge), F32),
            pltpu.VMEM((tile // far_rows, far_rows, packed), F32),
            pltpu.VMEM((peers, far_rows, packed), F32),
            pltpu.VMEM((tile // far_rows, far_rows, packed), F32),
            pltpu.VMEM((tile // far_rows, far_rows, size), F32),
            pltpu.VMEM((peers, far_rows, size), F32),
            pltpu.VMEM((tile // far_rows, far_rows, size), F32),
            pltpu.VMEM((tt, oc, sr, size), F32),
            pltpu.VMEM((tt, peers, sr, size), F32),
            pltpu.VMEM((size, 2 * size), F32),
            pltpu.VMEM((tile, 2 * tile), F32),
            dma((1,)),
            dma((1,)),
            dma((1,)),
            dma((1,)),
            dma((tt,)),
            dma((tt,)),
            dma((tt + 1,)),
            dma((tt + 1,)),
            dma((2, lines, pieces)),
            dma((2, lines, pieces)),
            dma((2, 2)),
            dma((2, 2)),
            dma((2, tt)),
            dma((2, tt)),
            dma((depth, 2)),
            dma((2,)),
            dma((1,)),
            dma((1,)),
            dma((1 + tt,)),
        ]
        + [pltpu.VMEM((total + blocks, SUB, BW), F32)] * tt,
        compiler_params=pltpu.CompilerParams(
            collective_id=3, has_side_effects=True, vmem_limit_bytes=40 << 20
        ),
        cost_estimate=pl.CostEstimate(
            flops=0, bytes_accessed=40 * trail.size * 4, transcendentals=0
        ),
    )(panel_shift, trail_shift, panel, trail)


def final_kernel(
    root,
    early,
    upper,
    inv,
    cross,
    q,
    reg,
    high_ref,
    low_ref,
    r_ref,
    coupling_ref,
    q_ref,
    out_ref,
    late,
    coupling,
    sems,
):
    size = inv.shape[0]
    ot, tt, blocks = reg.shape[:3]
    rows_t = ot * SUB
    chunks = list(range(early, tt))
    steps = 2 if blocks % 2 == 0 else 1
    span = blocks // steps
    copies = [pltpu.make_async_copy(q, q_ref, sems.at[0])]
    copies.append(pltpu.make_async_copy(upper, r_ref, sems.at[1]))
    for t in range(early):
        copies.append(pltpu.make_async_copy(reg.at[:, t], out_ref.at[:, t], sems.at[2 + t]))
    for copy in copies:
        copy.start()
    rows = joined([cross[t].reshape(rows_t, size) for t in chunks])
    left_side = three_part(rows_dot(rows, inv[...], HIGHEST))
    narrow = min(8, span)
    for h in range(steps):

        def body(b, carry, h=h):
            first = h * span + narrow * b
            both = removed(left_side, high_ref, low_ref, first, narrow)
            for k in range(narrow):
                lanes = slice(k * BW, (k + 1) * BW)
                for i, t in enumerate(chunks):
                    part = both[i * rows_t : (i + 1) * rows_t, lanes]
                    late[:, i, first + k] = reg[:, t, first + k] - part.reshape(ot, SUB, BW)
            return carry

        lax.fori_loop(0, span // narrow, body, 0)
        for i, t in enumerate(chunks):
            place = pl.ds(h * span, span)
            copy = pltpu.make_async_copy(
                late.at[:, i, place], out_ref.at[:, t, place], sems.at[2 + early + h * len(chunks) + i]
            )
            copy.start()
            copies.append(copy)
    every = jnp.stack([cross[t].reshape(ot, SUB, size) for t in range(tt)], axis=1)
    coupling[...] = rows_dot(
        inv[...] * (1.0 / root), every.reshape(ot * tt * SUB, size), HIGHEST
    )
    last = pltpu.make_async_copy(coupling, coupling_ref, sems.at[2 + early + steps * len(chunks)])
    last.start()
    copies.append(last)
    for copy in copies:
        copy.wait()


def final(upper, inv, cross, q, reg, high, low, root):
    size = inv.shape[0]
    ot, tt = reg.shape[:2]
    early = min(2, tt - 1)
    vmem = pl.BlockSpec(memory_space=pltpu.VMEM)
    hbm = pl.BlockSpec(memory_space=pl.ANY)
    near = [pltpu.with_memory_space_constraint(x, pltpu.VMEM) for x in (upper, inv, cross, q, reg, high, low)]
    return pl.pallas_call(
        functools.partial(final_kernel, root, early),
        out_shape=(
            jax.ShapeDtypeStruct((size, size), F32),
            jax.ShapeDtypeStruct((size, ot * tt * SUB), F32),
            jax.ShapeDtypeStruct(q.shape, F32),
            jax.ShapeDtypeStruct(reg.shape, F32),
        ),
        in_specs=[vmem] * 7,
        out_specs=(hbm,) * 4,
        scratch_shapes=[
            pltpu.VMEM((ot, tt - early) + reg.shape[2:], F32),
            pltpu.VMEM((size, ot * tt * SUB), F32),
            pltpu.SemaphoreType.DMA((3 + early + 2 * (tt - early),)),
        ],
        compiler_params=pltpu.CompilerParams(vmem_limit_bytes=24 << 20),
        cost_estimate=pl.CostEstimate(
            flops=2 * size * reg.size, bytes_accessed=8 * reg.size, transcendentals=0
        ),
    )(*near)


def tiled(raw):
    rows, pixels = raw.shape
    return raw.reshape(rows // SUB, SUB, pixels // BW, BW).transpose(0, 2, 1, 3)


def flat(blocked):
    cut, blocks = blocked.shape[0], blocked.shape[1]
    return blocked.transpose(0, 2, 1, 3).reshape(cut * SUB, blocks * BW)


def on_device(raw_panel, raw_trail, panel_shift, trail_shift):
    n = lax.axis_size("rows")
    depth = lax.axis_size("cols")
    pixels = raw_panel.shape[1]
    root = math.sqrt(pixels * n)
    raw = [
        pltpu.with_memory_space_constraint(tiled(x), pltpu.HBM) for x in (raw_panel, raw_trail)
    ]
    shifts = [
        pltpu.with_memory_space_constraint(x, pltpu.HBM) for x in (panel_shift, trail_shift)
    ]
    held = fused(
        *raw, *shifts, n, depth, root
    )
    r_factor, coupling, q_panel, out = final(*held, root)
    return (r_factor, coupling, flat(q_panel), flat(out.reshape((-1,) + out.shape[2:])))


def solution(mesh):
    placed = (P("cols", "rows"), P("cols", "rows"), P("cols"), P("cols"))
    return jax.shard_map(
        on_device,
        mesh=mesh,
        in_specs=placed,
        out_specs=(P(), P(None, "cols"), P("cols", "rows"), P("cols", "rows")),
        check_vma=False,
    )
```

```python
import functools
import math

import jax
import jax.numpy as jnp
from jax import lax
from jax.experimental import pallas as pl
from jax.experimental.pallas import tpu as pltpu
from jax.sharding import PartitionSpec as P

BW = 128
SUB = 8
MESH = pl.DeviceIdType.MESH
F32 = jnp.float32
HIGHEST = lax.Precision.HIGHEST
HIGH = lax.Precision.HIGH


def rows_dot(left, right, precision):
    return lax.dot_general(
        left,
        right,
        (((1,), (1,)), ((), ())),
        precision=precision,
        preferred_element_type=F32,
    )


def plain_dot(left, right, precision):
    return lax.dot_general(
        left,
        right,
        (((1,), (0,)), ((), ())),
        precision=precision,
        preferred_element_type=F32,
    )


def joined(parts):
    return jnp.concatenate(parts, axis=0) if len(parts) > 1 else parts[0]


def three_part(value):
    high = value.astype(jnp.bfloat16)
    low = (value - high.astype(F32)).astype(jnp.bfloat16)
    return jnp.concatenate([high, high, low], axis=1)


def removed(left_side, high_ref, low_ref, first, count):
    high = jnp.concatenate([high_ref[first + k] for k in range(count)], axis=1)
    low = jnp.concatenate([low_ref[first + k] for k in range(count)], axis=1)
    return plain_dot(left_side, jnp.concatenate([high, low, high], axis=0), None)


def only(cond, always):
    if always:
        return lambda fn: fn()
    return pl.when(cond)


def fused_kernel(
    n,
    depth,
    pieces,
    root,
    panel_shift,
    trail_shift,
    panel,
    trail,
    upper_ref,
    inv_ref,
    cross_ref,
    q_ref,
    reg,
    high_ref,
    low_ref,
    full,
    ring_p,
    moved_p,
    moved_t,
    near_all,
    near_part,
    near_land,
    near_sum,
    far_part,
    far_land,
    far_sum,
    cross_part,
    cross_land,
    aug,
    pair,
    p1_send,
    p1_recv,
    p2_send,
    p2_recv,
    t1_send,
    t1_recv,
    t2_send,
    t2_recv,
    z_send,
    z_recv,
    g_send,
    g_recv,
    c_send,
    c_recv,
    f_send,
    f_recv,
    h_send,
    h_recv,
    local_sem,
    *rings,
):
    me = lax.axis_index("rows")
    z = lax.axis_index("cols")
    ctp, blocks = panel.shape[0], panel.shape[1]
    ctt = trail.shape[0]
    total = n * blocks
    tp = ring_p.shape[0]
    tt = len(rings)
    op, ot = ctp // tp, ctt // tt
    rows_t = ot * SUB
    sr = cross_land.shape[2]
    oc = rows_t // sr
    size = inv_ref.shape[0]
    lead_z = max(depth // 2 - 1, 0)
    leads = z == lead_z
    helper_z = min(lead_z + 1, depth - 1)
    helps = z == helper_z
    tile = pair.shape[0]
    tiles = size // tile
    edge = size - tile
    near_count = edge // (ctp * SUB)
    mine = pl.ds(pl.multiple_of(me * blocks, blocks), blocks)

    def each_peer(fn):
        def body(d, carry):
            fn(d, lax.rem(me + d, n), lax.rem(me - d + n, n))
            return carry

        lax.fori_loop(1, n, body, 0)

    def linked(other):
        near = (z - other == 1) | (other - z == 1)
        return near | (z != other) & (leads | (other == lead_z))

    barrier = pltpu.get_barrier_semaphore()
    for d in range(1, n):
        pl.semaphore_signal(
            barrier, inc=1, device_id={"rows": lax.rem(me + d, n)}, device_id_type=MESH
        )
    greeted = n - 1
    for other in range(depth):

        @pl.when(linked(other))
        def _():
            pl.semaphore_signal(barrier, inc=1, device_id={"cols": other}, device_id_type=MESH)

        greeted = greeted + jnp.where(linked(other), 1, 0)
    pl.semaphore_wait(barrier, greeted)

    def row_copy(src, dst, send, recv, to):
        return pltpu.make_async_remote_copy(
            src_ref=src,
            dst_ref=dst,
            send_sem=send,
            recv_sem=recv,
            device_id={"rows": to},
            device_id_type=MESH,
        )

    def p1(d, to):
        return row_copy(
            panel.at[pl.ds(to * tp, tp)],
            ring_p.at[:, mine],
            p1_send.at[0],
            p1_recv.at[0],
            to,
        )

    def p2(d, to):
        return row_copy(
            moved_p.at[to],
            full.at[z, pl.ds(me * tp, tp)],
            p2_send.at[0],
            p2_recv.at[0],
            to,
        )

    def t1(t, d, to):
        return row_copy(
            trail.at[to * tt + t],
            rings[t].at[mine],
            t1_send.at[t],
            t1_recv.at[t],
            to,
        )

    def t2(t, half, d, to):
        cut = pl.ds(0, blocks) if half is None else pl.ds(half * (blocks // 2), blocks // 2)
        return row_copy(
            moved_t.at[t, to, cut],
            reg.at[me, t, cut],
            t2_send.at[t + (1 if half == 1 else 0)],
            t2_recv.at[t + (1 if half == 1 else 0)],
            to,
        )

    own_p = pltpu.make_async_copy(
        panel.at[pl.ds(me * tp, tp)], ring_p.at[:, mine], local_sem.at[0]
    )

    def own_t(t):
        return pltpu.make_async_copy(
            trail.at[me * tt + t], rings[t].at[mine], local_sem.at[1 + t]
        )

    def started(copies, active, count, first=1, stride=1, pick=None):
        def go(k, carry):
            d = first + stride * k
            to = lax.rem(me + d, n)
            wanted = active(to) if pick is None else active(to) & pick(d)

            @only(wanted, count == n and pick is None)
            def _():
                copies(d, to).start()

            return carry

        lax.fori_loop(0, -(-(n - first) // stride), go, 0)

    def whole(region, send, recv):
        return row_copy(region, region, send, recv, lax.rem(me + 1, n))

    def counted(active, count, per_copy, done):
        if count == n:
            done(per_copy(n - 1))
        else:

            @pl.when(active(me))
            def _():
                done(per_copy(count - 1))

            @pl.when(jnp.logical_not(active(me)))
            def _():
                done(per_copy(count))

    def once(active, count, per_copy, done):
        @only(active(me), count == n)
        def _():
            done(per_copy(n - 1))

    def take(copy):
        copy.wait_recv()

    def clear(copy):
        copy.wait_send()

    def has_p(j):
        return j < op

    def has_t(j):
        return j < ot

    sub = lax.broadcasted_iota(jnp.int32, (1, SUB, BW), 1)
    step = min(16, blocks)

    def compose(ring, shifts, to, put):
        starts = [lax.rem(to * blocks - s + total, total) for s in shifts]
        for h in range(0, blocks, step):
            block = ring[pl.ds(starts[0] + h, step)]
            for c in range(1, SUB):
                block = jnp.where(sub == c, ring[pl.ds(starts[c] + h, step)], block)
            put(h, block)

    def wrap(ring):
        ring[pl.ds(total, blocks)] = ring[pl.ds(0, blocks)]

    def line(side, d, q):
        step_z = 1 if side == 0 else -1
        origin = z - step_z * (d - 1)
        rows = pl.ds(q * (ctp // pieces), ctp // pieces)
        return pltpu.make_async_remote_copy(
            src_ref=full.at[origin, rows],
            dst_ref=full.at[origin, rows],
            send_sem=z_send.at[side, d - 1, q],
            recv_sem=z_recv.at[side, d - 1, q],
            device_id={"cols": z + step_z},
            device_id_type=MESH,
        )

    def sends(side, d):
        if side == 0:
            return (z + 1 < depth) & (z - (d - 1) >= 0)
        return (z >= 1) & (z + (d - 1) < depth)

    def receives(side, d):
        return z - d >= 0 if side == 0 else z + d < depth

    def arrived(side, d, q):
        step_z = 1 if side == 0 else -1
        origin = z - step_z * d
        rows = pl.ds(q * (ctp // pieces), ctp // pieces)
        return pltpu.make_async_remote_copy(
            src_ref=full.at[origin, rows],
            dst_ref=full.at[origin, rows],
            send_sem=z_send.at[side, d - 1, q],
            recv_sem=z_recv.at[side, d - 1, q],
            device_id={"cols": z - step_z},
            device_id_type=MESH,
        )

    def forward(d, some=None):
        for q in range(pieces) if some is None else some:
            for side in (0, 1):

                @pl.when(receives(side, d))
                def _():
                    arrived(side, d, q).wait_recv()

                if d + 1 < depth:

                    @pl.when(sends(side, d + 1))
                    def _():
                        line(side, d + 1, q).start()

    def ahead(d):
        return (d == 2) | (d == 4) | (d == 6)

    def behind(d):
        return jnp.logical_not(ahead(d))

    def start_t1(t, halves=(0, 1), picked=None):
        if 0 in halves and picked is not behind:

            @only(has_t(me), ot == n)
            def _():
                own_t(t).start()

        if len(halves) == 2:
            started(functools.partial(t1, t), has_t, ot, pick=picked)
        else:
            started(functools.partial(t1, t), has_t, ot, 2 - halves[0], 2)

    def turn_t(t):
        @only(has_t(me), ot == n)
        def _():
            own_t(t).wait()

        once(has_t, ot, lambda k: whole(rings[t].at[pl.ds(0, k * blocks)], t1_send.at[t], t1_recv.at[t]), take)

        @only(has_t(me), ot == n)
        def _():
            wrap(rings[t])
            shifts = [trail_shift[(me * tt + t) * SUB + c] for c in range(SUB)]

            def turn(d, to, origin):
                def put(h, block):
                    moved_t[t, to, pl.ds(h, step)] = block

                compose(rings[t], shifts, to, put)

            each_peer(turn)

            def keep(h, block):
                reg[me, t, pl.ds(h, step)] = block

            compose(rings[t], shifts, me, keep)

    def start_t2(t):
        @only(has_t(me), ot == n)
        def _():
            for half in (0, 1) if t == tt - 1 else (None,):
                started(functools.partial(t2, t, half), has_t, n)

    def wait_t2(t, half=None):
        cut = pl.ds(0, blocks if half is None else blocks // 2)
        sem = t + (1 if half == 1 else 0)
        counted(has_t, ot, lambda k: whole(reg.at[pl.ds(0, k), t, cut], t2_send.at[sem], t2_recv.at[sem]), take)

    def panel_block(b, count, lo=0, hi=depth):
        rows = (hi - lo) * ctp * SUB
        cut = [full[lo:hi, :, count * b + k].reshape(rows, BW) for k in range(count)]
        return jnp.concatenate(cut, axis=1)

    narrow = min(4, blocks)
    wide = min(8, blocks // 2)

    def gram_near():
        near_all[...] = jnp.zeros_like(near_all)

        def body(b, carry):
            block = panel_block(b, narrow, 0, near_count)
            near_all[...] += rows_dot(block, block, HIGHEST)
            return carry

        lax.fori_loop(0, blocks // narrow, body, 0)
        packed = [near_all[lo : lo + tile, lo:edge] for lo in range(0, edge, tile)]
        near_part[...] = jnp.concatenate(packed, axis=1).reshape(near_part.shape)

    def unpack_near():
        packed = near_sum[...].reshape(tile, near_sum.shape[2])
        first = 0
        for lo in range(0, edge, tile):
            aug[lo : lo + tile, lo:edge] = packed[:, first : first + edge - lo]
            first += edge - lo

    def gram_far():
        far_part[...] = jnp.zeros_like(far_part)

        def body(b, carry):
            block = panel_block(b, narrow, near_count, depth)
            both = rows_dot(block, panel_block(b, narrow), HIGHEST)
            far_part[...] += both.reshape(far_part.shape)
            return carry

        lax.fori_loop(0, blocks // narrow, body, 0)

    grams = ((near_part, near_land, near_sum), (far_part, far_land, far_sum))

    def g_one(k, d, to):
        part, land, _ = grams[k]
        return row_copy(part.at[to], land.at[d - 1], g_send.at[k, 0], g_recv.at[k, 0], to)

    def g_two(k, d, to):
        ref = grams[k][2]
        return row_copy(ref.at[me], ref.at[me], g_send.at[k, 1], g_recv.at[k, 1], to)

    def g_count(k):
        return grams[k][0].shape[0]

    def has_g(k):
        return lambda j: j < g_count(k)

    def gram_scatter(k):
        started(functools.partial(g_one, k), has_g(k), g_count(k))

    def gram_spread(k):
        part, land, total_ref = grams[k]

        @only(me < g_count(k), g_count(k) == n)
        def _():
            take(whole(land, g_send.at[k, 0], g_recv.at[k, 0]))
            total_g = part[me]
            for d in range(1, n):
                total_g = total_g + land[d - 1]
            total_ref[me] = total_g

            def go(d, to, origin):
                g_two(k, d, to).start()

            each_peer(go)

    def gram_done(k):
        ref = grams[k][2]
        counted(has_g(k), g_count(k), lambda m: whole(ref.at[pl.ds(0, m)], g_send.at[k, 1], g_recv.at[k, 1]), take)

    def gram_clear(k):
        land = grams[k][1]
        counted(has_g(k), g_count(k), lambda m: whole(land.at[pl.ds(0, m)], g_send.at[k, 0], g_recv.at[k, 0]), clear)
        once(has_g(k), g_count(k), lambda m: whole(land.at[pl.ds(0, m)], g_send.at[k, 1], g_recv.at[k, 1]), clear)

    def far_copy(to):
        return pltpu.make_async_remote_copy(
            src_ref=far_sum,
            dst_ref=far_sum,
            send_sem=h_send.at[0],
            recv_sem=h_recv.at[0],
            device_id={"cols": to},
            device_id_type=MESH,
        )

    def has_c(j):
        return j < oc

    def make_cross(t, lo=0, hi=blocks):
        if lo == 0:
            cross_part[t] = jnp.zeros_like(cross_part[t])

        def body(b, carry):
            cut = [reg[:, t, wide * b + k].reshape(rows_t, BW) for k in range(wide)]
            block = jnp.concatenate(cut, axis=1)
            both = rows_dot(block, panel_block(b, wide), HIGH)
            cross_part[t] += both.reshape(oc, sr, size)
            return carry

        lax.fori_loop(lo // wide, hi // wide, body, 0)

    def c_one(t, d, to):
        return row_copy(
            cross_part.at[t, to],
            cross_land.at[t, d - 1],
            c_send.at[0, t],
            c_recv.at[0, t],
            to,
        )

    def c_two(t, d, to):
        return row_copy(
            cross_ref.at[t, me],
            cross_ref.at[t, me],
            c_send.at[1, t],
            c_recv.at[1, t],
            to,
        )

    def cross_scatter(t):
        started(functools.partial(c_one, t), has_c, oc)

    def cross_spread(t):
        @only(has_c(me), oc == n)
        def _():
            take(whole(cross_land.at[t], c_send.at[0, t], c_recv.at[0, t]))
            total_c = cross_part[t, me]
            for d in range(1, n):
                total_c = total_c + cross_land[t, d - 1]
            cross_ref[t, me] = total_c

            def go(d, to, origin):
                c_two(t, d, to).start()

            each_peer(go)

    def cross_done(t):
        counted(has_c, oc, lambda k: whole(cross_ref.at[t, pl.ds(0, k)], c_send.at[1, t], c_recv.at[1, t]), take)

    def factor_copy(i, k, slot, to):
        ref = inv_ref if k == 0 else upper_ref
        rows = pl.ds(i * tile, tile)
        return pltpu.make_async_remote_copy(
            src_ref=ref.at[rows],
            dst_ref=ref.at[rows],
            send_sem=f_send.at[slot, k],
            recv_sem=f_recv.at[k],
            device_id={"cols": to},
            device_id_type=MESH,
        )

    def factor_whole(k, slot=0):
        ref = inv_ref if k == 0 else upper_ref
        return pltpu.make_async_remote_copy(
            src_ref=ref,
            dst_ref=ref,
            send_sem=f_send.at[slot, k],
            recv_sem=f_recv.at[k],
            device_id={"cols": lax.rem(z + 1, depth)},
            device_id_type=MESH,
        )

    def send_factor(i, k, act):
        for other in range(depth):
            if other != lead_z:
                act(factor_copy(i, k, other, other))

    def factor_tile(i):
        lo = i * tile
        hi = lo + tile
        row = lax.broadcasted_iota(jnp.int32, (tile, 2 * tile), 0)
        col = lax.broadcasted_iota(jnp.int32, (tile, 2 * tile), 1)
        pair[...] = jnp.where(col == row + tile, 1.0, 0.0)
        pair[:, 0:tile] = aug[lo:hi, lo:hi]
        w = pair[...]
        pivots = jnp.zeros((tile, 1), F32)
        for j in range(tile):
            base = j // 8 * 8
            live = w[base:, :]
            lead = w[j : j + 1, :]
            pivot = lead[:, j : j + 1]
            pivots = jnp.where(row[:, 0:1] == j, pivot, pivots)
            if j + 1 == tile:
                break
            mult = jnp.where(row[base:, 0:1] > j, live[:, j : j + 1], 0.0)
            live = live - mult * (lead / pivot)
            w = live if base == 0 else jnp.concatenate([w[:base], live], axis=0)
        pair[...] = w * (1.0 / jnp.sqrt(pivots))
        inverse = pair[:, tile : 2 * tile]
        lead_rows = plain_dot(inverse, aug[lo:hi, :], HIGHEST)
        grow = lax.broadcasted_iota(jnp.int32, (tile, size), 0) + lo
        gcol = lax.broadcasted_iota(jnp.int32, (tile, size), 1)
        upper = jnp.where(gcol >= grow, lead_rows[:, 0:size], 0.0)
        upper_ref[lo:hi, :] = upper * (1.0 / root)
        inv_ref[lo:hi, :] = lead_rows[:, size : 2 * size]
        if hi < edge:
            aug[...] = aug[...] - lax.dot_general(
                upper,
                lead_rows,
                (((0,), (0,)), ((), ())),
                precision=HIGHEST,
                preferred_element_type=F32,
            )

    def make_basis():
        factor = inv_ref[...]
        own = pl.ds(pl.multiple_of(z * (ctp * SUB), ctp * SUB), ctp * SUB)

        def body(b, carry):
            both = plain_dot(factor, panel_block(b, narrow), HIGH)
            mine_only = plain_dot(inv_ref[own, :] * root, panel_block(b, narrow), HIGH)
            for k in range(narrow):
                lanes = slice(k * BW, (k + 1) * BW)
                place = narrow * b + k
                part = both[:, lanes]
                upper_half = part.astype(jnp.bfloat16)
                high_ref[place] = upper_half
                low_ref[place] = (part - upper_half.astype(F32)).astype(jnp.bfloat16)
                q_ref[:, place] = mine_only[:, lanes].reshape(ctp, SUB, BW)
            return carry

        lax.fori_loop(0, blocks // narrow, body, 0)

    def emit(chunks):
        for t in chunks:
            cross_done(t)
        rows = [cross_ref[t].reshape(rows_t, size) for t in chunks]
        left_side = three_part(rows_dot(joined(rows), inv_ref[...], HIGHEST))

        def body(b, carry):
            both = removed(left_side, high_ref, low_ref, wide * b, wide)
            for k in range(wide):
                lanes = slice(k * BW, (k + 1) * BW)
                place = wide * b + k
                for i, t in enumerate(chunks):
                    part = both[i * rows_t : (i + 1) * rows_t, lanes]
                    reg[:, t, place] = reg[:, t, place] - part.reshape(ot, SUB, BW)
            return carry

        lax.fori_loop(0, blocks // wide, body, 0)

    def start_copy(copy):
        copy.start()

    @only(has_p(me), op == n)
    def _():
        own_p.start()

    started(p1, has_p, op)

    start_t1(0, picked=ahead)

    @only(has_p(me), op == n)
    def _():
        own_p.wait()

    once(has_p, op, lambda k: whole(ring_p.at[:, pl.ds(0, k * blocks)], p1_send.at[0], p1_recv.at[0]), take)

    @only(has_p(me), op == n)
    def _():
        for t in range(tp):
            wrap(ring_p.at[t])
        shifts = [
            [panel_shift[(me * tp + t) * SUB + c] for c in range(SUB)] for t in range(tp)
        ]

        def turn(d, to, origin):
            for t in range(tp):

                def put(h, block, t=t):
                    moved_p[to, t, pl.ds(h, step)] = block

                compose(ring_p.at[t], shifts[t], to, put)

        each_peer(turn)

        def go(d, to, origin):
            p2(d, to).start()

        each_peer(go)
        for t in range(tp):

            def keep(h, block, t=t):
                full[z, me * tp + t, pl.ds(h, step)] = block

            compose(ring_p.at[t], shifts[t], me, keep)

    last = tt - 1
    start_t1(0, picked=behind)
    if tt > 1:
        start_t1(1)
    counted(has_p, op, lambda k: whole(full.at[z, pl.ds(0, k * tp)], p2_send.at[0], p2_recv.at[0]), take)
    for q in range(pieces):
        for side in (0, 1):

            @pl.when(sends(side, 1))
            def _():
                line(side, 1, q).start()

    middle = max(depth // 2, 1)
    turn_t(0)
    if last > 0:
        start_t2(0)
    follows = jnp.logical_not(leads)

    @pl.when(follows)
    def _():
        for t in range(2, last):
            start_t1(t)

    for d in range(1, middle):
        forward(d)

    def rest_t1():
        if last > 1:
            start_t1(last)

    def rest_t2():
        for t in range(2, last):
            start_t2(t)

    def finish_turns():
        if last > 0:
            turn_t(last)
        start_t2(last)

    def cross_chunk(t):
        if t == last:
            wait_t2(t, 0)
            make_cross(t, 0, blocks // 2)
            wait_t2(t, 1)
            make_cross(t, blocks // 2, blocks)
        else:
            wait_t2(t)
            make_cross(t)
        cross_scatter(t)

    early = min(2, last)

    def border():
        far = far_sum[...].reshape(tile, size)
        corner = rows_dot(inv_ref[0:edge, 0:edge], far[:, 0:edge], HIGHEST)
        upper_ref[0:edge, edge:size] = corner * (1.0 / root)

        def turned(right):
            return lax.dot_general(
                corner,
                right,
                (((0,), (0,)), ((), ())),
                precision=HIGHEST,
                preferred_element_type=F32,
            )

        aug[edge:size, edge:size] = far[:, edge:size] - turned(corner)
        aug[edge:size, size : 2 * size] = aug[edge:size, size : 2 * size] - turned(inv_ref[0:edge, :])

    @pl.when(leads)
    def _():
        gram_near()
        gram_scatter(0)
        if last > 2:
            start_t1(2, (0,))
        if last > 1:
            turn_t(1)
        aug_row = lax.broadcasted_iota(jnp.int32, (size, 2 * size), 0)
        aug_col = lax.broadcasted_iota(jnp.int32, (size, 2 * size), 1)
        aug[...] = jnp.where(aug_col == aug_row + size, 1.0, 0.0)
        gram_spread(0)
        for t in range(2, last):
            start_t1(t, (1,) if t == 2 else (0, 1))
        if last > 1:
            start_t2(1)
        forward(middle, range(pieces // 2))
        gram_done(0)
        forward(middle, range(pieces // 2, pieces - 1))
        unpack_near()
        for i in range(tiles - 1):
            factor_tile(i)
            send_factor(i, 0, start_copy)
            if i == 0:
                forward(middle, range(pieces - 1, pieces))
                rest_t1()
                for t in range(2, last):
                    turn_t(t)
            if i == min(1, tiles - 2):
                rest_t2()
        far_copy(helper_z).wait_recv()
        border()
        factor_tile(tiles - 1)
        send_factor(tiles - 1, 0, start_copy)
        for i in range(tiles):
            send_factor(i, 1, start_copy)
        finish_turns()
        for t in range(early):
            cross_chunk(t)
        gram_clear(0)

    @pl.when(follows)
    def _():
        for t in range(1, last):
            turn_t(t)
            if t == 1:
                start_t2(t)
                for d in range(middle, middle + 1):
                    forward(d)
        if last < 2:
            for d in range(middle, middle + 1):
                forward(d)

        @pl.when(helps)
        def _():
            gram_far()
            gram_scatter(1)
            if last > 1:
                start_t1(last, picked=ahead)
            gram_spread(1)
            if last > 1:
                start_t1(last, picked=behind)

        @pl.when(jnp.logical_not(helps))
        def _():
            rest_t1()

        rest_t2()

        @pl.when(helps)
        def _():
            gram_done(1)
            far_copy(lead_z).start()
            gram_clear(1)

        finish_turns()
        for d in range(middle + 1, depth):
            forward(d)
        for t in range(early):
            cross_chunk(t)
        factor_whole(0).wait_recv()

    make_basis()
    for t in range(early, tt):
        cross_chunk(t)
    for t in range(tt):
        cross_spread(t)
    if early > 0:
        emit(list(range(early)))
    for t in range(early, tt):
        cross_done(t)

    @pl.when(follows)
    def _():
        factor_whole(1).wait_recv()

    @pl.when(helps)
    def _():
        far_copy(lead_z).wait_send()

    @pl.when(leads)
    def _():
        for other in range(depth):
            if other != lead_z:
                for k in (0, 1):
                    factor_whole(k, other).wait_send()

    counted(has_p, op, lambda k: whole(ring_p.at[:, pl.ds(0, k * blocks)], p1_send.at[0], p1_recv.at[0]), clear)
    once(has_p, op, lambda k: whole(ring_p.at[:, pl.ds(0, k * blocks)], p2_send.at[0], p2_recv.at[0]), clear)
    for t in range(tt):
        ring = rings[t]
        counted(has_t, ot, lambda k: whole(ring.at[pl.ds(0, k * blocks)], t1_send.at[t], t1_recv.at[t]), clear)
        for sem in (t, t + 1) if t == tt - 1 else (t,):
            bulk = blocks // 2 if t == tt - 1 else blocks
            once(has_t, ot, lambda k: whole(ring.at[pl.ds(0, k * bulk)], t2_send.at[sem], t2_recv.at[sem]), clear)
        land = cross_land.at[t]
        counted(has_c, oc, lambda k: whole(land.at[pl.ds(0, k)], c_send.at[0, t], c_recv.at[0, t]), clear)
        once(has_c, oc, lambda k: whole(land.at[pl.ds(0, k)], c_send.at[1, t], c_recv.at[1, t]), clear)
    for d in range(1, depth):
        for q in range(pieces):
            for side in (0, 1):

                @pl.when(sends(side, d))
                def _():
                    line(side, d, q).wait_send()


def fused(panel, trail, panel_shift, trail_shift, n, depth, root):
    ctp, blocks = panel.shape[0], panel.shape[1]
    ctt = trail.shape[0]
    tp = -(-ctp // n)
    tt = -(-ctt // n)
    op, ot = ctp // tp, ctt // tt
    size = depth * ctp * SUB
    rows_t = ot * SUB
    sr = max(SUB, rows_t // n)
    oc = rows_t // sr
    tile = 64
    tiles = size // tile
    edge = size - tile
    packed = tile * (tiles * (tiles - 1) // 2)
    far_rows = -(-tile // (n * SUB)) * SUB
    pieces = 2 if ctp % 2 == 0 else 1
    total = n * blocks
    smem = pl.BlockSpec(memory_space=pltpu.SMEM)
    vmem = pl.BlockSpec(memory_space=pltpu.VMEM)
    hbm = pl.BlockSpec(memory_space=pl.ANY)
    dma = pltpu.SemaphoreType.DMA
    peers = max(n - 1, 1)
    lines = max(depth - 1, 1)
    return pl.pallas_call(
        functools.partial(fused_kernel, n, depth, pieces, root),
        out_shape=(
            pltpu.VMEM((size, size), F32),
            pltpu.VMEM((size, size), F32),
            pltpu.VMEM((tt, oc, sr, size), F32),
            pltpu.VMEM(panel.shape, F32),
            pltpu.VMEM((ot, tt) + trail.shape[1:], F32),
            pltpu.VMEM((blocks, size, BW), jnp.bfloat16),
            pltpu.VMEM((blocks, size, BW), jnp.bfloat16),
        ),
        in_specs=[smem, smem, hbm, hbm],
        out_specs=(vmem,) * 7,
        scratch_shapes=[
            pltpu.VMEM((depth,) + panel.shape, F32),
            pltpu.VMEM((tp, total + blocks, SUB, BW), F32),
            pltpu.VMEM((n, tp, blocks, SUB, BW), F32),
            pltpu.VMEM((tt, n, blocks, SUB, BW), F32),
            pltpu.VMEM((edge, edge), F32),
            pltpu.VMEM((tile // far_rows, far_rows, packed), F32),
            pltpu.VMEM((peers, far_rows, packed), F32),
            pltpu.VMEM((tile // far_rows, far_rows, packed), F32),
            pltpu.VMEM((tile // far_rows, far_rows, size), F32),
            pltpu.VMEM((peers, far_rows, size), F32),
            pltpu.VMEM((tile // far_rows, far_rows, size), F32),
            pltpu.VMEM((tt, oc, sr, size), F32),
            pltpu.VMEM((tt, peers, sr, size), F32),
            pltpu.VMEM((size, 2 * size), F32),
            pltpu.VMEM((tile, 2 * tile), F32),
            dma((1,)),
            dma((1,)),
            dma((1,)),
            dma((1,)),
            dma((tt,)),
            dma((tt,)),
            dma((tt + 1,)),
            dma((tt + 1,)),
            dma((2, lines, pieces)),
            dma((2, lines, pieces)),
            dma((2, 2)),
            dma((2, 2)),
            dma((2, tt)),
            dma((2, tt)),
            dma((depth, 2)),
            dma((2,)),
            dma((1,)),
            dma((1,)),
            dma((1 + tt,)),
        ]
        + [pltpu.VMEM((total + blocks, SUB, BW), F32)] * tt,
        compiler_params=pltpu.CompilerParams(
            collective_id=3, has_side_effects=True, vmem_limit_bytes=40 << 20
        ),
        cost_estimate=pl.CostEstimate(
            flops=0, bytes_accessed=40 * trail.size * 4, transcendentals=0
        ),
    )(panel_shift, trail_shift, panel, trail)


def final_kernel(
    root,
    early,
    upper,
    inv,
    cross,
    q,
    reg,
    high_ref,
    low_ref,
    r_ref,
    coupling_ref,
    q_ref,
    out_ref,
    late,
    coupling,
    sems,
):
    size = inv.shape[0]
    ot, tt, blocks = reg.shape[:3]
    rows_t = ot * SUB
    chunks = list(range(early, tt))
    steps = 4 if blocks % 4 == 0 else 1
    span = blocks // steps
    copies = [pltpu.make_async_copy(q, q_ref, sems.at[0])]
    copies.append(pltpu.make_async_copy(upper, r_ref, sems.at[1]))
    for t in range(early):
        copies.append(pltpu.make_async_copy(reg.at[:, t], out_ref.at[:, t], sems.at[2 + t]))
    for copy in copies:
        copy.start()
    rows = joined([cross[t].reshape(rows_t, size) for t in chunks])
    left_side = three_part(rows_dot(rows, inv[...], HIGHEST))
    narrow = min(8, span)
    for h in range(steps):

        def body(b, carry, h=h):
            first = h * span + narrow * b
            both = removed(left_side, high_ref, low_ref, first, narrow)
            for k in range(narrow):
                lanes = slice(k * BW, (k + 1) * BW)
                for i, t in enumerate(chunks):
                    part = both[i * rows_t : (i + 1) * rows_t, lanes]
                    late[:, i, first + k] = reg[:, t, first + k] - part.reshape(ot, SUB, BW)
            return carry

        lax.fori_loop(0, span // narrow, body, 0)
        for i, t in enumerate(chunks):
            place = pl.ds(h * span, span)
            copy = pltpu.make_async_copy(
                late.at[:, i, place], out_ref.at[:, t, place], sems.at[2 + early + h * len(chunks) + i]
            )
            copy.start()
            copies.append(copy)
    every = jnp.stack([cross[t].reshape(ot, SUB, size) for t in range(tt)], axis=1)
    coupling[...] = rows_dot(
        inv[...] * (1.0 / root), every.reshape(ot * tt * SUB, size), HIGHEST
    )
    last = pltpu.make_async_copy(coupling, coupling_ref, sems.at[2 + early + steps * len(chunks)])
    last.start()
    copies.append(last)
    for copy in copies:
        copy.wait()


def final(upper, inv, cross, q, reg, high, low, root):
    size = inv.shape[0]
    ot, tt = reg.shape[:2]
    early = min(2, tt - 1)
    vmem = pl.BlockSpec(memory_space=pltpu.VMEM)
    hbm = pl.BlockSpec(memory_space=pl.ANY)
    near = [pltpu.with_memory_space_constraint(x, pltpu.VMEM) for x in (upper, inv, cross, q, reg, high, low)]
    return pl.pallas_call(
        functools.partial(final_kernel, root, early),
        out_shape=(
            jax.ShapeDtypeStruct((size, size), F32),
            jax.ShapeDtypeStruct((size, ot * tt * SUB), F32),
            jax.ShapeDtypeStruct(q.shape, F32),
            jax.ShapeDtypeStruct(reg.shape, F32),
        ),
        in_specs=[vmem] * 7,
        out_specs=(hbm,) * 4,
        scratch_shapes=[
            pltpu.VMEM((ot, tt - early) + reg.shape[2:], F32),
            pltpu.VMEM((size, ot * tt * SUB), F32),
            pltpu.SemaphoreType.DMA((3 + early + 4 * (tt - early),)),
        ],
        compiler_params=pltpu.CompilerParams(vmem_limit_bytes=24 << 20),
        cost_estimate=pl.CostEstimate(
            flops=2 * size * reg.size, bytes_accessed=8 * reg.size, transcendentals=0
        ),
    )(*near)


def tiled(raw):
    rows, pixels = raw.shape
    return raw.reshape(rows // SUB, SUB, pixels // BW, BW).transpose(0, 2, 1, 3)


def flat(blocked):
    cut, blocks = blocked.shape[0], blocked.shape[1]
    return blocked.transpose(0, 2, 1, 3).reshape(cut * SUB, blocks * BW)


def on_device(raw_panel, raw_trail, panel_shift, trail_shift):
    n = lax.axis_size("rows")
    depth = lax.axis_size("cols")
    pixels = raw_panel.shape[1]
    root = math.sqrt(pixels * n)
    raw = [
        pltpu.with_memory_space_constraint(tiled(x), pltpu.HBM) for x in (raw_panel, raw_trail)
    ]
    shifts = [
        pltpu.with_memory_space_constraint(x, pltpu.HBM) for x in (panel_shift, trail_shift)
    ]
    held = fused(
        *raw, *shifts, n, depth, root
    )
    r_factor, coupling, q_panel, out = final(*held, root)
    return (r_factor, coupling, flat(q_panel), flat(out.reshape((-1,) + out.shape[2:])))


def solution(mesh):
    placed = (P("cols", "rows"), P("cols", "rows"), P("cols"), P("cols"))
    return jax.shard_map(
        on_device,
        mesh=mesh,
        in_specs=placed,
        out_specs=(P(), P(None, "cols"), P("cols", "rows"), P("cols", "rows")),
        check_vma=False,
    )
```
